128 devices in a mesh: tensor: 4 (over x_hi, core), expert: 16 (over z, y), dp: 2 (over x_lo).
Axes of the slice: x: 4 (x_hi: 2, x_lo: 2; x = x_hi * 2 + x_lo), y: 4, z: 4, core: 2. Of those that a mesh axis runs over, the one named last changes fastest.
Arguments:
- queries: bfloat16 [32, 256, 2, 4096], P(('dp', 'expert'), None, None, 'tensor'), parts along dimension 0, may hold values from -6 to 6
- keys: bfloat16 [32, 256, 2, 512], P(('dp', 'expert'), None, None, 'tensor'), parts along dimension 0, may hold values from -6 to 6
- values: bfloat16 [32, 256, 2, 512], P(('dp', 'expert'), None, None, 'tensor'), parts along dimension 0, may hold values from -12 to 12
- q_gain: float32 [128], replicated, may hold values from 0 to 7
- k_gain: float32 [128], replicated, may hold values from 0 to 7
- out_weight: bfloat16 [4096, 4096], P('tensor', 'expert'), may hold values from -0.09375 to 0.09375
- hidden_in: bfloat16 [32, 256, 2, 4096], P(('dp', 'expert'), 'tensor'), parts along dimension 0, may hold values from -3 to 3
- norm_gain: float32 [4096], replicated, may hold values from 0.1 to 1.9
- router: bfloat16 [4096, 64], replicated, may hold values from -4 to 4
- expert_ids: int32 [32, 256, 2, 8], P(('dp', 'expert'), 'tensor'), parts along dimension 0, may hold values from 0 to 63, all different within a row; in each aligned block of 128 rows (0 to 127, 128 to 255, ..., all dimensions but the last counted through in order) at most 17 rows name the same one
- w_gate: bfloat16 [64, 4096, 768], P(('tensor', 'expert')), may hold values from -0.09375 to 0.09375
- w_up: bfloat16 [64, 4096, 768], P(('tensor', 'expert')), may hold values from -0.09375 to 0.09375
- w_down: bfloat16 [64, 768, 4096], P(('tensor', 'expert')), may hold values from -0.21875 to 0.21875
Outputs:
- hidden_out: bfloat16 [32, 256, 2, 4096], P(('dp', 'expert'), 'tensor'), parts along dimension 0
The draws below stay inside these ranges and needn't reach their ends.
There are 2 independent parts, one for each index of `dp`. The reference program is written for one: setup_inputs(seed, part) draws one part's arguments, and reference() takes and returns one part's arrays. A program takes and returns all parts, laid end to end along the dimension named above; an argument that names none is the same for every part. Nothing has to cross between parts.
Inputs may be any that keep to these rules, and one draw needn't show every extreme that they name: `expert_ids`: each row names 8 different experts; among the 128 rows of one device no expert is named by more than 17 rows, a bound that some block reaches.
All inputs are finite; a program needn't handle non-finite values.
Results may differ from the reference program's by a relative error of at most 0.03.
The reference program's roundings to bfloat16 on the way count: a program that leaves them out, or rounds other values in their place, can miss the bound.
Values may be sent and summed in bfloat16 or wider, within the bound.
No kernel may reach another device: no remote copies, remote signals or barrier semaphores. Data moves between devices by JAX's collectives and lax.ppermute only.
A program may use at most 256 MiB of HBM per device.

```python
import math
import jax
import jax.numpy as jnp
import numpy as np
from jax import lax

D = 4096
HD = 128
FF = 768
TOPK = 8
SEQS = 2
HEADS = 32
KV_HEADS = 4
EXPERTS = 64
BLOCK = 256
BLOCKS = 16
ROWS_DEV = 128
CAP = 17


def draw_q_gain(key, part):
    folded = jax.random.fold_in(key, 11)
    result = jax.random.uniform(folded, (HD,), jnp.float32, 0.5, 2.0)
    return result


def draw_k_gain(key, part):
    folded = jax.random.fold_in(key, 23)
    result = jax.random.uniform(folded, (HD,), jnp.float32, 0.5, 2.0)
    return result


def draw_router(key, part):
    folded = jax.random.fold_in(key, 37)
    spread = jax.random.normal(folded, (D, EXPERTS), jnp.float32)
    spread = spread * D ** (-0.5)
    return jnp.clip(spread, -4.0, 4.0).astype(jnp.bfloat16)


def block_scale(stream_key, extent, split, least, top_value):
    def one(dim, shards_of):
        steps = jax.random.uniform(jax.random.fold_in(jax.random.fold_in(stream_key, 6), dim), (shards_of,), jnp.float32, least / len(split), top_value / len(split))
        return jnp.repeat(jnp.exp(steps), extent[dim] // shards_of).reshape((-1,) + (1,) * (len(extent) - dim - 1))

    factor_of = one(*split[0])
    for cut in split[1:]:
        factor_of = factor_of * one(*cut)
    return factor_of


def assign_block(own_key, own, number, rows, amount, top, limit, lean):
    order = jax.random.permutation(own_key, amount)
    packed, common = portions_of(amount, rows * top, limit, lean, True), portions_of(amount, rows * top, limit, lean, False)
    places = jnp.arange(amount)

    def named(sizes, turn):
        used = int((sizes > 0).sum())
        fixed = max(1, used // 4)
        moved = fixed + (places - fixed + turn * (used - fixed)) % max(1, amount - fixed)
        return jnp.zeros((amount,), jnp.int32).at[order[jnp.where(places < fixed, places, moved)]].set(jnp.asarray(sizes, jnp.int32))

    sizes = jnp.where(number % 4 == 0, named(packed, number // 4), named(common, number - number // 4 - 1))
    mixed = jax.random.permutation(jax.random.fold_in(own, 3), amount)
    source_of, sink = mixed[0:amount // 2 * 2:2], mixed[1:amount // 2 * 2:2]
    room = jnp.minimum(sizes[source_of] - 1, limit - sizes[sink]) // 2
    room = jnp.where((source_of == order[0]) | (sink == order[0]) | (sizes[sink] == 0), 0, jnp.maximum(room, 0))
    moved = jax.random.randint(jax.random.fold_in(own, 4), (amount // 2,), 0, 1 << 20) % (room + 1)
    sizes = sizes.at[source_of].add(-moved).at[sink].add(moved)
    items = jnp.searchsorted(jnp.cumsum(sizes), jnp.arange(rows * top), side="right").astype(jnp.int32)
    listing = items.reshape(top, rows).T
    listing = listing[jax.random.permutation(jax.random.fold_in(own, 1), rows)]
    turn = jax.random.randint(jax.random.fold_in(own, 2), (rows, 1), 0, top)
    return jnp.take_along_axis(listing, (jnp.arange(top)[None, :] + turn) % top, axis=1)


def portions_of(amount, total, limit, slope, full):
    weights = [(1 << 20) // math.isqrt(rank ** slope) + 1 for rank in range(1, amount + 1)]
    largest = limit if full else min(limit, max(-(-total // amount), total * weights[0] // sum(weights)))
    least = 1 if total - largest >= amount - 1 else 0
    counts, spare = [largest] + [least] * (amount - 1), total - largest - least * (amount - 1)
    while spare > 0:
        free = [i for i in range(1, amount) if counts[i] < largest] or [i for i in range(1, amount) if counts[i] < limit]
        whole, left = sum([weights[i] for i in free]), spare
        for i in free:
            addition = min(limit - counts[i], max(1, left * weights[i] // whole), spare)
            counts[i] = counts[i] + addition
            spare = spare - addition
    return np.array(counts)


def scatter_about(stream_key, extent, deviation, most, cuts=(), held_as=jnp.bfloat16):
    entries = deviation * jax.random.normal(stream_key, extent, jnp.float32)
    if cuts:
        entries = entries * block_scale(stream_key, extent, cuts, -0.22, 0.18)
    return jnp.clip(entries, -most, most).astype(held_as)


def setup_inputs(seed: int = 0, part: int = 0) -> dict:
    seeds = jax.random.split(jax.random.key(seed), 14)
    own_keys = jax.random.split(jax.random.fold_in(seeds[13], part), 14)
    queries = scatter_about(own_keys[0], (BLOCKS, BLOCK, SEQS, HEADS * HD), 1.0, 6.0, ((0, 16), (3, 4)))
    keys = scatter_about(own_keys[1], (BLOCKS, BLOCK, SEQS, KV_HEADS * HD), 1.0, 6.0, ((0, 16), (3, 4)))
    values = scatter_about(own_keys[2], (BLOCKS, BLOCK, SEQS, KV_HEADS * HD), 2.0, 12.0, ((0, 16), (3, 4)))
    q_gain = draw_q_gain(jax.random.fold_in(seeds[13], 71), part)
    k_gain = draw_k_gain(jax.random.fold_in(seeds[13], 71), part)
    out_weight = scatter_about(seeds[5], (HEADS * HD, D), (HEADS * HD) ** -0.5, 0.09375, ((0, 4), (1, 16)))
    hidden_in = scatter_about(own_keys[6], (BLOCKS, BLOCK, SEQS, D), 0.5, 3.0, ((0, 16), (1, 4)))
    norm_gain = jnp.clip(1.0 + 0.18 * jax.random.normal(seeds[7], (D,), jnp.float32), 0.1, 1.9)
    router = draw_router(jax.random.fold_in(seeds[13], 71), part)
    expert_ids_keys = jax.random.split(jax.random.fold_in(own_keys[9], 1), BLOCKS * BLOCK * SEQS // ROWS_DEV)
    expert_ids_turns = jax.random.permutation(jax.random.fold_in(own_keys[9], 3), BLOCKS * BLOCK * SEQS // ROWS_DEV)
    expert_ids = jax.vmap(lambda own, number: assign_block(jax.random.fold_in(own_keys[9], 2), own, number, ROWS_DEV, EXPERTS, TOPK, CAP, 2))(expert_ids_keys, expert_ids_turns).reshape((BLOCKS, BLOCK, SEQS, TOPK))
    w_gate = scatter_about(seeds[10], (EXPERTS, D, FF), D ** -0.5, 0.09375, ((0, 64),))
    w_up = scatter_about(seeds[11], (EXPERTS, D, FF), D ** -0.5, 0.09375, ((0, 64),))
    w_down = scatter_about(seeds[12], (EXPERTS, FF, D), FF ** -0.5, 0.21875, ((0, 64),))
    return {"queries": queries, "keys": keys, "values": values, "q_gain": q_gain, "k_gain": k_gain, "out_weight": out_weight, "hidden_in": hidden_in, "norm_gain": norm_gain, "router": router, "expert_ids": expert_ids, "w_gate": w_gate, "w_up": w_up, "w_down": w_down}


theta_base = 1000000.0
eps_norm = 1e-06
neg_fill = -1e+30

def head_norm(values_in, gain_vec):
    scale_row = lax.rsqrt(lax.optimization_barrier(jnp.mean(values_in * values_in, axis=-1, keepdims=True)) + eps_norm)
    return values_in * scale_row * gain_vec

def rotary(values_in, places):
    width_all = values_in.shape[-1]
    half_width = width_all // 2
    frequency = theta_base ** (-2.0 * jnp.arange(half_width, dtype=jnp.float32) / width_all)
    angles = places.astype(jnp.float32)[:, None] * frequency[None, :]
    tile_shape = (places.shape[0],) + (1,) * (values_in.ndim - 2) + (half_width,)
    cosine = jnp.cos(angles).reshape(tile_shape)
    sine_part = jnp.sin(angles).reshape(tile_shape)
    first_half = values_in[..., :half_width]
    second = values_in[..., half_width:]
    return jnp.concatenate([first_half * cosine - second * sine_part, second * cosine + first_half * sine_part], axis=-1)

def reference(queries, keys, values, q_gain, k_gain, out_weight, hidden_in, norm_gain, router, expert_ids, w_gate, w_up, w_down):
    length_all = BLOCKS * BLOCK
    group_size = HEADS // KV_HEADS
    score_scale = HD ** (-0.5)
    places = jnp.arange(length_all, dtype=jnp.int32)
    q_field = queries.reshape(length_all, SEQS, HEADS, HD).astype(jnp.float32)
    k_field = keys.reshape(length_all, SEQS, KV_HEADS, HD).astype(jnp.float32)
    q_ready = rotary(head_norm(q_field, q_gain), places).astype(jnp.bfloat16).reshape(length_all, SEQS, KV_HEADS, group_size, HD)
    k_ready = lax.optimization_barrier(rotary(head_norm(k_field, k_gain), places).astype(jnp.bfloat16)).astype(jnp.float32)
    v_all = values.reshape(length_all, SEQS, KV_HEADS, HD).astype(jnp.float32)
    step_len = math.gcd(length_all, 128)
    block_count = length_all // step_len

    def one_block(block_index):
        q_block = lax.optimization_barrier(lax.dynamic_slice_in_dim(q_ready, block_index * step_len, step_len, 0)).astype(jnp.float32)
        scores = jnp.einsum('pskgd,nskd->skgpn', q_block, k_ready) * score_scale
        q_places = block_index * step_len + jnp.arange(step_len, dtype=jnp.int32)
        allowed = places[None, :] <= q_places[:, None]
        scores = jnp.where(allowed, scores, neg_fill)
        row_top = lax.optimization_barrier(jnp.max(scores, axis=-1, keepdims=True))
        weights = jnp.where(allowed, jnp.exp(scores - row_top), 0.0)
        total_sum = lax.optimization_barrier(jnp.sum(weights, axis=-1))
        rounded = lax.optimization_barrier(weights.astype(jnp.bfloat16)).astype(jnp.float32)
        mixed_rows = jnp.einsum('skgpn,nskd->pskgd', rounded, v_all) / jnp.transpose(total_sum, (3, 0, 1, 2))[..., None]
        return mixed_rows.astype(jnp.bfloat16)
    attended = lax.map(one_block, jnp.arange(block_count, dtype=jnp.int32))
    row_count = length_all * SEQS
    attended = attended.reshape(row_count, HEADS * HD)
    projected = jnp.dot(attended, out_weight, preferred_element_type=jnp.float32)
    stream = (hidden_in.reshape(row_count, D).astype(jnp.float32) + projected).astype(jnp.bfloat16)
    stream_f = stream.astype(jnp.float32)
    normed = (stream_f * lax.rsqrt(lax.optimization_barrier(jnp.mean(stream_f * stream_f, axis=-1, keepdims=True)) + eps_norm) * norm_gain).astype(jnp.bfloat16)
    logits = jnp.dot(normed, router, preferred_element_type=jnp.float32)
    chosen = expert_ids.reshape(row_count, TOPK)
    catalog = jnp.arange(EXPERTS, dtype=jnp.int32)
    chosen_mask = chosen[:, :, None] == catalog[None, None, :]
    picked = lax.optimization_barrier(jnp.sum(jnp.where(chosen_mask, logits[:, None, :], 0.0), axis=-1))
    gate_weights = jax.nn.softmax(picked, axis=-1)
    pair_count = ROWS_DEV * TOPK
    device_blocks = row_count // ROWS_DEV
    grouped = chosen.reshape(device_blocks, pair_count)

    def slot_block(ids_row):
        hit_table = (ids_row[:, None] == catalog[None, :]).astype(jnp.int32)
        return lax.optimization_barrier(jnp.sum((jnp.cumsum(hit_table, axis=0) - hit_table) * hit_table, axis=1))
    slot_index = lax.map(slot_block, grouped)
    owners = jnp.arange(device_blocks, dtype=jnp.int32)[:, None] * CAP + slot_index
    total_pairs = row_count * TOPK
    pair_ids = jnp.arange(total_pairs, dtype=jnp.int32).reshape(device_blocks, pair_count)
    table = jnp.full((EXPERTS, device_blocks * CAP), total_pairs, jnp.int32).at[grouped, owners].set(pair_ids)
    normed_pad = jnp.concatenate([normed, jnp.zeros((1, D), jnp.bfloat16)], axis=0)
    gates_pad = jnp.concatenate([gate_weights.reshape(total_pairs), jnp.zeros((1,), jnp.float32)], axis=0)

    def per_expert(accum_state, expert):
        pair_pick = table[expert]
        row_index = (pair_pick // TOPK).astype(jnp.int32)
        inputs = normed_pad[row_index]
        gate_part = jnp.dot(inputs, w_gate[expert], preferred_element_type=jnp.float32)
        up_part = jnp.dot(inputs, w_up[expert], preferred_element_type=jnp.float32)
        inner_act = (jax.nn.silu(gate_part) * up_part).astype(jnp.bfloat16)
        expert_out = lax.optimization_barrier(jnp.dot(inner_act, w_down[expert], preferred_element_type=jnp.float32).astype(jnp.bfloat16)).astype(jnp.float32)
        accum_state = accum_state.at[row_index].add(gates_pad[pair_pick][:, None] * expert_out)
        return (accum_state, None)
    blended, _ = lax.scan(per_expert, jnp.zeros((row_count + 1, D), jnp.float32), jnp.arange(EXPERTS, dtype=jnp.int32))
    final_rows = (stream_f + blended[:row_count]).astype(jnp.bfloat16)
    return final_rows.reshape(BLOCKS, BLOCK, SEQS, D)
```

```python
import functools

import jax
import jax.numpy as jnp
from jax import lax
from jax.experimental import pallas as pl
from jax.experimental.pallas import tpu as pltpu
from jax.sharding import PartitionSpec as P


theta_base = 1000000.0
eps_norm = 1e-06
neg_fill = -1e30
LOG2E = 1.4426950408889634

BF = jnp.bfloat16
F32 = jnp.float32
HD = 128
PB = 256
SEQ = 2
DM = 4096
FF = 768
NE = 64
TOP = 8
ROWS = 128
SLOT = 16
NMAIN = NE * SLOT
NALL = NMAIN + NE
XR = 17 * 32
VMEM_BIG = 60 * 1024 * 1024


def spot(z, y):
    return (z % 4) * 4 + (y % 4)


def y_move(k):
    return [(spot(z, y), spot(z, y + k)) for z in range(4) for y in range(4)]


def z_move(k):
    return [(spot(z, y), spot(z + k, y)) for z in range(4) for y in range(4)]


CORE_SWAP = [(i, i ^ 1) for i in range(4)]
X_SWAP = [(i, i ^ 2) for i in range(4)]


def ring_four(x, move):
    return [x] + [lax.ppermute(x, "expert", move(k)) for k in (1, 2, 3)]


def grid_gather(first, second):
    a1 = jnp.stack(ring_four(first, y_move))
    b1 = jnp.stack(ring_four(second, z_move))
    return ring_four(a1, z_move), ring_four(b1, y_move)


def rotate_tables(positions):
    freq = theta_base ** (-2.0 * jnp.arange(HD // 2, dtype=F32) / HD)
    ang = positions.astype(F32)[:, None] * freq[None, :]
    cs, sn = jnp.cos(ang), jnp.sin(ang)
    return jnp.concatenate([cs, cs], axis=1), jnp.concatenate([-sn, sn], axis=1)


def attn_kernel(sc, q_ref, cos_ref, sin_ref, gain_ref, *rest):
    kv_in, (o_ref, kv, sem) = rest[:8], rest[8:]
    z, y = sc[2], sc[3]
    step = pl.program_id(0)

    @pl.when(step == 0)
    def _():
        copies = [pltpu.make_async_copy(kv_in[i], kv.at[i, :, 0], sem.at[i]) for i in range(4)]
        copies += [
            pltpu.make_async_copy(kv_in[4 + i], kv.at[:, i, 1], sem.at[4 + i]) for i in range(4)
        ]
        for cp in copies:
            cp.start()
        for cp in copies:
            cp.wait()

    s_lane = pl.multiple_of((step // 4) * HD, HD)
    v_lane = pl.multiple_of(2 * HD + (step // 4) * HD, HD)
    cs, sn, gain = cos_ref[...], sin_ref[...], gain_ref[...]
    heads = []
    for h in range(2):
        q = q_ref[:, h * HD : (h + 1) * HD].astype(F32)
        q = q * lax.rsqrt(jnp.mean(q * q, axis=-1, keepdims=True) + eps_norm) * gain
        heads.append((q * cs + pltpu.roll(q, HD // 2, 1) * sn).astype(BF))
    qq = jnp.concatenate(heads, axis=0)
    c2 = HD ** (-0.5) * LOG2E

    def part(dz, carry, masked):
        m_old, l_old, acc = carry
        k = kv[dz, :, :, :, pl.ds(s_lane, HD)].reshape(1024, HD)
        v = kv[dz, :, :, :, pl.ds(v_lane, HD)].reshape(1024, HD)
        s = lax.dot_general(qq, k, (((1,), (1,)), ((), ())), preferred_element_type=F32)
        if masked:
            key = lax.broadcasted_iota(jnp.int32, (1, 1024), 1)
            row = lax.broadcasted_iota(jnp.int32, (512, 1), 0) & (PB - 1)
            ahead = key >> 8
            limit = jnp.where(ahead == 0, key & 255, jnp.where(ahead <= y, -1, PB))
            s = jnp.where(limit <= row, s, neg_fill)
        m_new = jnp.maximum(m_old, jnp.max(s, axis=-1, keepdims=True))
        p = jnp.exp2((s - m_new) * c2)
        alpha = jnp.exp2((m_old - m_new) * c2)
        l_new = l_old * alpha + jnp.sum(p, axis=-1, keepdims=True)
        acc = acc * alpha + jnp.dot(p.astype(BF), v, preferred_element_type=F32)
        return m_new, l_new, acc

    start = (
        jnp.full((512, 1), neg_fill, F32),
        jnp.zeros((512, 1), F32),
        jnp.zeros((512, HD), F32),
    )
    state = part(0, start, True)
    state = lax.fori_loop(1, z + 1, lambda i, c: part(i, c, False), state)
    out = (state[2] / state[1]).astype(BF)
    o_ref[:, 0:HD] = out[:PB]
    o_ref[:, HD : 2 * HD] = out[PB:]


def attention(scal, q2, cs, sn, gain, ka, kb):
    whole = lambda i, sc: (0, 0)
    return pl.pallas_call(
        attn_kernel,
        out_shape=jax.ShapeDtypeStruct((PB, SEQ * 1024), BF),
        grid_spec=pltpu.PrefetchScalarGridSpec(
            num_scalar_prefetch=1,
            grid=(8,),
            in_specs=[
                pl.BlockSpec((PB, 256), lambda i, sc: (0, i)),
                pl.BlockSpec((PB, HD), whole),
                pl.BlockSpec((PB, HD), whole),
                pl.BlockSpec((1, HD), whole),
            ]
            + [pl.BlockSpec(memory_space=pl.ANY)] * 8,
            out_specs=pl.BlockSpec((PB, 256), lambda i, sc: (0, i)),
            scratch_shapes=[
                pltpu.VMEM((4, 4, 2, 128, 512), BF),
                pltpu.SemaphoreType.DMA((8,)),
            ],
        ),
        compiler_params=pltpu.CompilerParams(vmem_limit_bytes=VMEM_BIG),
        cost_estimate=pl.CostEstimate(
            flops=8 * 2**30, bytes_accessed=8 * 2**20, transcendentals=16 * 2**20
        ),
        name="attend",
    )(scal, q2, cs, sn, gain, *ka, *kb)


def proj_kernel(sc, a_ref, *rest):
    w_in, (keep, send, lhs, w, sem) = rest[:8], rest[8:]
    c, xh, z, y = sc[0], sc[1], sc[2], sc[3]
    first = [
        pltpu.make_async_copy(w_in[4 + i], w.at[:, i, pl.ds(512, 512)], sem.at[4 + i])
        for i in range(4)
    ]
    later = [
        pltpu.make_async_copy(w_in[i], w.at[i, :, pl.ds(0, 512)], sem.at[i]) for i in range(4)
    ]
    for cp in first + later:
        cp.start()
    for cc in range(2):
        for xx in range(2):
            base = pl.multiple_of(64 * (2 * (xh ^ xx) + (c ^ cc)), 64)
            for s in range(SEQ):
                at = cc * 256 + xx * 128 + s * 64
                lhs[at : at + 64, :] = a_ref[pl.ds(base, 64), s * 1024 : (s + 1) * 1024]
    for cp in first:
        cp.wait()
    for dz in range(4):
        later[dz].wait()
        for dy in range(4):
            col = ((z - dz) & 3) * 4 + ((y - dy) & 3)
            res = jnp.dot(lhs[...], w[dz, dy], preferred_element_type=F32).astype(BF)
            lane = pl.multiple_of(col * 256, 256)
            keep[:, pl.ds(lane, 256)] = res[:256]
            send[:, pl.ds(lane, 256)] = res[256:]


def project(scal, attn, wa, wb):
    full = pl.BlockSpec(memory_space=pltpu.VMEM)
    return pl.pallas_call(
        proj_kernel,
        out_shape=(
            jax.ShapeDtypeStruct((256, DM), BF),
            jax.ShapeDtypeStruct((256, DM), BF),
        ),
        in_specs=[pl.BlockSpec(memory_space=pltpu.SMEM), full]
        + [pl.BlockSpec(memory_space=pl.ANY)] * 8,
        out_specs=(full, full),
        scratch_shapes=[
            pltpu.VMEM((512, 1024), BF),
            pltpu.VMEM((4, 4, 1024, 256), BF),
            pltpu.SemaphoreType.DMA((8,)),
        ],
        compiler_params=pltpu.CompilerParams(vmem_limit_bytes=VMEM_BIG),
        cost_estimate=pl.CostEstimate(
            flops=4 * 2**30, bytes_accessed=13 * 2**20, transcendentals=0
        ),
        name="project",
    )(scal, attn, *wa, *wb)


def dispatch_kernel(k_ref, g_ref, r_ref, h_ref, gain_ref, tgt_ref, st_ref, nm_ref, x_ref):
    total = (
        h_ref[...].astype(F32)
        + (k_ref[...].astype(F32) + g_ref[...].astype(F32))
        + r_ref[...].astype(F32)
    )
    st = total.astype(BF)
    st_ref[...] = st
    sf = st.astype(F32)
    scale = lax.rsqrt(jnp.mean(sf * sf, axis=-1, keepdims=True) + eps_norm)
    nm_ref[...] = (sf * scale * gain_ref[...]).astype(BF)
    line = lax.broadcasted_iota(jnp.int32, (NALL, ROWS), 0)
    hit = jnp.zeros((NALL, ROWS), F32)
    for k in range(TOP):
        hit = jnp.where(line == tgt_ref[k : k + 1, :], 1.0, hit)
    pick = hit.astype(BF)
    for j in range(8):
        n = nm_ref[:, j * 512 : (j + 1) * 512]
        main = jnp.dot(pick[:NMAIN], n, preferred_element_type=F32).astype(BF)
        for i in range(4):
            f = 4 * j + i
            x_ref[:, f * SLOT : (f + 1) * SLOT, :] = main[:, i * 128 : (i + 1) * 128].reshape(
                NE, SLOT, 128
            )
    ov = jnp.dot(pick[NMAIN:], nm_ref[...], preferred_element_type=F32).astype(BF)
    x_ref[:, 512:544, :] = ov.reshape(NE, 32, 128)


def dispatch(keep, got, rest, hid, gain, tgt_t):
    half = pl.BlockSpec((128, DM), lambda i: (0, 0))
    return pl.pallas_call(
        dispatch_kernel,
        grid=(1,),
        out_shape=(
            jax.ShapeDtypeStruct((ROWS, DM), BF),
            jax.ShapeDtypeStruct((ROWS, DM), BF),
            jax.ShapeDtypeStruct((NE, XR, 128), BF),
        ),
        in_specs=[
            half,
            half,
            half,
            half,
            pl.BlockSpec((1, DM), lambda i: (0, 0)),
            pl.BlockSpec((TOP, ROWS), lambda i: (0, 0)),
        ],
        out_specs=(half, half, pl.BlockSpec((NE, XR, 128), lambda i: (0, 0, 0))),
        compiler_params=pltpu.CompilerParams(vmem_limit_bytes=VMEM_BIG),
        cost_estimate=pl.CostEstimate(
            flops=2**30, bytes_accessed=14 * 2**20, transcendentals=0
        ),
        name="dispatch",
    )(keep, got, rest, hid, gain, tgt_t)


def expert_kernel(x_ref, xo_ref, wg_ref, wu_ref, wd_ref, y_hbm, ga, ua, inner, xov, yb, yo, sem):
    step = pl.program_id(0)

    @pl.when(step == 0)
    def _():
        xov[...] = xo_ref[...].reshape(NE, DM)

    @pl.when(step < 4)
    def _():
        pieces = [
            x_ref[:, i * SLOT : (i + 1) * SLOT, :].reshape(NMAIN, 128) for i in range(8)
        ]
        main = jnp.concatenate(pieces, axis=1)
        lane = pl.multiple_of(step * 1024, 1024)
        rows = jnp.concatenate([main, xov[:, pl.ds(lane, 1024)]], axis=0)
        g = jnp.dot(rows, wg_ref[0], preferred_element_type=F32)
        u = jnp.dot(rows, wu_ref[0], preferred_element_type=F32)

        @pl.when(step == 0)
        def _():
            ga[...] = g
            ua[...] = u

        @pl.when(step > 0)
        def _():
            ga[...] += g
            ua[...] += u

    @pl.when(step == 4)
    def _():
        g = ga[...]
        inner[...] = (g / (1.0 + jnp.exp(-g)) * ua[...]).astype(BF)

    for j in range(4):

        @pl.when(step == 4 + j)
        def _(j=j):
            slot = j % 2
            out = jnp.dot(inner[...], wd_ref[0], preferred_element_type=F32).astype(BF)
            if j >= 2:
                pltpu.make_async_copy(
                    yb.at[slot], y_hbm.at[:, pl.ds((j - 2) * 128, 128)], sem.at[slot]
                ).wait()
            for i in range(8):
                yb[slot, :, i * SLOT : (i + 1) * SLOT, :] = out[
                    :NMAIN, i * 128 : (i + 1) * 128
                ].reshape(NE, SLOT, 128)
            xov[:, j * 1024 : (j + 1) * 1024] = out[NMAIN:]
            pltpu.make_async_copy(
                yb.at[slot], y_hbm.at[:, pl.ds(j * 128, 128)], sem.at[slot]
            ).start()
            if j == 3:
                yo[...] = xov[...].reshape(NE, 32, 128)
                last = pltpu.make_async_copy(yo, y_hbm.at[:, pl.ds(512, 32)], sem.at[2])
                last.start()
                for k in (2, 3):
                    pltpu.make_async_copy(
                        yb.at[k % 2], y_hbm.at[:, pl.ds(k * 128, 128)], sem.at[k % 2]
                    ).wait()
                last.wait()


def run_experts(x, wg, wu, wd):
    lo = lambda i: jnp.minimum(i, 3)
    return pl.pallas_call(
        expert_kernel,
        grid=(8,),
        out_shape=jax.ShapeDtypeStruct((NE, XR, 128), BF),
        in_specs=[
            pl.BlockSpec((NE, 128, 128), lambda i: (0, lo(i), 0)),
            pl.BlockSpec((NE, 32, 128), lambda i: (0, 16, 0)),
            pl.BlockSpec((1, 1024, FF), lambda i: (0, lo(i), 0)),
            pl.BlockSpec((1, 1024, FF), lambda i: (0, lo(i), 0)),
            pl.BlockSpec((1, FF, 1024), lambda i: (0, 0, jnp.maximum(i - 4, 0))),
        ],
        out_specs=pl.BlockSpec(memory_space=pl.ANY),
        scratch_shapes=[
            pltpu.VMEM((NALL, FF), F32),
            pltpu.VMEM((NALL, FF), F32),
            pltpu.VMEM((NALL, FF), BF),
            pltpu.VMEM((NE, DM), BF),
            pltpu.VMEM((2, NE, 128, 128), BF),
            pltpu.VMEM((NE, 32, 128), BF),
            pltpu.SemaphoreType.DMA((3,)),
        ],
        compiler_params=pltpu.CompilerParams(vmem_limit_bytes=VMEM_BIG),
        cost_estimate=pl.CostEstimate(
            flops=20 * 2**30, bytes_accessed=36 * 2**20, transcendentals=2**20
        ),
        name="experts",
    )(x, x, wg, wu, wd)


def combine_kernel(y_ref, yo_ref, st_ref, tgt_ref, gate_ref, o_ref, gm, go, yov):
    step = pl.program_id(0)

    @pl.when(step == 0)
    def _():
        yov[...] = yo_ref[...].reshape(NE, DM)
        lane = lax.broadcasted_iota(jnp.int32, (ROWS, NALL), 1)
        mix = jnp.zeros((ROWS, NALL), F32)
        for k in range(TOP):
            mix = jnp.where(lane == tgt_ref[:, k : k + 1], gate_ref[:, k : k + 1], mix)
        hi = mix.astype(BF)
        lo = (mix - hi.astype(F32)).astype(BF)
        gm[:ROWS] = hi[:, :NMAIN]
        gm[ROWS:] = lo[:, :NMAIN]
        go[:ROWS] = hi[:, NMAIN:]
        go[ROWS:] = lo[:, NMAIN:]

    pieces = [y_ref[:, i * SLOT : (i + 1) * SLOT, :].reshape(NMAIN, 128) for i in range(8)]
    main = jnp.concatenate(pieces, axis=1)
    at = pl.multiple_of(step * 1024, 1024)
    both = jnp.dot(gm[...], main, preferred_element_type=F32) + jnp.dot(
        go[...], yov[:, pl.ds(at, 1024)], preferred_element_type=F32
    )
    o_ref[...] = (st_ref[...].astype(F32) + (both[:ROWS] + both[ROWS:])).astype(BF)


def combine(y, stream, tgt, gates):
    return pl.pallas_call(
        combine_kernel,
        grid=(4,),
        out_shape=jax.ShapeDtypeStruct((ROWS, DM), BF),
        in_specs=[
            pl.BlockSpec((NE, 128, 128), lambda i: (0, i, 0)),
            pl.BlockSpec((NE, 32, 128), lambda i: (0, 16, 0)),
            pl.BlockSpec((ROWS, 1024), lambda i: (0, i)),
            pl.BlockSpec((ROWS, TOP), lambda i: (0, 0)),
            pl.BlockSpec((ROWS, TOP), lambda i: (0, 0)),
        ],
        out_specs=pl.BlockSpec((ROWS, 1024), lambda i: (0, i)),
        scratch_shapes=[
            pltpu.VMEM((2 * ROWS, NMAIN), BF),
            pltpu.VMEM((2 * ROWS, NE), BF),
            pltpu.VMEM((NE, DM), BF),
        ],
        compiler_params=pltpu.CompilerParams(vmem_limit_bytes=VMEM_BIG),
        cost_estimate=pl.CostEstimate(
            flops=2 * 2**30, bytes_accessed=11 * 2**20, transcendentals=0
        ),
        name="combine",
    )(y, y, stream, tgt, gates)


def slots(ids):
    catalog = jnp.arange(NE, dtype=jnp.int32)
    hits = jnp.any(ids[:, :, None] == catalog, axis=1).astype(BF)
    below = (jnp.arange(ROWS)[:, None] > jnp.arange(ROWS)[None, :]).astype(BF)
    before = jnp.dot(below, hits, preferred_element_type=F32)
    slot = jnp.sum(
        jnp.where(ids[:, :, None] == catalog, before[:, None, :], 0.0), axis=-1
    ).astype(jnp.int32)
    return jnp.where(slot < SLOT, ids * SLOT + slot, NMAIN + ids)


def on_device(
    queries,
    keys,
    values,
    q_gain,
    k_gain,
    out_weight,
    hidden_in,
    norm_gain,
    router,
    expert_ids,
    w_gate,
    w_up,
    w_down,
):
    t, e = lax.axis_index("tensor"), lax.axis_index("expert")
    scal = jnp.stack([t % 2, t // 2, e // 4, e % 4]).astype(jnp.int32)
    cs, sn = rotate_tables(e * PB + jnp.arange(PB, dtype=jnp.int32))

    k = keys[0].astype(F32)
    k = k * lax.rsqrt(jnp.mean(k * k, axis=-1, keepdims=True) + eps_norm) * k_gain
    turned = jnp.concatenate([k[..., HD // 2 :], k[..., : HD // 2]], axis=-1)
    k = (k * cs[:, None, :] + turned * sn[:, None, :]).astype(BF)
    kv = jnp.concatenate([k.reshape(PB, SEQ * HD), values[0].reshape(PB, SEQ * HD)], axis=1)
    ka, kb = grid_gather(kv[:128], kv[128:])
    wa, wb = grid_gather(out_weight[:512], out_weight[512:])

    q2 = queries[0].reshape(PB, SEQ * 1024)
    ids = jnp.transpose(expert_ids[0], (1, 0, 2)).reshape(ROWS, TOP)
    tgt = slots(ids)
    hid = jnp.transpose(hidden_in[0], (1, 0, 2)).reshape(ROWS, DM)

    attn = attention(scal, q2, cs, sn, q_gain.reshape(1, HD), ka, kb)
    keep, send = project(scal, attn, wa, wb)
    got = lax.ppermute(send, "tensor", CORE_SWAP)
    other = (keep[128:].astype(F32) + got[128:].astype(F32)).astype(BF)
    rest = lax.ppermute(other, "tensor", X_SWAP)
    stream, normed, x = dispatch(
        keep, got, rest, hid, norm_gain.reshape(1, DM), jnp.transpose(tgt)
    )
    arrived = lax.all_to_all(x, ("tensor", "expert"), split_axis=0, concat_axis=0, tiled=True)

    logits = jnp.dot(normed, router, preferred_element_type=F32)
    chosen = ids[:, :, None] == jnp.arange(NE, dtype=jnp.int32)
    gates = jax.nn.softmax(jnp.sum(jnp.where(chosen, logits[:, None, :], 0.0), axis=-1), axis=-1)

    done = run_experts(arrived, w_gate, w_up, w_down)
    back = lax.all_to_all(done, ("tensor", "expert"), split_axis=0, concat_axis=0, tiled=True)
    out = combine(back, stream, tgt, gates)
    return jnp.transpose(out.reshape(SEQ, 64, DM), (1, 0, 2))[None]


def solution(mesh):
    return jax.shard_map(
        on_device,
        mesh=mesh,
        in_specs=(
            P(("dp", "expert"), None, None, "tensor"),
            P(("dp", "expert"), None, None, "tensor"),
            P(("dp", "expert"), None, None, "tensor"),
            P(),
            P(),
            P("tensor", "expert"),
            P(("dp", "expert"), "tensor", None, None),
            P(),
            P(),
            P(("dp", "expert"), "tensor", None, None),
            P(("tensor", "expert"), None, None),
            P(("tensor", "expert"), None, None),
            P(("tensor", "expert"), None, None),
        ),
        out_specs=P(("dp", "expert"), "tensor", None, None),
        check_vma=False,
    )
```

```python
import functools

import jax
import jax.numpy as jnp
from jax import lax
from jax.experimental import pallas as pl
from jax.experimental.pallas import tpu as pltpu
from jax.sharding import PartitionSpec as P


theta_base = 1000000.0
eps_norm = 1e-06
neg_fill = -1e30
LOG2E = 1.4426950408889634

BF = jnp.bfloat16
F32 = jnp.float32
HD = 128
PB = 256
SEQ = 2
DM = 4096
FF = 768
NE = 64
TOP = 8
ROWS = 128
SLOT = 16
NMAIN = NE * SLOT
NALL = NMAIN + NE
XR = 17 * 32
VMEM_BIG = 60 * 1024 * 1024


def spot(z, y):
    return (z % 4) * 4 + (y % 4)


def y_move(k):
    return [(spot(z, y), spot(z, y + k)) for z in range(4) for y in range(4)]


def z_move(k):
    return [(spot(z, y), spot(z + k, y)) for z in range(4) for y in range(4)]


CORE_SWAP = [(i, i ^ 1) for i in range(4)]
X_SWAP = [(i, i ^ 2) for i in range(4)]


def ring_four(x, move):
    return [x] + [lax.ppermute(x, "expert", move(k)) for k in (1, 2, 3)]


def ring_relay(x, move):
    half = x.shape[0] // 2
    left = lax.ppermute(x, "expert", move(1))
    right = lax.ppermute(x, "expert", move(3))
    lo = lax.ppermute(left[:half], "expert", move(1))
    hi = lax.ppermute(right[half:], "expert", move(3))
    return x, left, right, lo, hi


def rotate_tables(positions):
    freq = theta_base ** (-2.0 * jnp.arange(HD // 2, dtype=F32) / HD)
    ang = positions.astype(F32)[:, None] * freq[None, :]
    cs, sn = jnp.cos(ang), jnp.sin(ang)
    return jnp.concatenate([cs, cs], axis=1), jnp.concatenate([-sn, sn], axis=1)


def keys_kernel(k_ref, v_ref, cos_ref, sin_ref, gain_ref, o_ref):
    cs, sn, gain = cos_ref[...], sin_ref[...], gain_ref[...]
    for s in range(SEQ):
        k = k_ref[:, s * HD : (s + 1) * HD].astype(F32)
        k = k * lax.rsqrt(jnp.mean(k * k, axis=-1, keepdims=True) + eps_norm) * gain
        at = 2 * s * HD
        o_ref[:, at : at + HD] = (k * cs + pltpu.roll(k, HD // 2, 1) * sn).astype(BF)
        o_ref[:, at + HD : at + 2 * HD] = v_ref[:, s * HD : (s + 1) * HD]


def ready_keys(k2, v2, cs, sn, gain):
    return pl.pallas_call(
        keys_kernel, out_shape=jax.ShapeDtypeStruct((PB, 4 * HD), BF), name="ready_keys"
    )(k2, v2, cs, sn, gain)


C2 = HD ** (-0.5) * LOG2E


def attn_part(q, k, v_wide, state, limit):
    m_old, l_old, acc = state
    s = lax.dot_general(q, k, (((1,), (1,)), ((), ())), preferred_element_type=F32)
    if limit is not None:
        row = lax.broadcasted_iota(jnp.int32, (PB, 1), 0)
        s = jnp.where(limit <= row, s, neg_fill)
    m_new = jnp.maximum(m_old, jnp.max(s, axis=-1, keepdims=True))
    p = jnp.exp2((s - m_new) * C2).astype(BF)
    alpha = jnp.exp2((m_old - m_new) * C2)
    pv = jnp.dot(p, v_wide, preferred_element_type=F32)
    return m_new, l_old * alpha + pv[:, HD : HD + 1], acc * alpha + pv[:, :HD]


def keys_of(kv):
    k = kv[:, :HD]
    v = kv[:, HD : 2 * HD]
    return k, jnp.concatenate([v, jnp.ones_like(v)], axis=1)


def put_state(ml_ref, acc_ref, states):
    lane = lax.broadcasted_iota(jnp.int32, (PB, HD), 1)
    (m0, l0, a0), (m1, l1, a1) = states
    ml_ref[...] = jnp.where(
        lane == 0, m0, jnp.where(lane == 1, l0, jnp.where(lane == 2, m1, l1))
    )
    acc_ref[:, :HD] = a0
    acc_ref[:, HD:] = a1


def get_state(ml_ref, acc_ref):
    return [
        (ml_ref[:, 2 * h : 2 * h + 1], ml_ref[:, 2 * h + 1 : 2 * h + 2],
         acc_ref[:, h * HD : (h + 1) * HD])
        for h in range(2)
    ]


def attn_first(sc, q_ref, cos_ref, sin_ref, gain_ref, kv_ref, qr_ref, ml_ref, acc_ref):
    y = sc[3]
    cs, sn, gain = cos_ref[...], sin_ref[...], gain_ref[...]
    k, v = keys_of(kv_ref[...].reshape(1024, 256))
    key = lax.broadcasted_iota(jnp.int32, (1, 1024), 1)
    ahead = key >> 8
    limit = jnp.where(ahead == 0, key & 255, jnp.where(ahead <= y, -1, PB))
    states = []
    for h in range(2):
        q = q_ref[:, h * HD : (h + 1) * HD].astype(F32)
        q = q * lax.rsqrt(jnp.mean(q * q, axis=-1, keepdims=True) + eps_norm) * gain
        q = (q * cs + pltpu.roll(q, HD // 2, 1) * sn).astype(BF)
        qr_ref[:, h * HD : (h + 1) * HD] = q
        start = (
            jnp.full((PB, 1), neg_fill, F32),
            jnp.zeros((PB, 1), F32),
            jnp.zeros((PB, HD), F32),
        )
        states.append(attn_part(q, k, v, start, limit))
    put_state(ml_ref, acc_ref, states)


def attn_next(sc, q_ref, ml_in, acc_in, ka_ref, kb_ref, ml_ref, acc_ref):
    z = sc[2]
    ml_ref[...] = ml_in[...]
    acc_ref[...] = acc_in[...]
    for need, kv_ref in ((1, ka_ref), (3, kb_ref)):

        @pl.when(z >= need)
        def _(kv_ref=kv_ref):
            k, v = keys_of(kv_ref[...].reshape(1024, 256))
            states = [
                attn_part(q_ref[:, h * HD : (h + 1) * HD], k, v, st, None)
                for h, st in enumerate(get_state(ml_ref, acc_ref))
            ]
            put_state(ml_ref, acc_ref, states)


def attn_last(sc, q_ref, ml_in, acc_in, ka_ref, kb_ref, o_ref):
    z = sc[2]

    def finish(states):
        for h, (_, total, acc) in enumerate(states):
            o_ref[:, h * HD : (h + 1) * HD] = (acc / total).astype(BF)

    @pl.when(z >= 2)
    def _():
        kv = jnp.concatenate(
            [ka_ref[...].reshape(512, 256), kb_ref[...].reshape(512, 256)], axis=0
        )
        k, v = keys_of(kv)
        finish(
            [
                attn_part(q_ref[:, h * HD : (h + 1) * HD], k, v, st, None)
                for h, st in enumerate(get_state(ml_in, acc_in))
            ]
        )

    @pl.when(z < 2)
    def _():
        finish(get_state(ml_in, acc_in))


Q_SPEC = pl.BlockSpec((PB, 256), lambda i, sc: (0, i))
ML_SPEC = pl.BlockSpec((PB, HD), lambda i, sc: (0, i))


def kv_spec(n):
    return pl.BlockSpec((n, PB, 256), lambda i, sc: (0, 0, i // 4))


def attn_call(kernel, in_specs, out_specs, out_shape, parts):
    return pl.pallas_call(
        kernel,
        out_shape=out_shape,
        grid_spec=pltpu.PrefetchScalarGridSpec(
            num_scalar_prefetch=1, grid=(8,), in_specs=in_specs, out_specs=out_specs
        ),
        compiler_params=pltpu.CompilerParams(vmem_limit_bytes=VMEM_BIG),
        cost_estimate=pl.CostEstimate(
            flops=parts * 4 * 2**30, bytes_accessed=8 * 2**20, transcendentals=parts * 4 * 2**20
        ),
    )


STATE = (
    jax.ShapeDtypeStruct((PB, 8 * HD), F32),
    jax.ShapeDtypeStruct((PB, SEQ * 1024), F32),
)


def attention(scal, q2, cs, sn, gain, pieces):
    own, left, right, lo, hi = pieces
    table = pl.BlockSpec((PB, HD), lambda i, sc: (0, 0))
    qr, ml, acc = attn_call(
        attn_first,
        [Q_SPEC, table, table, pl.BlockSpec((1, HD), lambda i, sc: (0, 0)), kv_spec(4)],
        (Q_SPEC, ML_SPEC, Q_SPEC),
        (jax.ShapeDtypeStruct((PB, SEQ * 1024), BF),) + STATE,
        1,
    )(scal, q2, cs, sn, gain, own)
    ml, acc = attn_call(
        attn_next, [Q_SPEC, ML_SPEC, Q_SPEC, kv_spec(4), kv_spec(4)], (ML_SPEC, Q_SPEC), STATE, 2
    )(scal, qr, ml, acc, left, right)
    return attn_call(
        attn_last,
        [Q_SPEC, ML_SPEC, Q_SPEC, kv_spec(2), kv_spec(2)],
        Q_SPEC,
        jax.ShapeDtypeStruct((PB, SEQ * 1024), BF),
        1,
    )(scal, qr, ml, acc, lo, hi)


WA = 768
WB = 1024 - WA


def proj_kernel(part, sc, a_ref, *rest):
    n_in = 6 if part == 0 else 7
    w_in, (keep, send, lhs, w, sem) = rest[:n_in], rest[n_in:]
    c, xh = sc[0], sc[1]
    top, low = pl.ds(0, WA), pl.ds(WA, WB)
    two = pl.ds(2 * part, 2)
    moves = [
        (w_in[0].at[two], w.at[:, 0, top]),
        (w_in[1].at[two], w.at[:, 1, top]),
        (w_in[2].at[two], w.at[:, 3, top]),
        (w_in[3], w.at[:, 2, top]),
    ]
    if part == 0:
        moves += [(w_in[4], w.at[0, :, low]), (w_in[5], w.at[1, :, low])]
    else:
        moves += [
            (w_in[4], w.at[1, :, low]),
            (w_in[5], w.at[0, pl.ds(0, 2), low]),
            (w_in[6], w.at[0, pl.ds(2, 2), low]),
        ]
    copies = [pltpu.make_async_copy(a, b, sem.at[i]) for i, (a, b) in enumerate(moves)]
    for cp in copies:
        cp.start()
    for cc in range(2):
        for xx in range(2):
            base = pl.multiple_of(64 * (2 * (xh ^ xx) + (c ^ cc)), 64)
            for s in range(SEQ):
                at = cc * 256 + xx * 128 + s * 64
                lhs[at : at + 64, :] = a_ref[pl.ds(base, 64), s * 1024 : (s + 1) * 1024]
    for cp in copies:
        cp.wait()
    for i in range(2):
        for dy in range(4):
            res = jnp.dot(lhs[...], w[i, dy], preferred_element_type=F32).astype(BF)
            lane = (i * 4 + dy) * 256
            keep[:, lane : lane + 256] = res[:256]
            send[:, lane : lane + 256] = res[256:]


def project(part, scal, attn, pa, pb):
    pieces = list(pa[:3]) + [pa[3 + part]]
    pieces += [pb[0], pb[1]] if part == 0 else [pb[2], pb[3], pb[4]]
    full = pl.BlockSpec(memory_space=pltpu.VMEM)
    return pl.pallas_call(
        functools.partial(proj_kernel, part),
        out_shape=(
            jax.ShapeDtypeStruct((256, DM // 2), BF),
            jax.ShapeDtypeStruct((256, DM // 2), BF),
        ),
        in_specs=[pl.BlockSpec(memory_space=pltpu.SMEM), full]
        + [pl.BlockSpec(memory_space=pl.ANY)] * len(pieces),
        out_specs=(full, full),
        scratch_shapes=[
            pltpu.VMEM((512, 1024), BF),
            pltpu.VMEM((2, 4, 1024, 256), BF),
            pltpu.SemaphoreType.DMA((8,)),
        ],
        compiler_params=pltpu.CompilerParams(vmem_limit_bytes=VMEM_BIG),
        cost_estimate=pl.CostEstimate(
            flops=2 * 2**30, bytes_accessed=7 * 2**20, transcendentals=0
        ),
    )(scal, attn, *pieces)


def dispatch_kernel(
    sc, k0, k1, g0, g1, r0, r1, h_ref, gain_ref, tgt_ref, st_ref, nm_ref, x_ref
):
    z, y = sc[2], sc[3]
    square = jnp.zeros((ROWS, 1), F32)
    for dz in range(4):
        k_ref, g_ref, r_ref = (k0, g0, r0) if dz < 2 else (k1, g1, r1)
        for dy in range(4):
            here = (dz & 1) * 1024 + dy * 256
            there = pl.multiple_of((((z - dz) & 3) * 4 + ((y - dy) & 3)) * 256, 256)
            span = slice(here, here + 256)
            total = (
                h_ref[:, pl.ds(there, 256)].astype(F32)
                + (k_ref[:, span].astype(F32) + g_ref[:, span].astype(F32))
                + r_ref[:, span].astype(F32)
            )
            st = total.astype(BF)
            st_ref[:, pl.ds(there, 256)] = st
            sf = st.astype(F32)
            square = square + jnp.sum(sf * sf, axis=-1, keepdims=True)
    scale = lax.rsqrt(square / DM + eps_norm)
    nm_ref[...] = (st_ref[...].astype(F32) * scale * gain_ref[...]).astype(BF)
    line = lax.broadcasted_iota(jnp.int32, (NALL, ROWS), 0)
    hit = jnp.zeros((NALL, ROWS), F32)
    for k in range(TOP):
        hit = jnp.where(line == tgt_ref[k : k + 1, :], 1.0, hit)
    pick = hit.astype(BF)
    for j in range(8):
        n = nm_ref[:, j * 512 : (j + 1) * 512]
        main = jnp.dot(pick[:NMAIN], n, preferred_element_type=F32).astype(BF)
        for i in range(4):
            f = 4 * j + i
            x_ref[:, f * SLOT : (f + 1) * SLOT, :] = main[:, i * 128 : (i + 1) * 128].reshape(
                NE, SLOT, 128
            )
    ov = jnp.dot(pick[NMAIN:], nm_ref[...], preferred_element_type=F32).astype(BF)
    x_ref[:, 512:544, :] = ov.reshape(NE, 32, 128)


def dispatch(scal, keeps, gots, rests, hid, gain, tgt_t):
    at = lambda i, sc: (0, 0)
    half = pl.BlockSpec((ROWS, DM // 2), at)
    line = pl.BlockSpec((ROWS, DM), at)
    return pl.pallas_call(
        dispatch_kernel,
        out_shape=(
            jax.ShapeDtypeStruct((ROWS, DM), BF),
            jax.ShapeDtypeStruct((ROWS, DM), BF),
            jax.ShapeDtypeStruct((NE, XR, 128), BF),
        ),
        grid_spec=pltpu.PrefetchScalarGridSpec(
            num_scalar_prefetch=1,
            grid=(1,),
            in_specs=[half] * 6
            + [line, pl.BlockSpec((1, DM), at), pl.BlockSpec((TOP, ROWS), at)],
            out_specs=(line, line, pl.BlockSpec((NE, XR, 128), lambda i, sc: (0, 0, 0))),
        ),
        compiler_params=pltpu.CompilerParams(vmem_limit_bytes=VMEM_BIG),
        cost_estimate=pl.CostEstimate(
            flops=2**30, bytes_accessed=14 * 2**20, transcendentals=0
        ),
        name="dispatch",
    )(scal, *keeps, *gots, *rests, hid, gain, tgt_t)


def expert_kernel(x_ref, xo_ref, wg_ref, wu_ref, wd_ref, y_hbm, ga, ua, inner, xov, yb, yo, sem):
    step = pl.program_id(0)

    @pl.when(step == 0)
    def _():
        xov[...] = xo_ref[...].reshape(NE, DM)

    @pl.when(step < 4)
    def _():
        pieces = [
            x_ref[:, i * SLOT : (i + 1) * SLOT, :].reshape(NMAIN, 128) for i in range(8)
        ]
        main = jnp.concatenate(pieces, axis=1)
        lane = pl.multiple_of(step * 1024, 1024)
        rows = jnp.concatenate([main, xov[:, pl.ds(lane, 1024)]], axis=0)
        g = jnp.dot(rows, wg_ref[0], preferred_element_type=F32)
        u = jnp.dot(rows, wu_ref[0], preferred_element_type=F32)

        @pl.when(step == 0)
        def _():
            ga[...] = g
            ua[...] = u

        @pl.when(step > 0)
        def _():
            ga[...] += g
            ua[...] += u

    @pl.when(step == 4)
    def _():
        g = ga[...]
        inner[...] = (g / (1.0 + jnp.exp(-g)) * ua[...]).astype(BF)

    for j in range(4):

        @pl.when(step == 4 + j)
        def _(j=j):
            slot = j % 2
            out = jnp.dot(inner[...], wd_ref[0], preferred_element_type=F32).astype(BF)
            if j >= 2:
                pltpu.make_async_copy(
                    yb.at[slot], y_hbm.at[:, pl.ds((j - 2) * 128, 128)], sem.at[slot]
                ).wait()
            for i in range(8):
                yb[slot, :, i * SLOT : (i + 1) * SLOT, :] = out[
                    :NMAIN, i * 128 : (i + 1) * 128
                ].reshape(NE, SLOT, 128)
            xov[:, j * 1024 : (j + 1) * 1024] = out[NMAIN:]
            pltpu.make_async_copy(
                yb.at[slot], y_hbm.at[:, pl.ds(j * 128, 128)], sem.at[slot]
            ).start()
            if j == 3:
                yo[...] = xov[...].reshape(NE, 32, 128)
                last = pltpu.make_async_copy(yo, y_hbm.at[:, pl.ds(512, 32)], sem.at[2])
                last.start()
                for k in (2, 3):
                    pltpu.make_async_copy(
                        yb.at[k % 2], y_hbm.at[:, pl.ds(k * 128, 128)], sem.at[k % 2]
                    ).wait()
                last.wait()


def run_experts(x, wg, wu, wd):
    lo = lambda i: jnp.minimum(i, 3)
    return pl.pallas_call(
        expert_kernel,
        grid=(8,),
        out_shape=jax.ShapeDtypeStruct((NE, XR, 128), BF),
        in_specs=[
            pl.BlockSpec((NE, 128, 128), lambda i: (0, lo(i), 0)),
            pl.BlockSpec((NE, 32, 128), lambda i: (0, 16, 0)),
            pl.BlockSpec((1, 1024, FF), lambda i: (0, lo(i), 0)),
            pl.BlockSpec((1, 1024, FF), lambda i: (0, lo(i), 0)),
            pl.BlockSpec((1, FF, 1024), lambda i: (0, 0, jnp.maximum(i - 4, 0))),
        ],
        out_specs=pl.BlockSpec(memory_space=pl.ANY),
        scratch_shapes=[
            pltpu.VMEM((NALL, FF), F32),
            pltpu.VMEM((NALL, FF), F32),
            pltpu.VMEM((NALL, FF), BF),
            pltpu.VMEM((NE, DM), BF),
            pltpu.VMEM((2, NE, 128, 128), BF),
            pltpu.VMEM((NE, 32, 128), BF),
            pltpu.SemaphoreType.DMA((3,)),
        ],
        compiler_params=pltpu.CompilerParams(vmem_limit_bytes=VMEM_BIG),
        cost_estimate=pl.CostEstimate(
            flops=20 * 2**30, bytes_accessed=36 * 2**20, transcendentals=2**20
        ),
        name="experts",
    )(x, x, wg, wu, wd)


def combine_kernel(y_ref, yo_ref, st_ref, tgt_ref, gate_ref, o_ref, gm, go, yov):
    step = pl.program_id(0)

    @pl.when(step == 0)
    def _():
        yov[...] = yo_ref[...].reshape(NE, DM)
        lane = lax.broadcasted_iota(jnp.int32, (ROWS, NALL), 1)
        mix = jnp.zeros((ROWS, NALL), F32)
        for k in range(TOP):
            mix = jnp.where(lane == tgt_ref[:, k : k + 1], gate_ref[:, k : k + 1], mix)
        hi = mix.astype(BF)
        lo = (mix - hi.astype(F32)).astype(BF)
        gm[:ROWS] = hi[:, :NMAIN]
        gm[ROWS:] = lo[:, :NMAIN]
        go[:ROWS] = hi[:, NMAIN:]
        go[ROWS:] = lo[:, NMAIN:]

    pieces = [y_ref[:, i * SLOT : (i + 1) * SLOT, :].reshape(NMAIN, 128) for i in range(8)]
    main = jnp.concatenate(pieces, axis=1)
    at = pl.multiple_of(step * 1024, 1024)
    both = jnp.dot(gm[...], main, preferred_element_type=F32) + jnp.dot(
        go[...], yov[:, pl.ds(at, 1024)], preferred_element_type=F32
    )
    r = lax.broadcasted_iota(jnp.int32, (ROWS, ROWS), 0)
    c = lax.broadcasted_iota(jnp.int32, (ROWS, ROWS), 1)
    turn = jnp.where(c == (r & 1) * 64 + (r >> 1), 1.0, 0.0).astype(BF)
    st = jnp.dot(turn, st_ref[...], preferred_element_type=F32)
    o_ref[...] = (st + (both[:ROWS] + both[ROWS:])).astype(BF)


def combine(y, stream, tgt, gates):
    return pl.pallas_call(
        combine_kernel,
        grid=(4,),
        out_shape=jax.ShapeDtypeStruct((ROWS, DM), BF),
        in_specs=[
            pl.BlockSpec((NE, 128, 128), lambda i: (0, i, 0)),
            pl.BlockSpec((NE, 32, 128), lambda i: (0, 16, 0)),
            pl.BlockSpec((ROWS, 1024), lambda i: (0, i)),
            pl.BlockSpec((ROWS, TOP), lambda i: (0, 0)),
            pl.BlockSpec((ROWS, TOP), lambda i: (0, 0)),
        ],
        out_specs=pl.BlockSpec((ROWS, 1024), lambda i: (0, i)),
        scratch_shapes=[
            pltpu.VMEM((2 * ROWS, NMAIN), BF),
            pltpu.VMEM((2 * ROWS, NE), BF),
            pltpu.VMEM((NE, DM), BF),
        ],
        compiler_params=pltpu.CompilerParams(vmem_limit_bytes=VMEM_BIG),
        cost_estimate=pl.CostEstimate(
            flops=2 * 2**30, bytes_accessed=11 * 2**20, transcendentals=0
        ),
        name="combine",
    )(y, y, stream, tgt, gates)


def slots(ids):
    catalog = jnp.arange(NE, dtype=jnp.int32)
    hits = jnp.any(ids[:, :, None] == catalog, axis=1).astype(BF)
    below = (jnp.arange(ROWS)[:, None] > jnp.arange(ROWS)[None, :]).astype(BF)
    before = jnp.dot(below, hits, preferred_element_type=F32)
    slot = jnp.sum(
        jnp.where(ids[:, :, None] == catalog, before[:, None, :], 0.0), axis=-1
    ).astype(jnp.int32)
    return jnp.where(slot < SLOT, ids * SLOT + slot, NMAIN + ids)


def on_device(
    queries,
    keys,
    values,
    q_gain,
    k_gain,
    out_weight,
    hidden_in,
    norm_gain,
    router,
    expert_ids,
    w_gate,
    w_up,
    w_down,
):
    t, e = lax.axis_index("tensor"), lax.axis_index("expert")
    scal = jnp.stack([t & 1, t >> 1, e >> 2, e & 3]).astype(jnp.int32)
    cs, sn = rotate_tables(e * PB + jnp.arange(PB, dtype=jnp.int32))

    kv = ready_keys(
        keys[0].reshape(PB, SEQ * HD), values[0].reshape(PB, SEQ * HD), cs, sn, k_gain.reshape(1, HD)
    )
    kv, weight = lax.optimization_barrier((kv, out_weight))
    kv_all = ring_relay(jnp.stack(ring_four(kv, y_move)), z_move)
    wa_all = ring_relay(jnp.stack(ring_four(weight[:WA], z_move)), y_move)
    wb_all = ring_relay(jnp.stack(ring_four(weight[WA:], y_move)), z_move)

    q2 = queries[0].reshape(PB, SEQ * 1024)
    ids = expert_ids[0].reshape(ROWS, TOP)
    tgt = slots(ids)
    tgt_t = jnp.transpose(tgt.reshape(64, SEQ, TOP), (2, 1, 0)).reshape(TOP, ROWS)
    hid = jnp.transpose(hidden_in[0], (1, 0, 2)).reshape(ROWS, DM)

    attn = attention(scal, q2, cs, sn, q_gain.reshape(1, HD), kv_all)
    keeps, gots, rests = [], [], []
    for part in range(2):
        keep, send = project(part, scal, attn, wa_all, wb_all)
        got = lax.ppermute(send, "tensor", CORE_SWAP)
        other = (keep[128:].astype(F32) + got[128:].astype(F32)).astype(BF)
        keeps.append(keep)
        gots.append(got)
        rests.append(lax.ppermute(other, "tensor", X_SWAP))
    stream, normed, x = dispatch(
        scal, keeps, gots, rests, hid, norm_gain.reshape(1, DM), tgt_t
    )
    arrived = lax.all_to_all(x, ("tensor", "expert"), split_axis=0, concat_axis=0, tiled=True)

    logits = jnp.dot(normed, router, preferred_element_type=F32)
    logits = jnp.transpose(logits.reshape(SEQ, 64, NE), (1, 0, 2)).reshape(ROWS, NE)
    chosen = ids[:, :, None] == jnp.arange(NE, dtype=jnp.int32)
    gates = jax.nn.softmax(jnp.sum(jnp.where(chosen, logits[:, None, :], 0.0), axis=-1), axis=-1)

    done = run_experts(arrived, w_gate, w_up, w_down)
    back = lax.all_to_all(done, ("tensor", "expert"), split_axis=0, concat_axis=0, tiled=True)
    out = combine(back, stream, tgt, gates)
    return out.reshape(hidden_in.shape)


def solution(mesh):
    return jax.shard_map(
        on_device,
        mesh=mesh,
        in_specs=(
            P(("dp", "expert"), None, None, "tensor"),
            P(("dp", "expert"), None, None, "tensor"),
            P(("dp", "expert"), None, None, "tensor"),
            P(),
            P(),
            P("tensor", "expert"),
            P(("dp", "expert"), "tensor", None, None),
            P(),
            P(),
            P(("dp", "expert"), "tensor", None, None),
            P(("tensor", "expert"), None, None),
            P(("tensor", "expert"), None, None),
            P(("tensor", "expert"), None, None),
        ),
        out_specs=P(("dp", "expert"), "tensor", None, None),
        check_vma=False,
    )
```

```python
import functools

import jax
import jax.numpy as jnp
from jax import lax
from jax.experimental import pallas as pl
from jax.experimental.pallas import tpu as pltpu
from jax.sharding import PartitionSpec as P


theta_base = 1000000.0
eps_norm = 1e-06
neg_fill = -1e30
LOG2E = 1.4426950408889634

BF = jnp.bfloat16
F32 = jnp.float32
HD = 128
PB = 256
SEQ = 2
DM = 4096
FF = 768
NE = 64
TOP = 8
ROWS = 128
SLOT = 16
NMAIN = NE * SLOT
NALL = NMAIN + NE
XR = 17 * 32
VMEM_BIG = 60 * 1024 * 1024


def spot(z, y):
    return (z % 4) * 4 + (y % 4)


def y_move(k):
    return [(spot(z, y), spot(z, y + k)) for z in range(4) for y in range(4)]


def z_move(k):
    return [(spot(z, y), spot(z + k, y)) for z in range(4) for y in range(4)]


CORE_SWAP = [(i, i ^ 1) for i in range(4)]
X_SWAP = [(i, i ^ 2) for i in range(4)]


def ring_four(x, move):
    return [x] + [lax.ppermute(x, "expert", move(k)) for k in (1, 2, 3)]


def ring_relay(x, move):
    half = x.shape[0] // 2
    left = lax.ppermute(x, "expert", move(1))
    right = lax.ppermute(x, "expert", move(3))
    lo = lax.ppermute(left[:half], "expert", move(1))
    hi = lax.ppermute(right[half:], "expert", move(3))
    return x, left, right, lo, hi


def rotate_tables(positions):
    freq = theta_base ** (-2.0 * jnp.arange(HD // 2, dtype=F32) / HD)
    ang = positions.astype(F32)[:, None] * freq[None, :]
    cs, sn = jnp.cos(ang), jnp.sin(ang)
    return jnp.concatenate([cs, cs], axis=1), jnp.concatenate([-sn, sn], axis=1)


def keys_kernel(k_ref, v_ref, cos_ref, sin_ref, gain_ref, o_ref):
    cs, sn, gain = cos_ref[...], sin_ref[...], gain_ref[...]
    for s in range(SEQ):
        k = k_ref[:, s * HD : (s + 1) * HD].astype(F32)
        k = k * lax.rsqrt(jnp.mean(k * k, axis=-1, keepdims=True) + eps_norm) * gain
        o_ref[s, 0:PB, :] = (k * cs + pltpu.roll(k, HD // 2, 1) * sn).astype(BF)
        v = jnp.transpose(v_ref[:, s * HD : (s + 1) * HD].astype(F32)).astype(BF)
        o_ref[s, PB : PB + HD, :] = v[:, :HD]
        o_ref[s, PB + HD :, :] = v[:, HD:]


def ready_keys(k2, v2, cs, sn, gain):
    return pl.pallas_call(
        keys_kernel, out_shape=jax.ShapeDtypeStruct((SEQ, 2 * PB, HD), BF), name="ready_keys"
    )(k2, v2, cs, sn, gain)


C2 = HD ** (-0.5) * LOG2E
VR = HD + 16
HEADS = 8


def attn_part(q_ref, key_of, val_of, load, save, s_buf, mask):
    ones = jnp.ones((16, PB), BF)

    def score(h, j):
        q = q_ref[:, pl.ds(pl.multiple_of(h * HD, HD), HD)]
        s = lax.dot_general(key_of(j), q, (((1,), (1,)), ((), ())), preferred_element_type=F32)
        return s if mask is None else mask(j, s)

    top = None
    for j in range(4):
        s = score(0, j)
        s_buf[0, j] = s
        part = jnp.max(s, axis=0, keepdims=True)
        top = part if j == 0 else jnp.maximum(top, part)

    def body(h, top):
        slot = h & 1
        m_old, acc = load(h)
        m_new = jnp.maximum(m_old, top)
        mc = m_new * C2
        acc = acc * jnp.exp2(m_old * C2 - mc)
        nxt = None
        for j in range(4):
            s = score((h + 1) & (HEADS - 1), j)
            p = jnp.exp2(s_buf[slot, j] * C2 - mc).astype(BF)
            s_buf[1 - slot, j] = s
            part = jnp.max(s, axis=0, keepdims=True)
            nxt = part if j == 0 else jnp.maximum(nxt, part)
            acc = acc + jnp.dot(
                jnp.concatenate([val_of(j), ones], axis=0), p, preferred_element_type=F32
            )
        save(h, m_new, acc)
        return nxt

    lax.fori_loop(0, HEADS, body, top)


def block_keys(kv_ref):
    return (
        lambda j: kv_ref[j, 0, 0:PB, :],
        lambda j: jnp.concatenate(
            [kv_ref[j, 0, PB : PB + HD, :], kv_ref[j, 0, PB + HD :, :]], axis=1
        ),
    )


def attn_first(sc, q_ref, cos_ref, sin_ref, gain_ref, kv_ref, qr_ref, m_ref, acc_ref, s_buf):
    y = sc[3]
    cs, sn, gain = cos_ref[...], sin_ref[...], gain_ref[...]
    for h in range(HEADS):
        q = q_ref[:, h * HD : (h + 1) * HD].astype(F32)
        q = q * lax.rsqrt(jnp.mean(q * q, axis=-1, keepdims=True) + eps_norm) * gain
        qr_ref[:, h * HD : (h + 1) * HD] = (q * cs + pltpu.roll(q, HD // 2, 1) * sn).astype(BF)

    def mask(j, s):
        if j > 0:
            return s + jnp.where(j <= y, 0.0, neg_fill)
        key = lax.broadcasted_iota(jnp.int32, (PB, PB), 0)
        row = lax.broadcasted_iota(jnp.int32, (PB, PB), 1)
        return jnp.where(key <= row, s, neg_fill)

    def load(h):
        return jnp.full((1, PB), neg_fill, F32), jnp.zeros((VR, PB), F32)

    def save(h, m, acc):
        m_ref[h] = jnp.broadcast_to(m, (8, PB))
        acc_ref[h] = acc

    key_of, val_of = block_keys(kv_ref)
    attn_part(qr_ref, key_of, val_of, load, save, s_buf, mask)


def attn_next(sc, q_ref, m_in, acc_in, ka_ref, kb_ref, m_ref, acc_ref, s_buf):
    z = sc[2]

    @pl.when(z == 0)
    def _():
        m_ref[...] = m_in[...]
        acc_ref[...] = acc_in[...]

    for need, kv_ref, m_from, acc_from in ((1, ka_ref, m_in, acc_in), (3, kb_ref, m_ref, acc_ref)):

        @pl.when(z >= need)
        def _(kv_ref=kv_ref, m_from=m_from, acc_from=acc_from):
            def load(h):
                return m_from[h, 0:1, :], acc_from[h]

            def save(h, m, acc):
                m_ref[h] = jnp.broadcast_to(m, (8, PB))
                acc_ref[h] = acc

            key_of, val_of = block_keys(kv_ref)
            attn_part(q_ref, key_of, val_of, load, save, s_buf, None)


def attn_last(sc, q_ref, m_in, acc_in, ka_ref, kb_ref, o_ref, s_buf):
    z = sc[2]

    def finish(h, acc):
        out = jnp.transpose(acc[:HD] / acc[HD : HD + 1])
        o_ref[:, pl.ds(pl.multiple_of(h * HD, HD), HD)] = out.astype(BF)

    @pl.when(z >= 2)
    def _():
        ka, va = block_keys(ka_ref)
        kb, vb = block_keys(kb_ref)
        attn_part(
            q_ref,
            lambda j: ka(j) if j < 2 else kb(j - 2),
            lambda j: va(j) if j < 2 else vb(j - 2),
            lambda h: (m_in[h, 0:1, :], acc_in[h]),
            lambda h, m, acc: finish(h, acc),
            s_buf,
            None,
        )

    @pl.when(z < 2)
    def _():
        def body(h, _):
            finish(h, acc_in[h])
            return 0

        lax.fori_loop(0, HEADS, body, 0)


Q_SPEC = pl.BlockSpec((PB, 1024), lambda i, sc: (0, i))
M_SPEC = pl.BlockSpec((HEADS, 8, PB), lambda i, sc: (i, 0, 0))
A_SPEC = pl.BlockSpec((HEADS, VR, PB), lambda i, sc: (i, 0, 0))


def kv_spec(n):
    return pl.BlockSpec((n, 1, 2 * PB, HD), lambda i, sc: (0, i, 0, 0))


def attn_call(kernel, in_specs, out_specs, out_shape, parts):
    return pl.pallas_call(
        kernel,
        out_shape=out_shape,
        grid_spec=pltpu.PrefetchScalarGridSpec(
            num_scalar_prefetch=1,
            grid=(SEQ,),
            in_specs=in_specs,
            out_specs=out_specs,
            scratch_shapes=[pltpu.VMEM((2, 4, PB, PB), F32)],
        ),
        compiler_params=pltpu.CompilerParams(vmem_limit_bytes=VMEM_BIG),
        cost_estimate=pl.CostEstimate(
            flops=parts * 4 * 2**30, bytes_accessed=8 * 2**20, transcendentals=parts * 4 * 2**20
        ),
    )


STATE = (
    jax.ShapeDtypeStruct((SEQ * HEADS, 8, PB), F32),
    jax.ShapeDtypeStruct((SEQ * HEADS, VR, PB), F32),
)


def attention(scal, q2, cs, sn, gain, pieces):
    own, left, right, lo, hi = pieces
    table = pl.BlockSpec((PB, HD), lambda i, sc: (0, 0))
    qr, m, acc = attn_call(
        attn_first,
        [Q_SPEC, table, table, pl.BlockSpec((1, HD), lambda i, sc: (0, 0)), kv_spec(4)],
        (Q_SPEC, M_SPEC, A_SPEC),
        (jax.ShapeDtypeStruct((PB, SEQ * 1024), BF),) + STATE,
        1,
    )(scal, q2, cs, sn, gain, own)
    m, acc = attn_call(
        attn_next, [Q_SPEC, M_SPEC, A_SPEC, kv_spec(4), kv_spec(4)], (M_SPEC, A_SPEC), STATE, 2
    )(scal, qr, m, acc, left, right)
    return attn_call(
        attn_last,
        [Q_SPEC, M_SPEC, A_SPEC, kv_spec(2), kv_spec(2)],
        Q_SPEC,
        jax.ShapeDtypeStruct((PB, SEQ * 1024), BF),
        1,
    )(scal, qr, m, acc, lo, hi)


WA = 768
WB = 1024 - WA


def proj_kernel(part, sc, a_ref, *rest):
    n_in = 6 if part == 0 else 7
    w_in, (keep, send, lhs, w, sem) = rest[:n_in], rest[n_in:]
    c, xh = sc[0], sc[1]
    top, low = pl.ds(0, WA), pl.ds(WA, WB)
    two = pl.ds(2 * part, 2)
    moves = [
        (w_in[0].at[two], w.at[:, 0, top]),
        (w_in[1].at[two], w.at[:, 1, top]),
        (w_in[2].at[two], w.at[:, 3, top]),
        (w_in[3], w.at[:, 2, top]),
    ]
    if part == 0:
        moves += [(w_in[4], w.at[0, :, low]), (w_in[5], w.at[1, :, low])]
    else:
        moves += [
            (w_in[4], w.at[1, :, low]),
            (w_in[5], w.at[0, pl.ds(0, 2), low]),
            (w_in[6], w.at[0, pl.ds(2, 2), low]),
        ]
    copies = [pltpu.make_async_copy(a, b, sem.at[i]) for i, (a, b) in enumerate(moves)]
    for cp in copies[4:] + copies[:4]:
        cp.start()
    for cc in (1, 0):
        for xx in range(2):
            base = pl.multiple_of(64 * (2 * (xh ^ xx) + (c ^ cc)), 64)
            for s in range(SEQ):
                at = cc * 256 + xx * 128 + s * 64
                lhs[at : at + 64, :] = a_ref[pl.ds(base, 64), s * 1024 : (s + 1) * 1024]
    for cp in copies[4:]:
        cp.wait()
    for cp, dy in zip(copies[:4], (0, 1, 3, 2)):
        cp.wait()
        for i in range(2):
            res = jnp.dot(lhs[...], w[i, dy], preferred_element_type=F32).astype(BF)
            lane = (i * 4 + dy) * 256
            keep[:, lane : lane + 256] = res[:256]
            send[:, lane : lane + 256] = res[256:]


def project(part, scal, attn, pa, pb):
    pieces = list(pa[:3]) + [pa[3 + part]]
    pieces += [pb[0], pb[1]] if part == 0 else [pb[2], pb[3], pb[4]]
    full = pl.BlockSpec(memory_space=pltpu.VMEM)
    return pl.pallas_call(
        functools.partial(proj_kernel, part),
        out_shape=(
            jax.ShapeDtypeStruct((256, DM // 2), BF),
            jax.ShapeDtypeStruct((256, DM // 2), BF),
        ),
        in_specs=[pl.BlockSpec(memory_space=pltpu.SMEM), full]
        + [pl.BlockSpec(memory_space=pl.ANY)] * len(pieces),
        out_specs=(full, full),
        scratch_shapes=[
            pltpu.VMEM((512, 1024), BF),
            pltpu.VMEM((2, 4, 1024, 256), BF),
            pltpu.SemaphoreType.DMA((8,)),
        ],
        compiler_params=pltpu.CompilerParams(vmem_limit_bytes=VMEM_BIG),
        cost_estimate=pl.CostEstimate(
            flops=2 * 2**30, bytes_accessed=7 * 2**20, transcendentals=0
        ),
    )(scal, attn, *pieces)


def dispatch_kernel(
    sc, k0, k1, g0, g1, r0, r1, h_ref, gain_ref, tgt_ref, st_ref, nm_ref, x_ref
):
    z, y = sc[2], sc[3]
    square = jnp.zeros((ROWS, 1), F32)
    for dz in range(4):
        k_ref, g_ref, r_ref = (k0, g0, r0) if dz < 2 else (k1, g1, r1)
        for dy in range(4):
            here = (dz & 1) * 1024 + dy * 256
            there = pl.multiple_of((((z - dz) & 3) * 4 + ((y - dy) & 3)) * 256, 256)
            span = slice(here, here + 256)
            total = (
                h_ref[:, pl.ds(there, 256)].astype(F32)
                + (k_ref[:, span].astype(F32) + g_ref[:, span].astype(F32))
                + r_ref[:, span].astype(F32)
            )
            st = total.astype(BF)
            st_ref[:, pl.ds(there, 256)] = st
            sf = st.astype(F32)
            square = square + jnp.sum(sf * sf, axis=-1, keepdims=True)
    scale = lax.rsqrt(square / DM + eps_norm)
    nm_ref[...] = (st_ref[...].astype(F32) * scale * gain_ref[...]).astype(BF)
    line = lax.broadcasted_iota(jnp.int32, (NALL, ROWS), 0)
    hit = jnp.zeros((NALL, ROWS), F32)
    for k in range(TOP):
        hit = jnp.where(line == tgt_ref[k : k + 1, :], 1.0, hit)
    pick = hit.astype(BF)
    for j in range(8):
        n = nm_ref[:, j * 512 : (j + 1) * 512]
        main = jnp.dot(pick[:NMAIN], n, preferred_element_type=F32).astype(BF)
        for i in range(4):
            f = 4 * j + i
            x_ref[:, f * SLOT : (f + 1) * SLOT, :] = main[:, i * 128 : (i + 1) * 128].reshape(
                NE, SLOT, 128
            )
    ov = jnp.dot(pick[NMAIN:], nm_ref[...], preferred_element_type=F32).astype(BF)
    x_ref[:, 512:544, :] = ov.reshape(NE, 32, 128)


def dispatch(scal, keeps, gots, rests, hid, gain, tgt_t):
    at = lambda i, sc: (0, 0)
    half = pl.BlockSpec((ROWS, DM // 2), at)
    line = pl.BlockSpec((ROWS, DM), at)
    return pl.pallas_call(
        dispatch_kernel,
        out_shape=(
            jax.ShapeDtypeStruct((ROWS, DM), BF),
            jax.ShapeDtypeStruct((ROWS, DM), BF),
            jax.ShapeDtypeStruct((NE, XR, 128), BF),
        ),
        grid_spec=pltpu.PrefetchScalarGridSpec(
            num_scalar_prefetch=1,
            grid=(1,),
            in_specs=[half] * 6
            + [line, pl.BlockSpec((1, DM), at), pl.BlockSpec((TOP, ROWS), at)],
            out_specs=(line, line, pl.BlockSpec((NE, XR, 128), lambda i, sc: (0, 0, 0))),
        ),
        compiler_params=pltpu.CompilerParams(vmem_limit_bytes=VMEM_BIG),
        cost_estimate=pl.CostEstimate(
            flops=2**30, bytes_accessed=14 * 2**20, transcendentals=0
        ),
        name="dispatch",
    )(scal, *keeps, *gots, *rests, hid, gain, tgt_t)


def expert_kernel(x_ref, xo_ref, wg_ref, wu_ref, wd_ref, y_hbm, ga, ua, inner, xov, yb, yo, sem):
    step = pl.program_id(0)

    @pl.when(step == 0)
    def _():
        xov[...] = xo_ref[...].reshape(NE, DM)

    @pl.when(step < 4)
    def _():
        pieces = [
            x_ref[:, i * SLOT : (i + 1) * SLOT, :].reshape(NMAIN, 128) for i in range(8)
        ]
        main = jnp.concatenate(pieces, axis=1)
        lane = pl.multiple_of(step * 1024, 1024)
        rows = jnp.concatenate([main, xov[:, pl.ds(lane, 1024)]], axis=0)
        g = jnp.dot(rows, wg_ref[0], preferred_element_type=F32)
        u = jnp.dot(rows, wu_ref[0], preferred_element_type=F32)

        @pl.when(step == 0)
        def _():
            ga[...] = g
            ua[...] = u

        @pl.when(step > 0)
        def _():
            ga[...] += g
            ua[...] += u

    @pl.when(step == 4)
    def _():
        g = ga[...]
        inner[...] = (g / (1.0 + jnp.exp(-g)) * ua[...]).astype(BF)

    for j in range(4):

        @pl.when(step == 4 + j)
        def _(j=j):
            slot = j % 2
            out = jnp.dot(inner[...], wd_ref[0], preferred_element_type=F32).astype(BF)
            if j >= 2:
                pltpu.make_async_copy(
                    yb.at[slot], y_hbm.at[:, pl.ds((j - 2) * 128, 128)], sem.at[slot]
                ).wait()
            for i in range(8):
                yb[slot, :, i * SLOT : (i + 1) * SLOT, :] = out[
                    :NMAIN, i * 128 : (i + 1) * 128
                ].reshape(NE, SLOT, 128)
            xov[:, j * 1024 : (j + 1) * 1024] = out[NMAIN:]
            pltpu.make_async_copy(
                yb.at[slot], y_hbm.at[:, pl.ds(j * 128, 128)], sem.at[slot]
            ).start()
            if j == 3:
                yo[...] = xov[...].reshape(NE, 32, 128)
                last = pltpu.make_async_copy(yo, y_hbm.at[:, pl.ds(512, 32)], sem.at[2])
                last.start()
                for k in (2, 3):
                    pltpu.make_async_copy(
                        yb.at[k % 2], y_hbm.at[:, pl.ds(k * 128, 128)], sem.at[k % 2]
                    ).wait()
                last.wait()


def run_experts(x, wg, wu, wd):
    lo = lambda i: jnp.minimum(i, 3)
    return pl.pallas_call(
        expert_kernel,
        grid=(8,),
        out_shape=jax.ShapeDtypeStruct((NE, XR, 128), BF),
        in_specs=[
            pl.BlockSpec((NE, 128, 128), lambda i: (0, lo(i), 0)),
            pl.BlockSpec((NE, 32, 128), lambda i: (0, 16, 0)),
            pl.BlockSpec((1, 1024, FF), lambda i: (0, lo(i), 0)),
            pl.BlockSpec((1, 1024, FF), lambda i: (0, lo(i), 0)),
            pl.BlockSpec((1, FF, 1024), lambda i: (0, 0, jnp.maximum(i - 4, 0))),
        ],
        out_specs=pl.BlockSpec(memory_space=pl.ANY),
        scratch_shapes=[
            pltpu.VMEM((NALL, FF), F32),
            pltpu.VMEM((NALL, FF), F32),
            pltpu.VMEM((NALL, FF), BF),
            pltpu.VMEM((NE, DM), BF),
            pltpu.VMEM((2, NE, 128, 128), BF),
            pltpu.VMEM((NE, 32, 128), BF),
            pltpu.SemaphoreType.DMA((3,)),
        ],
        compiler_params=pltpu.CompilerParams(vmem_limit_bytes=VMEM_BIG),
        cost_estimate=pl.CostEstimate(
            flops=20 * 2**30, bytes_accessed=36 * 2**20, transcendentals=2**20
        ),
        name="experts",
    )(x, x, wg, wu, wd)


def combine_kernel(y_ref, yo_ref, st_ref, tgt_ref, gate_ref, o_ref, gm, go, yov):
    step = pl.program_id(0)

    @pl.when(step == 0)
    def _():
        yov[...] = yo_ref[...].reshape(NE, DM)
        lane = lax.broadcasted_iota(jnp.int32, (ROWS, NALL), 1)
        mix = jnp.zeros((ROWS, NALL), F32)
        for k in range(TOP):
            mix = jnp.where(lane == tgt_ref[:, k : k + 1], gate_ref[:, k : k + 1], mix)
        hi = mix.astype(BF)
        lo = (mix - hi.astype(F32)).astype(BF)
        gm[:ROWS] = hi[:, :NMAIN]
        gm[ROWS:] = lo[:, :NMAIN]
        go[:ROWS] = hi[:, NMAIN:]
        go[ROWS:] = lo[:, NMAIN:]

    pieces = [y_ref[:, i * SLOT : (i + 1) * SLOT, :].reshape(NMAIN, 128) for i in range(8)]
    main = jnp.concatenate(pieces, axis=1)
    at = pl.multiple_of(step * 1024, 1024)
    both = jnp.dot(gm[...], main, preferred_element_type=F32) + jnp.dot(
        go[...], yov[:, pl.ds(at, 1024)], preferred_element_type=F32
    )
    r = lax.broadcasted_iota(jnp.int32, (ROWS, ROWS), 0)
    c = lax.broadcasted_iota(jnp.int32, (ROWS, ROWS), 1)
    turn = jnp.where(c == (r & 1) * 64 + (r >> 1), 1.0, 0.0).astype(BF)
    st = jnp.dot(turn, st_ref[...], preferred_element_type=F32)
    o_ref[...] = (st + (both[:ROWS] + both[ROWS:])).astype(BF)


def combine(y, stream, tgt, gates):
    return pl.pallas_call(
        combine_kernel,
        grid=(4,),
        out_shape=jax.ShapeDtypeStruct((ROWS, DM), BF),
        in_specs=[
            pl.BlockSpec((NE, 128, 128), lambda i: (0, i, 0)),
            pl.BlockSpec((NE, 32, 128), lambda i: (0, 16, 0)),
            pl.BlockSpec((ROWS, 1024), lambda i: (0, i)),
            pl.BlockSpec((ROWS, TOP), lambda i: (0, 0)),
            pl.BlockSpec((ROWS, TOP), lambda i: (0, 0)),
        ],
        out_specs=pl.BlockSpec((ROWS, 1024), lambda i: (0, i)),
        scratch_shapes=[
            pltpu.VMEM((2 * ROWS, NMAIN), BF),
            pltpu.VMEM((2 * ROWS, NE), BF),
            pltpu.VMEM((NE, DM), BF),
        ],
        compiler_params=pltpu.CompilerParams(vmem_limit_bytes=VMEM_BIG),
        cost_estimate=pl.CostEstimate(
            flops=2 * 2**30, bytes_accessed=11 * 2**20, transcendentals=0
        ),
        name="combine",
    )(y, y, stream, tgt, gates)


def slots(ids):
    catalog = jnp.arange(NE, dtype=jnp.int32)
    hits = jnp.any(ids[:, :, None] == catalog, axis=1).astype(BF)
    below = (jnp.arange(ROWS)[:, None] > jnp.arange(ROWS)[None, :]).astype(BF)
    before = jnp.dot(below, hits, preferred_element_type=F32)
    slot = jnp.sum(
        jnp.where(ids[:, :, None] == catalog, before[:, None, :], 0.0), axis=-1
    ).astype(jnp.int32)
    return jnp.where(slot < SLOT, ids * SLOT + slot, NMAIN + ids)


def on_device(
    queries,
    keys,
    values,
    q_gain,
    k_gain,
    out_weight,
    hidden_in,
    norm_gain,
    router,
    expert_ids,
    w_gate,
    w_up,
    w_down,
):
    t, e = lax.axis_index("tensor"), lax.axis_index("expert")
    scal = jnp.stack([t & 1, t >> 1, e >> 2, e & 3]).astype(jnp.int32)
    cs, sn = rotate_tables(e * PB + jnp.arange(PB, dtype=jnp.int32))

    kv = ready_keys(
        keys[0].reshape(PB, SEQ * HD), values[0].reshape(PB, SEQ * HD), cs, sn, k_gain.reshape(1, HD)
    )
    kv, weight = lax.optimization_barrier((kv, out_weight))
    kv_all = ring_relay(jnp.stack(ring_four(kv, y_move)), z_move)
    wa_all = ring_relay(jnp.stack(ring_four(weight[:WA], z_move)), y_move)
    wb_all = ring_relay(jnp.stack(ring_four(weight[WA:], y_move)), z_move)

    q2 = queries[0].reshape(PB, SEQ * 1024)
    ids = expert_ids[0].reshape(ROWS, TOP)
    tgt = slots(ids)
    tgt_t = jnp.transpose(tgt.reshape(64, SEQ, TOP), (2, 1, 0)).reshape(TOP, ROWS)
    hid = jnp.transpose(hidden_in[0], (1, 0, 2)).reshape(ROWS, DM)

    attn = attention(scal, q2, cs, sn, q_gain.reshape(1, HD), kv_all)
    keeps, gots, rests = [], [], []
    for part in range(2):
        keep, send = project(part, scal, attn, wa_all, wb_all)
        got = lax.ppermute(send, "tensor", CORE_SWAP)
        other = (keep[128:].astype(F32) + got[128:].astype(F32)).astype(BF)
        keeps.append(keep)
        gots.append(got)
        rests.append(lax.ppermute(other, "tensor", X_SWAP))
    stream, normed, x = dispatch(
        scal, keeps, gots, rests, hid, norm_gain.reshape(1, DM), tgt_t
    )
    arrived = lax.all_to_all(x, ("tensor", "expert"), split_axis=0, concat_axis=0, tiled=True)

    logits = jnp.dot(normed, router, preferred_element_type=F32)
    logits = jnp.transpose(logits.reshape(SEQ, 64, NE), (1, 0, 2)).reshape(ROWS, NE)
    chosen = ids[:, :, None] == jnp.arange(NE, dtype=jnp.int32)
    gates = jax.nn.softmax(jnp.sum(jnp.where(chosen, logits[:, None, :], 0.0), axis=-1), axis=-1)

    done = run_experts(arrived, w_gate, w_up, w_down)
    back = lax.all_to_all(done, ("tensor", "expert"), split_axis=0, concat_axis=0, tiled=True)
    out = combine(back, stream, tgt, gates)
    return out.reshape(hidden_in.shape)


def solution(mesh):
    return jax.shard_map(
        on_device,
        mesh=mesh,
        in_specs=(
            P(("dp", "expert"), None, None, "tensor"),
            P(("dp", "expert"), None, None, "tensor"),
            P(("dp", "expert"), None, None, "tensor"),
            P(),
            P(),
            P("tensor", "expert"),
            P(("dp", "expert"), "tensor", None, None),
            P(),
            P(),
            P(("dp", "expert"), "tensor", None, None),
            P(("tensor", "expert"), None, None),
            P(("tensor", "expert"), None, None),
            P(("tensor", "expert"), None, None),
        ),
        out_specs=P(("dp", "expert"), "tensor", None, None),
        check_vma=False,
    )
```

```python
import functools

import jax
import jax.numpy as jnp
from jax import lax
from jax.experimental import pallas as pl
from jax.experimental.pallas import tpu as pltpu
from jax.sharding import PartitionSpec as P


theta_base = 1000000.0
eps_norm = 1e-06
neg_fill = -1e30
LOG2E = 1.4426950408889634

BF = jnp.bfloat16
F32 = jnp.float32
HD = 128
PB = 256
SEQ = 2
DM = 4096
FF = 768
NE = 64
TOP = 8
ROWS = 128
SLOT = 16
NMAIN = NE * SLOT
NALL = NMAIN + NE
XR = 17 * 32
VMEM_BIG = 60 * 1024 * 1024


def spot(z, y):
    return (z % 4) * 4 + (y % 4)


def y_move(k):
    return [(spot(z, y), spot(z, y + k)) for z in range(4) for y in range(4)]


def z_move(k):
    return [(spot(z, y), spot(z + k, y)) for z in range(4) for y in range(4)]


CORE_SWAP = [(i, i ^ 1) for i in range(4)]
X_SWAP = [(i, i ^ 2) for i in range(4)]


def ring_four(x, move):
    return [x] + [lax.ppermute(x, "expert", move(k)) for k in (1, 2, 3)]


def ring_relay(x, move):
    half = x.shape[0] // 2
    left = lax.ppermute(x, "expert", move(1))
    right = lax.ppermute(x, "expert", move(3))
    lo = lax.ppermute(left[:half], "expert", move(1))
    hi = lax.ppermute(right[half:], "expert", move(3))
    return x, left, right, lo, hi


def rotate_tables(positions):
    freq = theta_base ** (-2.0 * jnp.arange(HD // 2, dtype=F32) / HD)
    ang = positions.astype(F32)[:, None] * freq[None, :]
    cs, sn = jnp.cos(ang), jnp.sin(ang)
    return jnp.concatenate([cs, cs], axis=1), jnp.concatenate([-sn, sn], axis=1)


def keys_kernel(k_ref, v_ref, cos_ref, sin_ref, gain_ref, o_ref):
    cs, sn, gain = cos_ref[...], sin_ref[...], gain_ref[...]
    for s in range(SEQ):
        k = k_ref[:, s * HD : (s + 1) * HD].astype(F32)
        k = k * lax.rsqrt(jnp.mean(k * k, axis=-1, keepdims=True) + eps_norm) * gain
        o_ref[s, 0:PB, :] = (k * cs + pltpu.roll(k, HD // 2, 1) * sn).astype(BF)
        v = jnp.transpose(v_ref[:, s * HD : (s + 1) * HD].astype(F32)).astype(BF)
        o_ref[s, PB : PB + HD, :] = v[:, :HD]
        o_ref[s, PB + HD :, :] = v[:, HD:]


def ready_keys(k2, v2, cs, sn, gain):
    return pl.pallas_call(
        keys_kernel, out_shape=jax.ShapeDtypeStruct((SEQ, 2 * PB, HD), BF), name="ready_keys"
    )(k2, v2, cs, sn, gain)


C2 = HD ** (-0.5) * LOG2E
VR = HD + 16
HEADS = 8


def attn_part(q_ref, key_of, val_of, load, save, s_buf, mask):
    ones = jnp.ones((16, PB), BF)

    def score(h, j):
        q = q_ref[:, pl.ds(pl.multiple_of(h * HD, HD), HD)]
        s = lax.dot_general(key_of(j), q, (((1,), (1,)), ((), ())), preferred_element_type=F32)
        return s if mask is None else mask(j, s)

    top = None
    for j in range(4):
        s = score(0, j)
        s_buf[0, j] = s
        part = jnp.max(s, axis=0, keepdims=True)
        top = part if j == 0 else jnp.maximum(top, part)

    def body(h, top):
        slot = h & 1
        m_old, acc = load(h)
        m_new = jnp.maximum(m_old, top)
        mc = m_new * C2
        acc = acc * jnp.exp2(m_old * C2 - mc)
        nxt = None
        for j in range(4):
            s = score((h + 1) & (HEADS - 1), j)
            p = jnp.exp2(s_buf[slot, j] * C2 - mc).astype(BF)
            s_buf[1 - slot, j] = s
            part = jnp.max(s, axis=0, keepdims=True)
            nxt = part if j == 0 else jnp.maximum(nxt, part)
            acc = acc + jnp.dot(
                jnp.concatenate([val_of(j), ones], axis=0), p, preferred_element_type=F32
            )
        save(h, m_new, acc)
        return nxt

    lax.fori_loop(0, HEADS, body, top)


def block_keys(kv_ref):
    return (
        lambda j: kv_ref[j, 0, 0:PB, :],
        lambda j: jnp.concatenate(
            [kv_ref[j, 0, PB : PB + HD, :], kv_ref[j, 0, PB + HD :, :]], axis=1
        ),
    )


def attn_first(sc, q_ref, cos_ref, sin_ref, gain_ref, kv_ref, qr_ref, m_ref, acc_ref, s_buf):
    y = sc[3]
    cs, sn, gain = cos_ref[...], sin_ref[...], gain_ref[...]
    for h in range(HEADS):
        q = q_ref[:, h * HD : (h + 1) * HD].astype(F32)
        q = q * lax.rsqrt(jnp.mean(q * q, axis=-1, keepdims=True) + eps_norm) * gain
        qr_ref[:, h * HD : (h + 1) * HD] = (q * cs + pltpu.roll(q, HD // 2, 1) * sn).astype(BF)

    def mask(j, s):
        if j > 0:
            return s + jnp.where(j <= y, 0.0, neg_fill)
        key = lax.broadcasted_iota(jnp.int32, (PB, PB), 0)
        row = lax.broadcasted_iota(jnp.int32, (PB, PB), 1)
        return jnp.where(key <= row, s, neg_fill)

    def load(h):
        return jnp.full((1, PB), neg_fill, F32), jnp.zeros((VR, PB), F32)

    def save(h, m, acc):
        m_ref[h] = jnp.broadcast_to(m, (8, PB))
        acc_ref[h] = acc

    key_of, val_of = block_keys(kv_ref)
    attn_part(qr_ref, key_of, val_of, load, save, s_buf, mask)


def attn_next(sc, q_ref, m_in, acc_in, ka_ref, kb_ref, m_ref, acc_ref, s_buf):
    z = sc[2]

    @pl.when(z == 0)
    def _():
        m_ref[...] = m_in[...]
        acc_ref[...] = acc_in[...]

    for need, kv_ref, m_from, acc_from in ((1, ka_ref, m_in, acc_in), (3, kb_ref, m_ref, acc_ref)):

        @pl.when(z >= need)
        def _(kv_ref=kv_ref, m_from=m_from, acc_from=acc_from):
            def load(h):
                return m_from[h, 0:1, :], acc_from[h]

            def save(h, m, acc):
                m_ref[h] = jnp.broadcast_to(m, (8, PB))
                acc_ref[h] = acc

            key_of, val_of = block_keys(kv_ref)
            attn_part(q_ref, key_of, val_of, load, save, s_buf, None)


def attn_last(sc, q_ref, m_in, acc_in, ka_ref, kb_ref, o_ref, s_buf):
    z = sc[2]

    def finish(h, acc):
        out = jnp.transpose(acc[:HD] / acc[HD : HD + 1])
        o_ref[:, pl.ds(pl.multiple_of(h * HD, HD), HD)] = out.astype(BF)

    @pl.when(z >= 2)
    def _():
        ka, va = block_keys(ka_ref)
        kb, vb = block_keys(kb_ref)
        attn_part(
            q_ref,
            lambda j: ka(j) if j < 2 else kb(j - 2),
            lambda j: va(j) if j < 2 else vb(j - 2),
            lambda h: (m_in[h, 0:1, :], acc_in[h]),
            lambda h, m, acc: finish(h, acc),
            s_buf,
            None,
        )

    @pl.when(z < 2)
    def _():
        def body(h, _):
            finish(h, acc_in[h])
            return 0

        lax.fori_loop(0, HEADS, body, 0)


Q_SPEC = pl.BlockSpec((PB, 1024), lambda i, sc: (0, i))
M_SPEC = pl.BlockSpec((HEADS, 8, PB), lambda i, sc: (i, 0, 0))
A_SPEC = pl.BlockSpec((HEADS, VR, PB), lambda i, sc: (i, 0, 0))


def kv_spec(n):
    return pl.BlockSpec((n, 1, 2 * PB, HD), lambda i, sc: (0, i, 0, 0))


def attn_call(kernel, in_specs, out_specs, out_shape, parts):
    return pl.pallas_call(
        kernel,
        out_shape=out_shape,
        grid_spec=pltpu.PrefetchScalarGridSpec(
            num_scalar_prefetch=1,
            grid=(SEQ,),
            in_specs=in_specs,
            out_specs=out_specs,
            scratch_shapes=[pltpu.VMEM((2, 4, PB, PB), F32)],
        ),
        compiler_params=pltpu.CompilerParams(vmem_limit_bytes=VMEM_BIG),
        cost_estimate=pl.CostEstimate(
            flops=parts * 4 * 2**30, bytes_accessed=8 * 2**20, transcendentals=parts * 4 * 2**20
        ),
    )


STATE = (
    jax.ShapeDtypeStruct((SEQ * HEADS, 8, PB), F32),
    jax.ShapeDtypeStruct((SEQ * HEADS, VR, PB), F32),
)


def attention(scal, q2, cs, sn, gain, pieces):
    own, left, right, lo, hi = pieces
    table = pl.BlockSpec((PB, HD), lambda i, sc: (0, 0))
    qr, m, acc = attn_call(
        attn_first,
        [Q_SPEC, table, table, pl.BlockSpec((1, HD), lambda i, sc: (0, 0)), kv_spec(4)],
        (Q_SPEC, M_SPEC, A_SPEC),
        (jax.ShapeDtypeStruct((PB, SEQ * 1024), BF),) + STATE,
        1,
    )(scal, q2, cs, sn, gain, own)
    m, acc = attn_call(
        attn_next, [Q_SPEC, M_SPEC, A_SPEC, kv_spec(4), kv_spec(4)], (M_SPEC, A_SPEC), STATE, 2
    )(scal, qr, m, acc, left, right)
    return attn_call(
        attn_last,
        [Q_SPEC, M_SPEC, A_SPEC, kv_spec(2), kv_spec(2)],
        Q_SPEC,
        jax.ShapeDtypeStruct((PB, SEQ * 1024), BF),
        1,
    )(scal, qr, m, acc, lo, hi)


def proj_kernel(part, sc, a_ref, *rest):
    w_in, (keep, send, lhs, w, sem) = rest[:4], rest[4:]
    c, xh = sc[0], sc[1]
    two = pl.ds(2 * part, 2)
    moves = [
        (w_in[0].at[two], w.at[:, 0]),
        (w_in[1].at[two], w.at[:, 1]),
        (w_in[2].at[two], w.at[:, 3]),
        (w_in[3], w.at[:, 2]),
    ]
    copies = [pltpu.make_async_copy(a, b, sem.at[i]) for i, (a, b) in enumerate(moves)]
    for cp in copies:
        cp.start()
    for cc in (1, 0):
        for xx in range(2):
            base = pl.multiple_of(64 * (2 * (xh ^ xx) + (c ^ cc)), 64)
            for s in range(SEQ):
                at = cc * 256 + xx * 128 + s * 64
                lhs[at : at + 64, :] = a_ref[pl.ds(base, 64), s * 1024 : (s + 1) * 1024]
    for cp, dy in zip(copies, (0, 1, 3, 2)):
        cp.wait()
        for i in range(2):
            res = jnp.dot(lhs[...], w[i, dy], preferred_element_type=F32).astype(BF)
            lane = (i * 4 + dy) * 256
            keep[:, lane : lane + 256] = res[:256]
            send[:, lane : lane + 256] = res[256:]


def project(part, scal, attn, pa):
    pieces = list(pa[:3]) + [pa[3 + part]]
    full = pl.BlockSpec(memory_space=pltpu.VMEM)
    return pl.pallas_call(
        functools.partial(proj_kernel, part),
        out_shape=(
            jax.ShapeDtypeStruct((256, DM // 2), BF),
            jax.ShapeDtypeStruct((256, DM // 2), BF),
        ),
        in_specs=[pl.BlockSpec(memory_space=pltpu.SMEM), full]
        + [pl.BlockSpec(memory_space=pl.ANY)] * len(pieces),
        out_specs=(full, full),
        scratch_shapes=[
            pltpu.VMEM((512, 1024), BF),
            pltpu.VMEM((2, 4, 1024, 256), BF),
            pltpu.SemaphoreType.DMA((4,)),
        ],
        compiler_params=pltpu.CompilerParams(vmem_limit_bytes=VMEM_BIG),
        cost_estimate=pl.CostEstimate(
            flops=2 * 2**30, bytes_accessed=7 * 2**20, transcendentals=0
        ),
    )(scal, attn, *pieces)


def dispatch_kernel(
    sc, k0, k1, g0, g1, r0, r1, h_ref, gain_ref, tgt_ref, st_ref, nm_ref, x_hbm, x_ref, sem
):
    z, y = sc[2], sc[3]
    square = jnp.zeros((ROWS, 1), F32)
    for dz in range(4):
        k_ref, g_ref, r_ref = (k0, g0, r0) if dz < 2 else (k1, g1, r1)
        for dy in range(4):
            here = (dz & 1) * 1024 + dy * 256
            there = pl.multiple_of((((z - dz) & 3) * 4 + ((y - dy) & 3)) * 256, 256)
            span = slice(here, here + 256)
            total = (
                h_ref[:, pl.ds(there, 256)].astype(F32)
                + (k_ref[:, span].astype(F32) + g_ref[:, span].astype(F32))
                + r_ref[:, span].astype(F32)
            )
            st = total.astype(BF)
            st_ref[:, pl.ds(there, 256)] = st
            sf = st.astype(F32)
            square = square + jnp.sum(sf * sf, axis=-1, keepdims=True)
    scale = lax.rsqrt(square / DM + eps_norm)
    nm_ref[...] = (st_ref[...].astype(F32) * scale * gain_ref[...]).astype(BF)
    line = lax.broadcasted_iota(jnp.int32, (NALL, ROWS), 0)
    hit = jnp.zeros((NALL, ROWS), F32)
    for k in range(TOP):
        hit = jnp.where(line == tgt_ref[k : k + 1, :], 1.0, hit)
    pick = hit.astype(BF)
    copies = [
        pltpu.make_async_copy(
            x_ref.at[:, pl.ds(j * 64, 64 if j < 8 else 32)],
            x_hbm.at[:, pl.ds(j * 64, 64 if j < 8 else 32)],
            sem.at[j],
        )
        for j in range(9)
    ]
    for j in range(8):
        n = nm_ref[:, j * 512 : (j + 1) * 512]
        main = jnp.dot(pick[:NMAIN], n, preferred_element_type=F32).astype(BF)
        for i in range(4):
            f = 4 * j + i
            x_ref[:, f * SLOT : (f + 1) * SLOT, :] = main[:, i * 128 : (i + 1) * 128].reshape(
                NE, SLOT, 128
            )
        copies[j].start()
    ov = jnp.dot(pick[NMAIN:], nm_ref[...], preferred_element_type=F32).astype(BF)
    x_ref[:, 512:544, :] = ov.reshape(NE, 32, 128)
    copies[8].start()
    for cp in copies:
        cp.wait()


def dispatch(scal, keeps, gots, rests, hid, gain, tgt_t):
    at = lambda i, sc: (0, 0)
    half = pl.BlockSpec((ROWS, DM // 2), at)
    line = pl.BlockSpec((ROWS, DM), at)
    return pl.pallas_call(
        dispatch_kernel,
        out_shape=(
            jax.ShapeDtypeStruct((ROWS, DM), BF),
            jax.ShapeDtypeStruct((ROWS, DM), BF),
            jax.ShapeDtypeStruct((NE, XR, 128), BF),
        ),
        grid_spec=pltpu.PrefetchScalarGridSpec(
            num_scalar_prefetch=1,
            grid=(1,),
            in_specs=[half] * 6
            + [line, pl.BlockSpec((1, DM), at), pl.BlockSpec((TOP, ROWS), at)],
            out_specs=(line, line, pl.BlockSpec(memory_space=pl.ANY)),
            scratch_shapes=[pltpu.VMEM((NE, XR, 128), BF), pltpu.SemaphoreType.DMA((9,))],
        ),
        compiler_params=pltpu.CompilerParams(vmem_limit_bytes=VMEM_BIG),
        cost_estimate=pl.CostEstimate(
            flops=2**30, bytes_accessed=14 * 2**20, transcendentals=0
        ),
        name="dispatch",
    )(scal, *keeps, *gots, *rests, hid, gain, tgt_t)


def expert_kernel(x_ref, xo_ref, wg_ref, wu_ref, wd_ref, y_hbm, ga, ua, inner, xov, yb, yo, sem):
    step = pl.program_id(0)

    @pl.when(step == 0)
    def _():
        xov[...] = xo_ref[...].reshape(NE, DM)

    @pl.when(step < 4)
    def _():
        pieces = [
            x_ref[:, i * SLOT : (i + 1) * SLOT, :].reshape(NMAIN, 128) for i in range(8)
        ]
        main = jnp.concatenate(pieces, axis=1)
        lane = pl.multiple_of(step * 1024, 1024)
        rows = jnp.concatenate([main, xov[:, pl.ds(lane, 1024)]], axis=0)
        g = jnp.dot(rows, wg_ref[0], preferred_element_type=F32)
        u = jnp.dot(rows, wu_ref[0], preferred_element_type=F32)

        @pl.when(step == 0)
        def _():
            ga[...] = g
            ua[...] = u

        @pl.when(step > 0)
        def _():
            ga[...] += g
            ua[...] += u

    @pl.when(step == 4)
    def _():
        g = ga[...]
        inner[...] = (g / (1.0 + jnp.exp(-g)) * ua[...]).astype(BF)

    for j in range(4):

        @pl.when(step == 4 + j)
        def _(j=j):
            slot = j % 2
            out = jnp.dot(inner[...], wd_ref[0], preferred_element_type=F32).astype(BF)
            if j >= 2:
                pltpu.make_async_copy(
                    yb.at[slot], y_hbm.at[:, pl.ds((j - 2) * 128, 128)], sem.at[slot]
                ).wait()
            for i in range(8):
                yb[slot, :, i * SLOT : (i + 1) * SLOT, :] = out[
                    :NMAIN, i * 128 : (i + 1) * 128
                ].reshape(NE, SLOT, 128)
            xov[:, j * 1024 : (j + 1) * 1024] = out[NMAIN:]
            pltpu.make_async_copy(
                yb.at[slot], y_hbm.at[:, pl.ds(j * 128, 128)], sem.at[slot]
            ).start()
            if j == 3:
                yo[...] = xov[...].reshape(NE, 32, 128)
                last = pltpu.make_async_copy(yo, y_hbm.at[:, pl.ds(512, 32)], sem.at[2])
                last.start()
                for k in (2, 3):
                    pltpu.make_async_copy(
                        yb.at[k % 2], y_hbm.at[:, pl.ds(k * 128, 128)], sem.at[k % 2]
                    ).wait()
                last.wait()


def run_experts(x, wg, wu, wd):
    lo = lambda i: jnp.minimum(i, 3)
    return pl.pallas_call(
        expert_kernel,
        grid=(8,),
        out_shape=jax.ShapeDtypeStruct((NE, XR, 128), BF),
        in_specs=[
            pl.BlockSpec((NE, 128, 128), lambda i: (0, lo(i), 0)),
            pl.BlockSpec((NE, 32, 128), lambda i: (0, 16, 0)),
            pl.BlockSpec((1, 1024, FF), lambda i: (0, lo(i), 0)),
            pl.BlockSpec((1, 1024, FF), lambda i: (0, lo(i), 0)),
            pl.BlockSpec((1, FF, 1024), lambda i: (0, 0, jnp.maximum(i - 4, 0))),
        ],
        out_specs=pl.BlockSpec(memory_space=pl.ANY),
        scratch_shapes=[
            pltpu.VMEM((NALL, FF), F32),
            pltpu.VMEM((NALL, FF), F32),
            pltpu.VMEM((NALL, FF), BF),
            pltpu.VMEM((NE, DM), BF),
            pltpu.VMEM((2, NE, 128, 128), BF),
            pltpu.VMEM((NE, 32, 128), BF),
            pltpu.SemaphoreType.DMA((3,)),
        ],
        compiler_params=pltpu.CompilerParams(vmem_limit_bytes=VMEM_BIG),
        cost_estimate=pl.CostEstimate(
            flops=20 * 2**30, bytes_accessed=36 * 2**20, transcendentals=2**20
        ),
        name="experts",
    )(x, x, wg, wu, wd)


def mix_kernel(tgt_ref, gate_ref, gm, go):
    lane = lax.broadcasted_iota(jnp.int32, (ROWS, NALL), 1)
    mix = jnp.zeros((ROWS, NALL), F32)
    for k in range(TOP):
        mix = jnp.where(lane == tgt_ref[:, k : k + 1], gate_ref[:, k : k + 1], mix)
    hi = mix.astype(BF)
    lo = (mix - hi.astype(F32)).astype(BF)
    gm[:ROWS] = hi[:, :NMAIN]
    gm[ROWS:] = lo[:, :NMAIN]
    go[:ROWS] = hi[:, NMAIN:]
    go[ROWS:] = lo[:, NMAIN:]


def mixing(tgt, gates):
    return pl.pallas_call(
        mix_kernel,
        out_shape=(
            jax.ShapeDtypeStruct((2 * ROWS, NMAIN), BF),
            jax.ShapeDtypeStruct((2 * ROWS, NE), BF),
        ),
        cost_estimate=pl.CostEstimate(flops=2**22, bytes_accessed=2**20, transcendentals=0),
        name="mixing",
    )(tgt, gates)


def combine_kernel(y_ref, yo_ref, st_ref, gm_ref, go_ref, o_ref, yov):
    step = pl.program_id(0)

    @pl.when(step == 0)
    def _():
        yov[...] = yo_ref[...].reshape(NE, DM)

    pieces = [y_ref[:, i * SLOT : (i + 1) * SLOT, :].reshape(NMAIN, 128) for i in range(8)]
    main = jnp.concatenate(pieces, axis=1)
    at = pl.multiple_of(step * 1024, 1024)
    both = jnp.dot(gm_ref[...], main, preferred_element_type=F32) + jnp.dot(
        go_ref[...], yov[:, pl.ds(at, 1024)], preferred_element_type=F32
    )
    r = lax.broadcasted_iota(jnp.int32, (ROWS, ROWS), 0)
    c = lax.broadcasted_iota(jnp.int32, (ROWS, ROWS), 1)
    turn = jnp.where(c == (r & 1) * 64 + (r >> 1), 1.0, 0.0).astype(BF)
    st = jnp.dot(turn, st_ref[...], preferred_element_type=F32)
    o_ref[...] = (st + (both[:ROWS] + both[ROWS:])).astype(BF)


def combine(y, stream, gm, go):
    return pl.pallas_call(
        combine_kernel,
        grid=(4,),
        out_shape=jax.ShapeDtypeStruct((ROWS, DM), BF),
        in_specs=[
            pl.BlockSpec((NE, 128, 128), lambda i: (0, i, 0)),
            pl.BlockSpec((NE, 32, 128), lambda i: (0, 16, 0)),
            pl.BlockSpec((ROWS, 1024), lambda i: (0, i)),
            pl.BlockSpec((2 * ROWS, NMAIN), lambda i: (0, 0)),
            pl.BlockSpec((2 * ROWS, NE), lambda i: (0, 0)),
        ],
        out_specs=pl.BlockSpec((ROWS, 1024), lambda i: (0, i)),
        scratch_shapes=[pltpu.VMEM((NE, DM), BF)],
        compiler_params=pltpu.CompilerParams(vmem_limit_bytes=VMEM_BIG),
        cost_estimate=pl.CostEstimate(
            flops=2 * 2**30, bytes_accessed=11 * 2**20, transcendentals=0
        ),
        name="combine",
    )(y, y, stream, gm, go)


def slots(ids):
    catalog = jnp.arange(NE, dtype=jnp.int32)
    hits = jnp.any(ids[:, :, None] == catalog, axis=1).astype(BF)
    below = (jnp.arange(ROWS)[:, None] > jnp.arange(ROWS)[None, :]).astype(BF)
    before = jnp.dot(below, hits, preferred_element_type=F32)
    slot = jnp.sum(
        jnp.where(ids[:, :, None] == catalog, before[:, None, :], 0.0), axis=-1
    ).astype(jnp.int32)
    return jnp.where(slot < SLOT, ids * SLOT + slot, NMAIN + ids)


def on_device(
    queries,
    keys,
    values,
    q_gain,
    k_gain,
    out_weight,
    hidden_in,
    norm_gain,
    router,
    expert_ids,
    w_gate,
    w_up,
    w_down,
):
    t, e = lax.axis_index("tensor"), lax.axis_index("expert")
    scal = jnp.stack([t & 1, t >> 1, e >> 2, e & 3]).astype(jnp.int32)
    cs, sn = rotate_tables(e * PB + jnp.arange(PB, dtype=jnp.int32))

    kv = ready_keys(
        keys[0].reshape(PB, SEQ * HD), values[0].reshape(PB, SEQ * HD), cs, sn, k_gain.reshape(1, HD)
    )
    kv_all = ring_relay(jnp.stack(ring_four(kv, y_move)), z_move)
    w_all = ring_relay(jnp.stack(ring_four(out_weight, z_move)), y_move)

    q2 = queries[0].reshape(PB, SEQ * 1024)
    ids = expert_ids[0].reshape(ROWS, TOP)
    tgt = slots(ids)
    tgt_t = jnp.transpose(tgt.reshape(64, SEQ, TOP), (2, 1, 0)).reshape(TOP, ROWS)
    hid = jnp.transpose(hidden_in[0], (1, 0, 2)).reshape(ROWS, DM)

    attn = attention(scal, q2, cs, sn, q_gain.reshape(1, HD), kv_all)
    keeps, gots, rests = [], [], []
    for part in range(2):
        keep, send = project(part, scal, attn, w_all)
        got = lax.ppermute(send, "tensor", CORE_SWAP)
        other = (keep[128:].astype(F32) + got[128:].astype(F32)).astype(BF)
        keeps.append(keep)
        gots.append(got)
        rests.append(lax.ppermute(other, "tensor", X_SWAP))
    stream, normed, x = dispatch(
        scal, keeps, gots, rests, hid, norm_gain.reshape(1, DM), tgt_t
    )
    arrived = lax.all_to_all(x, ("tensor", "expert"), split_axis=0, concat_axis=0, tiled=True)

    logits = jnp.dot(normed, router, preferred_element_type=F32)
    logits = jnp.transpose(logits.reshape(SEQ, 64, NE), (1, 0, 2)).reshape(ROWS, NE)
    chosen = ids[:, :, None] == jnp.arange(NE, dtype=jnp.int32)
    gates = jax.nn.softmax(jnp.sum(jnp.where(chosen, logits[:, None, :], 0.0), axis=-1), axis=-1)

    done = run_experts(arrived, w_gate, w_up, w_down)
    back = lax.all_to_all(done, ("tensor", "expert"), split_axis=0, concat_axis=0, tiled=True)
    out = combine(back, stream, *mixing(tgt, gates))
    return out.reshape(hidden_in.shape)


def solution(mesh):
    return jax.shard_map(
        on_device,
        mesh=mesh,
        in_specs=(
            P(("dp", "expert"), None, None, "tensor"),
            P(("dp", "expert"), None, None, "tensor"),
            P(("dp", "expert"), None, None, "tensor"),
            P(),
            P(),
            P("tensor", "expert"),
            P(("dp", "expert"), "tensor", None, None),
            P(),
            P(),
            P(("dp", "expert"), "tensor", None, None),
            P(("tensor", "expert"), None, None),
            P(("tensor", "expert"), None, None),
            P(("tensor", "expert"), None, None),
        ),
        out_specs=P(("dp", "expert"), "tensor", None, None),
        check_vma=False,
    )
```

```python
import functools

import jax
import jax.numpy as jnp
from jax import lax
from jax.experimental import pallas as pl
from jax.experimental.pallas import tpu as pltpu
from jax.sharding import PartitionSpec as P


theta_base = 1000000.0
eps_norm = 1e-06
neg_fill = -1e30
LOG2E = 1.4426950408889634

BF = jnp.bfloat16
F32 = jnp.float32
HD = 128
PB = 256
SEQ = 2
DM = 4096
FF = 768
NE = 64
TOP = 8
ROWS = 128
SLOT = 16
NMAIN = NE * SLOT
NALL = NMAIN + NE
HALF = 8
NHALF = NE * HALF
XA = HALF * 32
XB = XA + 32
VMEM_BIG = 60 * 1024 * 1024


def spot(z, y):
    return (z % 4) * 4 + (y % 4)


def y_move(k):
    return [(spot(z, y), spot(z, y + k)) for z in range(4) for y in range(4)]


def z_move(k):
    return [(spot(z, y), spot(z + k, y)) for z in range(4) for y in range(4)]


CORE_SWAP = [(i, i ^ 1) for i in range(4)]
X_SWAP = [(i, i ^ 2) for i in range(4)]


def ring_four(x, move):
    return [x] + [lax.ppermute(x, "expert", move(k)) for k in (1, 2, 3)]


def ring_relay(x, move):
    half = x.shape[0] // 2
    left = lax.ppermute(x, "expert", move(1))
    right = lax.ppermute(x, "expert", move(3))
    lo = lax.ppermute(left[:half], "expert", move(1))
    hi = lax.ppermute(right[half:], "expert", move(3))
    return x, left, right, lo, hi


def rotate_tables(positions):
    freq = theta_base ** (-2.0 * jnp.arange(HD // 2, dtype=F32) / HD)
    ang = positions.astype(F32)[:, None] * freq[None, :]
    cs, sn = jnp.cos(ang), jnp.sin(ang)
    return jnp.concatenate([cs, cs], axis=1), jnp.concatenate([-sn, sn], axis=1)


def keys_kernel(k_ref, v_ref, cos_ref, sin_ref, gain_ref, o_ref):
    cs, sn, gain = cos_ref[...], sin_ref[...], gain_ref[...]
    for s in range(SEQ):
        k = k_ref[:, s * HD : (s + 1) * HD].astype(F32)
        k = k * lax.rsqrt(jnp.mean(k * k, axis=-1, keepdims=True) + eps_norm) * gain
        o_ref[s, 0:PB, :] = (k * cs + pltpu.roll(k, HD // 2, 1) * sn).astype(BF)
        v = jnp.transpose(v_ref[:, s * HD : (s + 1) * HD].astype(F32)).astype(BF)
        o_ref[s, PB : PB + HD, :] = v[:, :HD]
        o_ref[s, PB + HD :, :] = v[:, HD:]


def ready_keys(k2, v2, cs, sn, gain):
    return pl.pallas_call(
        keys_kernel, out_shape=jax.ShapeDtypeStruct((SEQ, 2 * PB, HD), BF), name="ready_keys"
    )(k2, v2, cs, sn, gain)


C2 = HD ** (-0.5) * LOG2E
VR = HD + 16
HEADS = 8


def attn_part(q_ref, key_of, val_of, load, save, s_buf, mask):
    ones = jnp.ones((16, PB), BF)

    def score(h, j):
        q = q_ref[:, pl.ds(pl.multiple_of(h * HD, HD), HD)]
        s = lax.dot_general(key_of(j), q, (((1,), (1,)), ((), ())), preferred_element_type=F32)
        return s if mask is None else mask(j, s)

    top = None
    for j in range(4):
        s = score(0, j)
        s_buf[0, j] = s
        part = jnp.max(s, axis=0, keepdims=True)
        top = part if j == 0 else jnp.maximum(top, part)

    def body(h, top):
        slot = h & 1
        m_old, acc = load(h)
        m_new = jnp.maximum(m_old, top)
        mc = m_new * C2
        acc = acc * jnp.exp2(m_old * C2 - mc)
        nxt = None
        for j in range(4):
            s = score((h + 1) & (HEADS - 1), j)
            p = jnp.exp2(s_buf[slot, j] * C2 - mc).astype(BF)
            s_buf[1 - slot, j] = s
            part = jnp.max(s, axis=0, keepdims=True)
            nxt = part if j == 0 else jnp.maximum(nxt, part)
            acc = acc + jnp.dot(
                jnp.concatenate([val_of(j), ones], axis=0), p, preferred_element_type=F32
            )
        save(h, m_new, acc)
        return nxt

    lax.fori_loop(0, HEADS, body, top)


def block_keys(kv_ref):
    return (
        lambda j: kv_ref[j, 0, 0:PB, :],
        lambda j: jnp.concatenate(
            [kv_ref[j, 0, PB : PB + HD, :], kv_ref[j, 0, PB + HD :, :]], axis=1
        ),
    )


def attn_first(sc, q_ref, cos_ref, sin_ref, gain_ref, kv_ref, qr_ref, m_ref, acc_ref, s_buf):
    y = sc[3]
    cs, sn, gain = cos_ref[...], sin_ref[...], gain_ref[...]
    for h in range(HEADS):
        q = q_ref[:, h * HD : (h + 1) * HD].astype(F32)
        q = q * lax.rsqrt(jnp.mean(q * q, axis=-1, keepdims=True) + eps_norm) * gain
        qr_ref[:, h * HD : (h + 1) * HD] = (q * cs + pltpu.roll(q, HD // 2, 1) * sn).astype(BF)

    def mask(j, s):
        if j > 0:
            return s + jnp.where(j <= y, 0.0, neg_fill)
        key = lax.broadcasted_iota(jnp.int32, (PB, PB), 0)
        row = lax.broadcasted_iota(jnp.int32, (PB, PB), 1)
        return jnp.where(key <= row, s, neg_fill)

    def load(h):
        return jnp.full((1, PB), neg_fill, F32), jnp.zeros((VR, PB), F32)

    def save(h, m, acc):
        m_ref[h] = jnp.broadcast_to(m, (8, PB))
        acc_ref[h] = acc

    key_of, val_of = block_keys(kv_ref)
    attn_part(qr_ref, key_of, val_of, load, save, s_buf, mask)


def attn_next(sc, q_ref, m_in, acc_in, ka_ref, kb_ref, m_ref, acc_ref, s_buf):
    z = sc[2]

    @pl.when(z == 0)
    def _():
        m_ref[...] = m_in[...]
        acc_ref[...] = acc_in[...]

    for need, kv_ref, m_from, acc_from in ((1, ka_ref, m_in, acc_in), (3, kb_ref, m_ref, acc_ref)):

        @pl.when(z >= need)
        def _(kv_ref=kv_ref, m_from=m_from, acc_from=acc_from):
            def load(h):
                return m_from[h, 0:1, :], acc_from[h]

            def save(h, m, acc):
                m_ref[h] = jnp.broadcast_to(m, (8, PB))
                acc_ref[h] = acc

            key_of, val_of = block_keys(kv_ref)
            attn_part(q_ref, key_of, val_of, load, save, s_buf, None)


def attn_last(sc, q_ref, m_in, acc_in, ka_ref, kb_ref, o_ref, s_buf):
    z = sc[2]

    def finish(h, acc):
        out = jnp.transpose(acc[:HD] / acc[HD : HD + 1])
        o_ref[:, pl.ds(pl.multiple_of(h * HD, HD), HD)] = out.astype(BF)

    @pl.when(z >= 2)
    def _():
        ka, va = block_keys(ka_ref)
        kb, vb = block_keys(kb_ref)
        attn_part(
            q_ref,
            lambda j: ka(j) if j < 2 else kb(j - 2),
            lambda j: va(j) if j < 2 else vb(j - 2),
            lambda h: (m_in[h, 0:1, :], acc_in[h]),
            lambda h, m, acc: finish(h, acc),
            s_buf,
            None,
        )

    @pl.when(z < 2)
    def _():
        def body(h, _):
            finish(h, acc_in[h])
            return 0

        lax.fori_loop(0, HEADS, body, 0)


Q_SPEC = pl.BlockSpec((PB, 1024), lambda i, sc: (0, i))
M_SPEC = pl.BlockSpec((HEADS, 8, PB), lambda i, sc: (i, 0, 0))
A_SPEC = pl.BlockSpec((HEADS, VR, PB), lambda i, sc: (i, 0, 0))


def kv_spec(n):
    return pl.BlockSpec((n, 1, 2 * PB, HD), lambda i, sc: (0, i, 0, 0))


def attn_call(kernel, in_specs, out_specs, out_shape, parts):
    return pl.pallas_call(
        kernel,
        out_shape=out_shape,
        grid_spec=pltpu.PrefetchScalarGridSpec(
            num_scalar_prefetch=1,
            grid=(SEQ,),
            in_specs=in_specs,
            out_specs=out_specs,
            scratch_shapes=[pltpu.VMEM((2, 4, PB, PB), F32)],
        ),
        compiler_params=pltpu.CompilerParams(vmem_limit_bytes=VMEM_BIG),
        cost_estimate=pl.CostEstimate(
            flops=parts * 4 * 2**30, bytes_accessed=8 * 2**20, transcendentals=parts * 4 * 2**20
        ),
    )


STATE = (
    jax.ShapeDtypeStruct((SEQ * HEADS, 8, PB), F32),
    jax.ShapeDtypeStruct((SEQ * HEADS, VR, PB), F32),
)


def attention(scal, q2, cs, sn, gain, pieces):
    own, left, right, lo, hi = pieces
    table = pl.BlockSpec((PB, HD), lambda i, sc: (0, 0))
    qr, m, acc = attn_call(
        attn_first,
        [Q_SPEC, table, table, pl.BlockSpec((1, HD), lambda i, sc: (0, 0)), kv_spec(4)],
        (Q_SPEC, M_SPEC, A_SPEC),
        (jax.ShapeDtypeStruct((PB, SEQ * 1024), BF),) + STATE,
        1,
    )(scal, q2, cs, sn, gain, own)
    m, acc = attn_call(
        attn_next, [Q_SPEC, M_SPEC, A_SPEC, kv_spec(4), kv_spec(4)], (M_SPEC, A_SPEC), STATE, 2
    )(scal, qr, m, acc, left, right)
    return attn_call(
        attn_last,
        [Q_SPEC, M_SPEC, A_SPEC, kv_spec(2), kv_spec(2)],
        Q_SPEC,
        jax.ShapeDtypeStruct((PB, SEQ * 1024), BF),
        1,
    )(scal, qr, m, acc, lo, hi)


def proj_kernel(part, sc, a_ref, *rest):
    w_in, (keep, send, lhs, w, sem) = rest[:4], rest[4:]
    c, xh = sc[0], sc[1]
    two = pl.ds(2 * part, 2)
    moves = [
        (w_in[0].at[two], w.at[:, 0]),
        (w_in[1].at[two], w.at[:, 1]),
        (w_in[2].at[two], w.at[:, 3]),
        (w_in[3], w.at[:, 2]),
    ]
    copies = [pltpu.make_async_copy(a, b, sem.at[i]) for i, (a, b) in enumerate(moves)]
    for cp in copies:
        cp.start()
    for cc in (1, 0):
        for xx in range(2):
            base = pl.multiple_of(64 * (2 * (xh ^ xx) + (c ^ cc)), 64)
            for s in range(SEQ):
                at = cc * 256 + xx * 128 + s * 64
                lhs[at : at + 64, :] = a_ref[pl.ds(base, 64), s * 1024 : (s + 1) * 1024]
    for cp, dy in zip(copies, (0, 1, 3, 2)):
        cp.wait()

        def column(i, _, dy=dy):
            res = jnp.dot(lhs[...], w[i, dy], preferred_element_type=F32).astype(BF)
            lane = pl.multiple_of((i * 4 + dy) * 256, 256)
            keep[:, pl.ds(lane, 256)] = res[:256]
            send[:, pl.ds(lane, 256)] = res[256:]
            return 0

        lax.fori_loop(0, 2, column, 0)


def project(part, scal, attn, pa):
    pieces = list(pa[:3]) + [pa[3 + part]]
    full = pl.BlockSpec(memory_space=pltpu.VMEM)
    return pl.pallas_call(
        functools.partial(proj_kernel, part),
        out_shape=(
            jax.ShapeDtypeStruct((256, DM // 2), BF),
            jax.ShapeDtypeStruct((256, DM // 2), BF),
        ),
        in_specs=[pl.BlockSpec(memory_space=pltpu.SMEM), full]
        + [pl.BlockSpec(memory_space=pl.ANY)] * len(pieces),
        out_specs=(full, full),
        scratch_shapes=[
            pltpu.VMEM((512, 1024), BF),
            pltpu.VMEM((2, 4, 1024, 256), BF),
            pltpu.SemaphoreType.DMA((4,)),
        ],
        compiler_params=pltpu.CompilerParams(vmem_limit_bytes=VMEM_BIG),
        cost_estimate=pl.CostEstimate(
            flops=2 * 2**30, bytes_accessed=7 * 2**20, transcendentals=0
        ),
    )(scal, attn, *pieces)


def pair_tile(x):
    both = [x[:, k * 128 : (k + 1) * 128].reshape(NE, HALF, 128) for k in range(2)]
    return jnp.concatenate(both, axis=1).astype(BF)


def open_tiles(ref, count):
    out = []
    for i in range(count):
        x = ref[:, i * 16 : (i + 1) * 16, :].astype(F32)
        out += [x[:, :HALF].reshape(NHALF, 128), x[:, HALF:].reshape(NHALF, 128)]
    return jnp.concatenate(out, axis=1).astype(BF)


def pick_kernel(tgt_ref, o_ref):
    line = lax.broadcasted_iota(jnp.int32, (NALL, ROWS), 0)
    hit = jnp.zeros((NALL, ROWS), F32)
    for k in range(TOP):
        hit = jnp.where(line == tgt_ref[k : k + 1, :], 1.0, hit)
    o_ref[...] = hit.astype(BF)


def picking(tgt_t):
    return pl.pallas_call(
        pick_kernel,
        out_shape=jax.ShapeDtypeStruct((NALL, ROWS), BF),
        cost_estimate=pl.CostEstimate(flops=2**22, bytes_accessed=2**19, transcendentals=0),
        name="picking",
    )(tgt_t)


def dispatch_kernel(
    sc, k0, k1, g0, g1, r0, r1, h_ref, gain_ref, pick, st_ref, nm_ref, xa_hbm, xb_hbm, x_ref, sem
):
    z, y = sc[2], sc[3]
    square = jnp.zeros((ROWS, 1), F32)
    for dz in range(4):
        k_ref, g_ref, r_ref = (k0, g0, r0) if dz < 2 else (k1, g1, r1)
        for dy in range(4):
            here = (dz & 1) * 1024 + dy * 256
            there = pl.multiple_of((((z - dz) & 3) * 4 + ((y - dy) & 3)) * 256, 256)
            span = slice(here, here + 256)
            total = (
                h_ref[:, pl.ds(there, 256)].astype(F32)
                + (k_ref[:, span].astype(F32) + g_ref[:, span].astype(F32))
                + r_ref[:, span].astype(F32)
            )
            st = total.astype(BF)
            st_ref[:, pl.ds(there, 256)] = st
            sf = st.astype(F32)
            square = square + jnp.sum(sf * sf, axis=-1, keepdims=True)
    scale = lax.rsqrt(square / DM + eps_norm)
    nm_ref[...] = (st_ref[...].astype(F32) * scale * gain_ref[...]).astype(BF)

    def out_copy(chunk, j):
        rows = pl.ds(pl.multiple_of(j * 32, 32), 32)
        to = xa_hbm if chunk == 0 else xb_hbm
        return pltpu.make_async_copy(x_ref.at[chunk, :, rows], to.at[:, rows], sem.at[chunk, j])

    for chunk in range(2):

        def send_part(j, _, chunk=chunk):
            n = nm_ref[:, pl.ds(pl.multiple_of(j * 512, 512), 512)]
            main = jnp.dot(
                pick[chunk * NHALF : (chunk + 1) * NHALF, :], n, preferred_element_type=F32
            )
            for i in range(2):
                at = pl.multiple_of(j * 32 + i * 16, 16)
                x_ref[chunk, :, pl.ds(at, 16), :] = pair_tile(main[:, i * 256 : (i + 1) * 256])
            out_copy(chunk, j).start()
            return 0

        lax.fori_loop(0, 8, send_part, 0)
    ov = jnp.dot(pick[NMAIN:, :], nm_ref[...], preferred_element_type=F32).astype(BF)
    x_ref[1, :, XA:XB, :] = ov.reshape(NE, 32, 128)
    out_copy(1, 8).start()
    for chunk in range(2):
        for j in range(8 + chunk):
            out_copy(chunk, j).wait()


def dispatch(scal, keeps, gots, rests, hid, gain, pick):
    at = lambda i, sc: (0, 0)
    half = pl.BlockSpec((ROWS, DM // 2), at)
    line = pl.BlockSpec((ROWS, DM), at)
    return pl.pallas_call(
        dispatch_kernel,
        out_shape=(
            jax.ShapeDtypeStruct((ROWS, DM), BF),
            jax.ShapeDtypeStruct((ROWS, DM), BF),
            jax.ShapeDtypeStruct((NE, XA, 128), BF),
            jax.ShapeDtypeStruct((NE, XB, 128), BF),
        ),
        grid_spec=pltpu.PrefetchScalarGridSpec(
            num_scalar_prefetch=1,
            grid=(1,),
            in_specs=[half] * 6
            + [line, pl.BlockSpec((1, DM), at), pl.BlockSpec((NALL, ROWS), at)],
            out_specs=(line, line) + (pl.BlockSpec(memory_space=pl.ANY),) * 2,
            scratch_shapes=[pltpu.VMEM((2, NE, XB, 128), BF), pltpu.SemaphoreType.DMA((2, 9))],
        ),
        compiler_params=pltpu.CompilerParams(vmem_limit_bytes=VMEM_BIG),
        cost_estimate=pl.CostEstimate(
            flops=2**30, bytes_accessed=14 * 2**20, transcendentals=0
        ),
        name="dispatch",
    )(scal, *keeps, *gots, *rests, hid, gain, pick)


def expert_kernel(over, *refs):
    x_ref, refs = refs[0], refs[1:]
    if over:
        xo_ref, refs = refs[0], refs[1:]
    wg_ref, wu_ref, wd_ref, y_hbm, ga, ua, inner, yb, sem = refs[:9]
    if over:
        xov, yo = refs[9:]
    step = pl.program_id(0)

    if over:

        @pl.when(step == 0)
        def _():
            xov[...] = xo_ref[...].reshape(NE, DM)

    @pl.when(step < 4)
    def _():
        rows = open_tiles(x_ref, 4)
        if over:
            lane = pl.multiple_of(step * 1024, 1024)
            rows = jnp.concatenate([rows, xov[:, pl.ds(lane, 1024)]], axis=0)
        g = jnp.dot(rows, wg_ref[0], preferred_element_type=F32)
        u = jnp.dot(rows, wu_ref[0], preferred_element_type=F32)

        @pl.when(step == 0)
        def _():
            ga[...] = g
            ua[...] = u

        @pl.when(step > 0)
        def _():
            ga[...] += g
            ua[...] += u

    @pl.when(step == 4)
    def _():
        g = ga[...]
        inner[...] = (g / (1.0 + jnp.exp(-g)) * ua[...]).astype(BF)

    def out_copy(j):
        rows = pl.ds(pl.multiple_of(j * 64, 64), 64)
        return pltpu.make_async_copy(yb.at[j & 1], y_hbm.at[:, rows], sem.at[j & 1])

    @pl.when(step >= 4)
    def _():
        j = step - 4
        out = jnp.dot(inner[...], wd_ref[0], preferred_element_type=F32)

        @pl.when(j >= 2)
        def _():
            out_copy(j - 2).wait()

        for i in range(4):
            yb[j & 1, :, i * 16 : (i + 1) * 16, :] = pair_tile(
                out[:NHALF, i * 256 : (i + 1) * 256]
            )
        out_copy(j).start()
        if over:
            xov[:, pl.ds(pl.multiple_of(j * 1024, 1024), 1024)] = out[NHALF:].astype(BF)

        @pl.when(j == 3)
        def _():
            if over:
                yo[...] = xov[...].reshape(NE, 32, 128)
                last = pltpu.make_async_copy(yo, y_hbm.at[:, pl.ds(XA, 32)], sem.at[2])
                last.start()
                last.wait()
            out_copy(2).wait()
            out_copy(3).wait()


def run_experts(x, wg, wu, wd, over):
    lo = lambda i: jnp.minimum(i, 3)
    n = NHALF + (NE if over else 0)
    x_specs = [pl.BlockSpec((NE, 64, 128), lambda i: (0, lo(i), 0))]
    extra = []
    if over:
        x_specs.append(pl.BlockSpec((NE, 32, 128), lambda i: (0, 8, 0)))
        extra = [pltpu.VMEM((NE, DM), BF), pltpu.VMEM((NE, 32, 128), BF)]
    return pl.pallas_call(
        functools.partial(expert_kernel, over),
        grid=(8,),
        out_shape=jax.ShapeDtypeStruct(x.shape, BF),
        in_specs=x_specs
        + [
            pl.BlockSpec((1, 1024, FF), lambda i: (0, lo(i), 0)),
            pl.BlockSpec((1, 1024, FF), lambda i: (0, lo(i), 0)),
            pl.BlockSpec((1, FF, 1024), lambda i: (0, 0, jnp.maximum(i - 4, 0))),
        ],
        out_specs=pl.BlockSpec(memory_space=pl.ANY),
        scratch_shapes=[
            pltpu.VMEM((n, FF), F32),
            pltpu.VMEM((n, FF), F32),
            pltpu.VMEM((n, FF), BF),
            pltpu.VMEM((2, NE, 64, 128), BF),
            pltpu.SemaphoreType.DMA((3,)),
        ]
        + extra,
        compiler_params=pltpu.CompilerParams(vmem_limit_bytes=VMEM_BIG),
        cost_estimate=pl.CostEstimate(
            flops=10 * 2**30, bytes_accessed=27 * 2**20, transcendentals=2**19
        ),
        name="experts_b" if over else "experts_a",
    )(*([x] * len(x_specs)), wg, wu, wd)


def mix_kernel(tgt_ref, gate_ref, gm, go):
    lane = lax.broadcasted_iota(jnp.int32, (ROWS, NALL), 1)
    mix = jnp.zeros((ROWS, NALL), F32)
    for k in range(TOP):
        mix = jnp.where(lane == tgt_ref[:, k : k + 1], gate_ref[:, k : k + 1], mix)
    hi = mix.astype(BF)
    lo = (mix - hi.astype(F32)).astype(BF)
    gm[:ROWS] = hi[:, :NMAIN]
    gm[ROWS:] = lo[:, :NMAIN]
    go[:ROWS] = hi[:, NMAIN:]
    go[ROWS:] = lo[:, NMAIN:]


def mixing(tgt, gates):
    return pl.pallas_call(
        mix_kernel,
        out_shape=(
            jax.ShapeDtypeStruct((2 * ROWS, NMAIN), BF),
            jax.ShapeDtypeStruct((2 * ROWS, NE), BF),
        ),
        cost_estimate=pl.CostEstimate(flops=2**22, bytes_accessed=2**20, transcendentals=0),
        name="mixing",
    )(tgt, gates)


def combine_kernel(ya_ref, yb_ref, yo_ref, st_ref, gm_ref, go_ref, o_ref, yov):
    step = pl.program_id(0)

    @pl.when(step == 0)
    def _():
        yov[...] = yo_ref[...].reshape(NE, DM)

    main = jnp.concatenate([open_tiles(ya_ref, 4), open_tiles(yb_ref, 4)], axis=0)
    at = pl.multiple_of(step * 1024, 1024)
    both = jnp.dot(gm_ref[...], main, preferred_element_type=F32) + jnp.dot(
        go_ref[...], yov[:, pl.ds(at, 1024)], preferred_element_type=F32
    )
    r = lax.broadcasted_iota(jnp.int32, (ROWS, ROWS), 0)
    c = lax.broadcasted_iota(jnp.int32, (ROWS, ROWS), 1)
    turn = jnp.where(c == (r & 1) * 64 + (r >> 1), 1.0, 0.0).astype(BF)
    st = jnp.dot(turn, st_ref[...], preferred_element_type=F32)
    o_ref[...] = (st + (both[:ROWS] + both[ROWS:])).astype(BF)


def combine(ya, yb, stream, gm, go):
    return pl.pallas_call(
        combine_kernel,
        grid=(4,),
        out_shape=jax.ShapeDtypeStruct((ROWS, DM), BF),
        in_specs=[
            pl.BlockSpec((NE, 64, 128), lambda i: (0, i, 0)),
            pl.BlockSpec((NE, 64, 128), lambda i: (0, i, 0)),
            pl.BlockSpec((NE, 32, 128), lambda i: (0, 8, 0)),
            pl.BlockSpec((ROWS, 1024), lambda i: (0, i)),
            pl.BlockSpec((2 * ROWS, NMAIN), lambda i: (0, 0)),
            pl.BlockSpec((2 * ROWS, NE), lambda i: (0, 0)),
        ],
        out_specs=pl.BlockSpec((ROWS, 1024), lambda i: (0, i)),
        scratch_shapes=[pltpu.VMEM((NE, DM), BF)],
        compiler_params=pltpu.CompilerParams(vmem_limit_bytes=VMEM_BIG),
        cost_estimate=pl.CostEstimate(
            flops=2 * 2**30, bytes_accessed=11 * 2**20, transcendentals=0
        ),
        name="combine",
    )(ya, yb, yb, stream, gm, go)


def slots(ids):
    catalog = jnp.arange(NE, dtype=jnp.int32)
    hits = jnp.any(ids[:, :, None] == catalog, axis=1).astype(BF)
    below = (jnp.arange(ROWS)[:, None] > jnp.arange(ROWS)[None, :]).astype(BF)
    before = jnp.dot(below, hits, preferred_element_type=F32)
    slot = jnp.sum(
        jnp.where(ids[:, :, None] == catalog, before[:, None, :], 0.0), axis=-1
    ).astype(jnp.int32)
    main = ids * HALF + (slot & (HALF - 1)) + jnp.where(slot < HALF, 0, NHALF)
    return jnp.where(slot < SLOT, main, NMAIN + ids)


def on_device(
    queries,
    keys,
    values,
    q_gain,
    k_gain,
    out_weight,
    hidden_in,
    norm_gain,
    router,
    expert_ids,
    w_gate,
    w_up,
    w_down,
):
    t, e = lax.axis_index("tensor"), lax.axis_index("expert")
    scal = jnp.stack([t & 1, t >> 1, e >> 2, e & 3]).astype(jnp.int32)
    cs, sn = rotate_tables(e * PB + jnp.arange(PB, dtype=jnp.int32))

    kv = ready_keys(
        keys[0].reshape(PB, SEQ * HD), values[0].reshape(PB, SEQ * HD), cs, sn, k_gain.reshape(1, HD)
    )
    kv_all = ring_relay(jnp.stack(ring_four(kv, y_move)), z_move)
    w_all = ring_relay(jnp.stack(ring_four(out_weight, z_move)), y_move)

    q2 = queries[0].reshape(PB, SEQ * 1024)
    ids = expert_ids[0].reshape(ROWS, TOP)
    tgt = slots(ids)
    tgt_t = jnp.transpose(tgt.reshape(64, SEQ, TOP), (2, 1, 0)).reshape(TOP, ROWS)
    pick = picking(tgt_t)
    hid = jnp.transpose(hidden_in[0], (1, 0, 2)).reshape(ROWS, DM)

    attn = attention(scal, q2, cs, sn, q_gain.reshape(1, HD), kv_all)
    keeps, gots, rests = [], [], []
    for part in range(2):
        keep, send = project(part, scal, attn, w_all)
        got = lax.ppermute(send, "tensor", CORE_SWAP)
        other = (keep[128:].astype(F32) + got[128:].astype(F32)).astype(BF)
        keeps.append(keep)
        gots.append(got)
        rests.append(lax.ppermute(other, "tensor", X_SWAP))
    stream, normed, xa, xb = dispatch(scal, keeps, gots, rests, hid, norm_gain.reshape(1, DM), pick)

    def exchange(x):
        return lax.all_to_all(x, ("tensor", "expert"), split_axis=0, concat_axis=0, tiled=True)

    in_a, in_b = exchange(xa), exchange(xb)

    logits = jnp.dot(normed, router, preferred_element_type=F32)
    logits = jnp.transpose(logits.reshape(SEQ, 64, NE), (1, 0, 2)).reshape(ROWS, NE)
    chosen = ids[:, :, None] == jnp.arange(NE, dtype=jnp.int32)
    gates = jax.nn.softmax(jnp.sum(jnp.where(chosen, logits[:, None, :], 0.0), axis=-1), axis=-1)

    back_a = exchange(run_experts(in_a, w_gate, w_up, w_down, False))
    back_b = exchange(run_experts(in_b, w_gate, w_up, w_down, True))
    out = combine(back_a, back_b, stream, *mixing(tgt, gates))
    return out.reshape(hidden_in.shape)


def solution(mesh):
    return jax.shard_map(
        on_device,
        mesh=mesh,
        in_specs=(
            P(("dp", "expert"), None, None, "tensor"),
            P(("dp", "expert"), None, None, "tensor"),
            P(("dp", "expert"), None, None, "tensor"),
            P(),
            P(),
            P("tensor", "expert"),
            P(("dp", "expert"), "tensor", None, None),
            P(),
            P(),
            P(("dp", "expert"), "tensor", None, None),
            P(("tensor", "expert"), None, None),
            P(("tensor", "expert"), None, None),
            P(("tensor", "expert"), None, None),
        ),
        out_specs=P(("dp", "expert"), "tensor", None, None),
        check_vma=False,
    )
```

```python
import functools

import jax
import jax.numpy as jnp
from jax import lax
from jax.experimental import pallas as pl
from jax.experimental.pallas import tpu as pltpu
from jax.sharding import PartitionSpec as P


theta_base = 1000000.0
eps_norm = 1e-06
neg_fill = -1e30
LOG2E = 1.4426950408889634

BF = jnp.bfloat16
F32 = jnp.float32
HD = 128
PB = 256
SEQ = 2
DM = 4096
FF = 768
NE = 64
TOP = 8
ROWS = 128
SLOT = 16
NMAIN = NE * SLOT
NALL = NMAIN + NE
HALF = 8
NHALF = NE * HALF
XA = HALF * 32
XB = XA + 32
VMEM_BIG = 60 * 1024 * 1024


def spot(z, y):
    return (z % 4) * 4 + (y % 4)


def y_move(k):
    return [(spot(z, y), spot(z, y + k)) for z in range(4) for y in range(4)]


def z_move(k):
    return [(spot(z, y), spot(z + k, y)) for z in range(4) for y in range(4)]


CORE_SWAP = [(i, i ^ 1) for i in range(4)]
X_SWAP = [(i, i ^ 2) for i in range(4)]


def ring_four(x, move):
    return [x] + [lax.ppermute(x, "expert", move(k)) for k in (1, 2, 3)]


def ring_relay(x, move):
    half = x.shape[0] // 2
    left = lax.ppermute(x, "expert", move(1))
    right = lax.ppermute(x, "expert", move(3))
    lo = lax.ppermute(left[:half], "expert", move(1))
    hi = lax.ppermute(right[half:], "expert", move(3))
    return x, left, right, lo, hi


def rotate_tables(positions):
    freq = theta_base ** (-2.0 * jnp.arange(HD // 2, dtype=F32) / HD)
    ang = positions.astype(F32)[:, None] * freq[None, :]
    cs, sn = jnp.cos(ang), jnp.sin(ang)
    return jnp.concatenate([cs, cs], axis=1), jnp.concatenate([-sn, sn], axis=1)


def keys_kernel(k_ref, v_ref, cos_ref, sin_ref, gain_ref, o_ref):
    cs, sn, gain = cos_ref[...], sin_ref[...], gain_ref[...]
    for s in range(SEQ):
        k = k_ref[:, s * HD : (s + 1) * HD].astype(F32)
        k = k * lax.rsqrt(jnp.mean(k * k, axis=-1, keepdims=True) + eps_norm) * gain
        o_ref[s, 0:PB, :] = (k * cs + pltpu.roll(k, HD // 2, 1) * sn).astype(BF)
        v = jnp.transpose(v_ref[:, s * HD : (s + 1) * HD].astype(F32)).astype(BF)
        o_ref[s, PB : PB + HD, :] = v[:, :HD]
        o_ref[s, PB + HD :, :] = v[:, HD:]


def ready_keys(k2, v2, cs, sn, gain):
    return pl.pallas_call(
        keys_kernel, out_shape=jax.ShapeDtypeStruct((SEQ, 2 * PB, HD), BF), name="ready_keys"
    )(k2, v2, cs, sn, gain)


C2 = HD ** (-0.5) * LOG2E
VR = HD + 16
HEADS = 8


def attn_part(q_ref, key_of, val_of, load, save, s_buf, mask):
    ones = jnp.ones((16, PB), BF)

    def score(h, j):
        q = q_ref[:, pl.ds(pl.multiple_of(h * HD, HD), HD)]
        s = lax.dot_general(key_of(j), q, (((1,), (1,)), ((), ())), preferred_element_type=F32)
        return s if mask is None else mask(j, s)

    top = None
    for j in range(4):
        s = score(0, j)
        s_buf[0, j] = s
        part = jnp.max(s, axis=0, keepdims=True)
        top = part if j == 0 else jnp.maximum(top, part)

    def body(h, top):
        slot = h & 1
        m_old, acc = load(h)
        m_new = jnp.maximum(m_old, top)
        mc = m_new * C2
        acc = acc * jnp.exp2(m_old * C2 - mc)
        nxt = None
        for j in range(4):
            s = score((h + 1) & (HEADS - 1), j)
            p = jnp.exp2(s_buf[slot, j] * C2 - mc).astype(BF)
            s_buf[1 - slot, j] = s
            part = jnp.max(s, axis=0, keepdims=True)
            nxt = part if j == 0 else jnp.maximum(nxt, part)
            acc = acc + jnp.dot(
                jnp.concatenate([val_of(j), ones], axis=0), p, preferred_element_type=F32
            )
        save(h, m_new, acc)
        return nxt

    lax.fori_loop(0, HEADS, body, top)


def block_keys(kv_ref):
    return (
        lambda j: kv_ref[j, 0, 0:PB, :],
        lambda j: jnp.concatenate(
            [kv_ref[j, 0, PB : PB + HD, :], kv_ref[j, 0, PB + HD :, :]], axis=1
        ),
    )


def attn_first(sc, q_ref, cos_ref, sin_ref, gain_ref, kv_ref, qr_ref, m_ref, acc_ref, s_buf):
    y = sc[3]
    cs, sn, gain = cos_ref[...], sin_ref[...], gain_ref[...]

    def turn_head(h, _):
        lanes = pl.ds(pl.multiple_of(h * HD, HD), HD)
        q = q_ref[:, lanes].astype(F32)
        q = q * lax.rsqrt(jnp.mean(q * q, axis=-1, keepdims=True) + eps_norm) * gain
        qr_ref[:, lanes] = (q * cs + pltpu.roll(q, HD // 2, 1) * sn).astype(BF)
        return 0

    lax.fori_loop(0, HEADS, turn_head, 0)

    def mask(j, s):
        if j > 0:
            return s + jnp.where(j <= y, 0.0, neg_fill)
        key = lax.broadcasted_iota(jnp.int32, (PB, PB), 0)
        row = lax.broadcasted_iota(jnp.int32, (PB, PB), 1)
        return jnp.where(key <= row, s, neg_fill)

    def load(h):
        return jnp.full((1, PB), neg_fill, F32), jnp.zeros((VR, PB), F32)

    def save(h, m, acc):
        m_ref[h] = jnp.broadcast_to(m, (8, PB))
        acc_ref[h] = acc

    key_of, val_of = block_keys(kv_ref)
    attn_part(qr_ref, key_of, val_of, load, save, s_buf, mask)


def attn_next(sc, q_ref, m_in, acc_in, ka_ref, kb_ref, m_ref, acc_ref, s_buf):
    z = sc[2]

    @pl.when(z == 0)
    def _():
        m_ref[...] = m_in[...]
        acc_ref[...] = acc_in[...]

    for need, kv_ref, m_from, acc_from in ((1, ka_ref, m_in, acc_in), (3, kb_ref, m_ref, acc_ref)):

        @pl.when(z >= need)
        def _(kv_ref=kv_ref, m_from=m_from, acc_from=acc_from):
            def load(h):
                return m_from[h, 0:1, :], acc_from[h]

            def save(h, m, acc):
                m_ref[h] = jnp.broadcast_to(m, (8, PB))
                acc_ref[h] = acc

            key_of, val_of = block_keys(kv_ref)
            attn_part(q_ref, key_of, val_of, load, save, s_buf, None)


def attn_last(sc, q_ref, m_in, acc_in, ka_ref, kb_ref, o_ref, s_buf):
    z = sc[2]

    def finish(h, acc):
        out = jnp.transpose(acc[:HD] / acc[HD : HD + 1])
        o_ref[:, pl.ds(pl.multiple_of(h * HD, HD), HD)] = out.astype(BF)

    @pl.when(z >= 2)
    def _():
        ka, va = block_keys(ka_ref)
        kb, vb = block_keys(kb_ref)
        attn_part(
            q_ref,
            lambda j: ka(j) if j < 2 else kb(j - 2),
            lambda j: va(j) if j < 2 else vb(j - 2),
            lambda h: (m_in[h, 0:1, :], acc_in[h]),
            lambda h, m, acc: finish(h, acc),
            s_buf,
            None,
        )

    @pl.when(z < 2)
    def _():
        def body(h, _):
            finish(h, acc_in[h])
            return 0

        lax.fori_loop(0, HEADS, body, 0)


Q_SPEC = pl.BlockSpec((PB, 1024), lambda i, sc: (0, i))
M_SPEC = pl.BlockSpec((HEADS, 8, PB), lambda i, sc: (i, 0, 0))
A_SPEC = pl.BlockSpec((HEADS, VR, PB), lambda i, sc: (i, 0, 0))


def kv_spec(n):
    return pl.BlockSpec((n, 1, 2 * PB, HD), lambda i, sc: (0, i, 0, 0))


def attn_call(kernel, in_specs, out_specs, out_shape, parts):
    return pl.pallas_call(
        kernel,
        out_shape=out_shape,
        grid_spec=pltpu.PrefetchScalarGridSpec(
            num_scalar_prefetch=1,
            grid=(SEQ,),
            in_specs=in_specs,
            out_specs=out_specs,
            scratch_shapes=[pltpu.VMEM((2, 4, PB, PB), F32)],
        ),
        compiler_params=pltpu.CompilerParams(vmem_limit_bytes=VMEM_BIG),
        cost_estimate=pl.CostEstimate(
            flops=parts * 4 * 2**30, bytes_accessed=8 * 2**20, transcendentals=parts * 4 * 2**20
        ),
    )


STATE = (
    jax.ShapeDtypeStruct((SEQ * HEADS, 8, PB), F32),
    jax.ShapeDtypeStruct((SEQ * HEADS, VR, PB), F32),
)


def attention(scal, q2, cs, sn, gain, pieces):
    own, left, right, lo, hi = pieces
    table = pl.BlockSpec((PB, HD), lambda i, sc: (0, 0))
    qr, m, acc = attn_call(
        attn_first,
        [Q_SPEC, table, table, pl.BlockSpec((1, HD), lambda i, sc: (0, 0)), kv_spec(4)],
        (Q_SPEC, M_SPEC, A_SPEC),
        (jax.ShapeDtypeStruct((PB, SEQ * 1024), BF),) + STATE,
        1,
    )(scal, q2, cs, sn, gain, own)
    m, acc = attn_call(
        attn_next, [Q_SPEC, M_SPEC, A_SPEC, kv_spec(4), kv_spec(4)], (M_SPEC, A_SPEC), STATE, 2
    )(scal, qr, m, acc, left, right)
    return attn_call(
        attn_last,
        [Q_SPEC, M_SPEC, A_SPEC, kv_spec(2), kv_spec(2)],
        Q_SPEC,
        jax.ShapeDtypeStruct((PB, SEQ * 1024), BF),
        1,
    )(scal, qr, m, acc, lo, hi)


def proj_kernel(part, sc, a_ref, *rest):
    w_in, (keep, send, lhs, w, sem) = rest[:8], rest[8:]
    c, xh = sc[0], sc[1]
    two = pl.ds(2 * part, 2)
    moves = []
    for half in range(2):
        rows = pl.ds(half * 512, 512)
        for k, dy in enumerate((0, 1, 3)):
            moves.append((dy, w_in[4 * half + k].at[two], w.at[:, dy, rows]))
        moves.append((2, w_in[4 * half + 3], w.at[:, 2, rows]))
    copies = [(d, pltpu.make_async_copy(a, b, sem.at[i])) for i, (d, a, b) in enumerate(moves)]
    for _, cp in copies:
        cp.start()
    for cc in (1, 0):
        for xx in range(2):
            base = pl.multiple_of(64 * (2 * (xh ^ xx) + (c ^ cc)), 64)
            for s in range(SEQ):
                at = cc * 256 + xx * 128 + s * 64
                lhs[at : at + 64, :] = a_ref[pl.ds(base, 64), s * 1024 : (s + 1) * 1024]
    for dy in (0, 1, 3, 2):
        for d, cp in copies:
            if d == dy:
                cp.wait()
        for i in range(2):
            res = jnp.dot(lhs[...], w[i, dy], preferred_element_type=F32).astype(BF)
            lane = (i * 4 + dy) * 256
            keep[:, lane : lane + 256] = res[:256]
            send[:, lane : lane + 256] = res[256:]


def project(part, scal, attn, halves):
    pieces = [x for h in halves for x in (h[0], h[1], h[2], h[3 + part])]
    full = pl.BlockSpec(memory_space=pltpu.VMEM)
    return pl.pallas_call(
        functools.partial(proj_kernel, part),
        out_shape=(
            jax.ShapeDtypeStruct((256, DM // 2), BF),
            jax.ShapeDtypeStruct((256, DM // 2), BF),
        ),
        in_specs=[pl.BlockSpec(memory_space=pltpu.SMEM), full]
        + [pl.BlockSpec(memory_space=pl.ANY)] * len(pieces),
        out_specs=(full, full),
        scratch_shapes=[
            pltpu.VMEM((512, 1024), BF),
            pltpu.VMEM((2, 4, 1024, 256), BF),
            pltpu.SemaphoreType.DMA((8,)),
        ],
        compiler_params=pltpu.CompilerParams(vmem_limit_bytes=VMEM_BIG),
        cost_estimate=pl.CostEstimate(
            flops=2 * 2**30, bytes_accessed=7 * 2**20, transcendentals=0
        ),
    )(scal, attn, *pieces)


def pair_tile(x):
    both = [x[:, k * 128 : (k + 1) * 128].reshape(NE, HALF, 128) for k in range(2)]
    return jnp.concatenate(both, axis=1).astype(BF)


def open_tiles(ref, count):
    out = []
    for i in range(count):
        x = ref[:, i * 16 : (i + 1) * 16, :].astype(F32)
        out += [x[:, :HALF].reshape(NHALF, 128), x[:, HALF:].reshape(NHALF, 128)]
    return jnp.concatenate(out, axis=1).astype(BF)


def pick_kernel(tgt_ref, o_ref):
    def block(b, _):
        base = pl.multiple_of(b * 64, 64)
        line = lax.broadcasted_iota(jnp.int32, (64, ROWS), 0) + base
        hit = jnp.zeros((64, ROWS), F32)
        for k in range(TOP):
            hit = jnp.where(line == tgt_ref[k : k + 1, :], 1.0, hit)
        o_ref[pl.ds(base, 64), :] = hit.astype(BF)
        return 0

    lax.fori_loop(0, NALL // 64, block, 0)


def picking(tgt_t):
    return pl.pallas_call(
        pick_kernel,
        out_shape=jax.ShapeDtypeStruct((NALL, ROWS), BF),
        cost_estimate=pl.CostEstimate(flops=2**22, bytes_accessed=2**19, transcendentals=0),
        name="picking",
    )(tgt_t)


def dispatch_kernel(
    sc, k0, k1, g0, g1, r0, r1, h_ref, gain_ref, pick, st_ref, nm_ref, xa_hbm, xb_hbm, x_ref, sem
):
    z, y = sc[2], sc[3]
    square = jnp.zeros((ROWS, 1), F32)
    for dz in range(4):
        k_ref, g_ref, r_ref = (k0, g0, r0) if dz < 2 else (k1, g1, r1)
        for dy in range(4):
            here = (dz & 1) * 1024 + dy * 256
            there = pl.multiple_of((((z - dz) & 3) * 4 + ((y - dy) & 3)) * 256, 256)
            span = slice(here, here + 256)
            total = (
                h_ref[:, pl.ds(there, 256)].astype(F32)
                + (k_ref[:, span].astype(F32) + g_ref[:, span].astype(F32))
                + r_ref[:, span].astype(F32)
            )
            st = total.astype(BF)
            st_ref[:, pl.ds(there, 256)] = st
            sf = st.astype(F32)
            square = square + jnp.sum(sf * sf, axis=-1, keepdims=True)
    scale = lax.rsqrt(square / DM + eps_norm)
    nm_ref[...] = (st_ref[...].astype(F32) * scale * gain_ref[...]).astype(BF)

    def out_copy(chunk, j):
        rows = pl.ds(pl.multiple_of(j * 32, 32), 32)
        to = xa_hbm if chunk == 0 else xb_hbm
        return pltpu.make_async_copy(x_ref.at[chunk, :, rows], to.at[:, rows], sem.at[chunk, j])

    def send_part(it, _):
        for jj in range(2):
            j = 2 * it + jj
            n = nm_ref[:, pl.ds(pl.multiple_of(j * 512, 512), 512)]
            for chunk in range(2):
                main = jnp.dot(
                    pick[chunk * NHALF : (chunk + 1) * NHALF, :], n, preferred_element_type=F32
                )
                for i in range(2):
                    at = pl.multiple_of(j * 32 + i * 16, 16)
                    x_ref[chunk, :, pl.ds(at, 16), :] = pair_tile(
                        main[:, i * 256 : (i + 1) * 256]
                    )
                out_copy(chunk, j).start()
        return 0

    lax.fori_loop(0, 4, send_part, 0)
    ov = jnp.dot(pick[NMAIN:, :], nm_ref[...], preferred_element_type=F32).astype(BF)
    x_ref[1, :, XA:XB, :] = ov.reshape(NE, 32, 128)
    out_copy(1, 8).start()
    for chunk in range(2):
        for j in range(8 + chunk):
            out_copy(chunk, j).wait()


def dispatch(scal, keeps, gots, rests, hid, gain, pick):
    at = lambda i, sc: (0, 0)
    half = pl.BlockSpec((ROWS, DM // 2), at)
    line = pl.BlockSpec((ROWS, DM), at)
    return pl.pallas_call(
        dispatch_kernel,
        out_shape=(
            jax.ShapeDtypeStruct((ROWS, DM), BF),
            jax.ShapeDtypeStruct((ROWS, DM), BF),
            jax.ShapeDtypeStruct((NE, XA, 128), BF),
            jax.ShapeDtypeStruct((NE, XB, 128), BF),
        ),
        grid_spec=pltpu.PrefetchScalarGridSpec(
            num_scalar_prefetch=1,
            grid=(1,),
            in_specs=[half] * 6
            + [line, pl.BlockSpec((1, DM), at), pl.BlockSpec((NALL, ROWS), at)],
            out_specs=(line, line) + (pl.BlockSpec(memory_space=pl.ANY),) * 2,
            scratch_shapes=[pltpu.VMEM((2, NE, XB, 128), BF), pltpu.SemaphoreType.DMA((2, 9))],
        ),
        compiler_params=pltpu.CompilerParams(vmem_limit_bytes=VMEM_BIG),
        cost_estimate=pl.CostEstimate(
            flops=2**30, bytes_accessed=14 * 2**20, transcendentals=0
        ),
        name="dispatch",
    )(scal, *keeps, *gots, *rests, hid, gain, pick)


def expert_kernel(over, *refs):
    x_ref, refs = refs[0], refs[1:]
    if over:
        xo_ref, refs = refs[0], refs[1:]
    wg_ref, wu_ref, wd_ref, y_hbm, ga, ua, inner, yb, sem = refs[:9]
    if over:
        xov, yo = refs[9:]
    step = pl.program_id(0)

    if over:

        @pl.when(step == 0)
        def _():
            xov[...] = xo_ref[...].reshape(NE, DM)

    @pl.when(step < 4)
    def _():
        rows = open_tiles(x_ref, 4)
        if over:
            lane = pl.multiple_of(step * 1024, 1024)
            rows = jnp.concatenate([rows, xov[:, pl.ds(lane, 1024)]], axis=0)
        g = jnp.dot(rows, wg_ref[0], preferred_element_type=F32)
        u = jnp.dot(rows, wu_ref[0], preferred_element_type=F32)

        @pl.when(step == 0)
        def _():
            ga[...] = g
            ua[...] = u

        @pl.when(step > 0)
        def _():
            ga[...] += g
            ua[...] += u

    @pl.when(step == 4)
    def _():
        g = ga[...]
        inner[...] = (g / (1.0 + jnp.exp(-g)) * ua[...]).astype(BF)

    def out_copy(j):
        rows = pl.ds(pl.multiple_of(j * 64, 64), 64)
        return pltpu.make_async_copy(yb.at[j & 1], y_hbm.at[:, rows], sem.at[j & 1])

    @pl.when(step >= 4)
    def _():
        j = step - 4
        out = jnp.dot(inner[...], wd_ref[0], preferred_element_type=F32)

        @pl.when(j >= 2)
        def _():
            out_copy(j - 2).wait()

        for i in range(4):
            yb[j & 1, :, i * 16 : (i + 1) * 16, :] = pair_tile(
                out[:NHALF, i * 256 : (i + 1) * 256]
            )
        out_copy(j).start()
        if over:
            xov[:, pl.ds(pl.multiple_of(j * 1024, 1024), 1024)] = out[NHALF:].astype(BF)

        @pl.when(j == 3)
        def _():
            if over:
                yo[...] = xov[...].reshape(NE, 32, 128)
                last = pltpu.make_async_copy(yo, y_hbm.at[:, pl.ds(XA, 32)], sem.at[2])
                last.start()
                last.wait()
            out_copy(2).wait()
            out_copy(3).wait()


def run_experts(x, wg, wu, wd, over):
    lo = lambda i: jnp.minimum(i, 3)
    n = NHALF + (NE if over else 0)
    x_specs = [pl.BlockSpec((NE, 64, 128), lambda i: (0, lo(i), 0))]
    extra = []
    if over:
        x_specs.append(pl.BlockSpec((NE, 32, 128), lambda i: (0, 8, 0)))
        extra = [pltpu.VMEM((NE, DM), BF), pltpu.VMEM((NE, 32, 128), BF)]
    return pl.pallas_call(
        functools.partial(expert_kernel, over),
        grid=(8,),
        out_shape=jax.ShapeDtypeStruct(x.shape, BF),
        in_specs=x_specs
        + [
            pl.BlockSpec((1, 1024, FF), lambda i: (0, lo(i), 0)),
            pl.BlockSpec((1, 1024, FF), lambda i: (0, lo(i), 0)),
            pl.BlockSpec((1, FF, 1024), lambda i: (0, 0, jnp.maximum(i - 4, 0))),
        ],
        out_specs=pl.BlockSpec(memory_space=pl.ANY),
        scratch_shapes=[
            pltpu.VMEM((n, FF), F32),
            pltpu.VMEM((n, FF), F32),
            pltpu.VMEM((n, FF), BF),
            pltpu.VMEM((2, NE, 64, 128), BF),
            pltpu.SemaphoreType.DMA((3,)),
        ]
        + extra,
        compiler_params=pltpu.CompilerParams(vmem_limit_bytes=VMEM_BIG),
        cost_estimate=pl.CostEstimate(
            flops=10 * 2**30, bytes_accessed=27 * 2**20, transcendentals=2**19
        ),
        name="experts_b" if over else "experts_a",
    )(*([x] * len(x_specs)), wg, wu, wd)


def mix_kernel(tgt_ref, gate_ref, gm, go):
    def block(b, _):
        base = pl.multiple_of(b * 32, 32)
        own, other = pl.ds(base, 32), pl.ds(base + ROWS, 32)
        lane = lax.broadcasted_iota(jnp.int32, (32, NALL), 1)
        mix = jnp.zeros((32, NALL), F32)
        for k in range(TOP):
            mix = jnp.where(lane == tgt_ref[own, k : k + 1], gate_ref[own, k : k + 1], mix)
        hi = mix.astype(BF)
        lo = (mix - hi.astype(F32)).astype(BF)
        gm[own, :] = hi[:, :NMAIN]
        gm[other, :] = lo[:, :NMAIN]
        go[own, :] = hi[:, NMAIN:]
        go[other, :] = lo[:, NMAIN:]
        return 0

    lax.fori_loop(0, ROWS // 32, block, 0)


def mixing(tgt, gates):
    return pl.pallas_call(
        mix_kernel,
        out_shape=(
            jax.ShapeDtypeStruct((2 * ROWS, NMAIN), BF),
            jax.ShapeDtypeStruct((2 * ROWS, NE), BF),
        ),
        cost_estimate=pl.CostEstimate(flops=2**22, bytes_accessed=2**20, transcendentals=0),
        name="mixing",
    )(tgt, gates)


def combine_first(y_ref, st_ref, gm_ref, o_ref):
    both = jnp.dot(gm_ref[...], open_tiles(y_ref, 4), preferred_element_type=F32)
    r = lax.broadcasted_iota(jnp.int32, (ROWS, ROWS), 0)
    c = lax.broadcasted_iota(jnp.int32, (ROWS, ROWS), 1)
    turn = jnp.where(c == (r & 1) * 64 + (r >> 1), 1.0, 0.0).astype(BF)
    st = jnp.dot(turn, st_ref[...], preferred_element_type=F32)
    o_ref[...] = st + (both[:ROWS] + both[ROWS:])


def combine_last(y_ref, yo_ref, sum_ref, gm_ref, go_ref, o_ref, yov):
    step = pl.program_id(0)

    @pl.when(step == 0)
    def _():
        yov[...] = yo_ref[...].reshape(NE, DM)

    at = pl.multiple_of(step * 1024, 1024)
    both = jnp.dot(gm_ref[...], open_tiles(y_ref, 4), preferred_element_type=F32) + jnp.dot(
        go_ref[...], yov[:, pl.ds(at, 1024)], preferred_element_type=F32
    )
    o_ref[...] = (sum_ref[...] + (both[:ROWS] + both[ROWS:])).astype(BF)


def combine(ya, yb, stream, gm, go):
    tile = pl.BlockSpec((NE, 64, 128), lambda i: (0, i, 0))
    line = pl.BlockSpec((ROWS, 1024), lambda i: (0, i))
    params = pltpu.CompilerParams(vmem_limit_bytes=VMEM_BIG)
    cost = pl.CostEstimate(flops=2**30, bytes_accessed=6 * 2**20, transcendentals=0)
    total = pl.pallas_call(
        combine_first,
        grid=(4,),
        out_shape=jax.ShapeDtypeStruct((ROWS, DM), F32),
        in_specs=[tile, line, pl.BlockSpec((2 * ROWS, NHALF), lambda i: (0, 0))],
        out_specs=line,
        compiler_params=params,
        cost_estimate=cost,
        name="combine_first",
    )(ya, stream, gm)
    return pl.pallas_call(
        combine_last,
        grid=(4,),
        out_shape=jax.ShapeDtypeStruct((ROWS, DM), BF),
        in_specs=[
            tile,
            pl.BlockSpec((NE, 32, 128), lambda i: (0, 8, 0)),
            line,
            pl.BlockSpec((2 * ROWS, NHALF), lambda i: (0, 1)),
            pl.BlockSpec((2 * ROWS, NE), lambda i: (0, 0)),
        ],
        out_specs=line,
        scratch_shapes=[pltpu.VMEM((NE, DM), BF)],
        compiler_params=params,
        cost_estimate=cost,
        name="combine_last",
    )(yb, yb, total, gm, go)


def slots(ids):
    catalog = jnp.arange(NE, dtype=jnp.int32)
    hits = jnp.any(ids[:, :, None] == catalog, axis=1).astype(BF)
    below = (jnp.arange(ROWS)[:, None] > jnp.arange(ROWS)[None, :]).astype(BF)
    before = jnp.dot(below, hits, preferred_element_type=F32)
    slot = jnp.sum(
        jnp.where(ids[:, :, None] == catalog, before[:, None, :], 0.0), axis=-1
    ).astype(jnp.int32)
    main = ids * HALF + (slot & (HALF - 1)) + jnp.where(slot < HALF, 0, NHALF)
    return jnp.where(slot < SLOT, main, NMAIN + ids)


def on_device(
    queries,
    keys,
    values,
    q_gain,
    k_gain,
    out_weight,
    hidden_in,
    norm_gain,
    router,
    expert_ids,
    w_gate,
    w_up,
    w_down,
):
    t, e = lax.axis_index("tensor"), lax.axis_index("expert")
    scal = jnp.stack([t & 1, t >> 1, e >> 2, e & 3]).astype(jnp.int32)
    cs, sn = rotate_tables(e * PB + jnp.arange(PB, dtype=jnp.int32))

    kv = ready_keys(
        keys[0].reshape(PB, SEQ * HD), values[0].reshape(PB, SEQ * HD), cs, sn, k_gain.reshape(1, HD)
    )
    kv_all = ring_relay(jnp.stack(ring_four(kv, y_move)), z_move)
    w_all = [
        ring_relay(jnp.stack(ring_four(w, z_move)), y_move)
        for w in (out_weight[:512], out_weight[512:])
    ]

    q2 = queries[0].reshape(PB, SEQ * 1024)
    ids = expert_ids[0].reshape(ROWS, TOP)
    tgt = slots(ids)
    tgt_t = jnp.transpose(tgt.reshape(64, SEQ, TOP), (2, 1, 0)).reshape(TOP, ROWS)
    pick = picking(tgt_t)
    hid = jnp.transpose(hidden_in[0], (1, 0, 2)).reshape(ROWS, DM)

    attn = attention(scal, q2, cs, sn, q_gain.reshape(1, HD), kv_all)
    keeps, gots, rests = [], [], []
    for part in range(2):
        keep, send = project(part, scal, attn, w_all)
        got = lax.ppermute(send, "tensor", CORE_SWAP)
        other = (keep[128:].astype(F32) + got[128:].astype(F32)).astype(BF)
        keeps.append(keep)
        gots.append(got)
        rests.append(lax.ppermute(other, "tensor", X_SWAP))
    stream, normed, xa, xb = dispatch(scal, keeps, gots, rests, hid, norm_gain.reshape(1, DM), pick)

    def exchange(x):
        return lax.all_to_all(x, ("tensor", "expert"), split_axis=0, concat_axis=0, tiled=True)

    in_a, in_b = exchange(xa), exchange(xb)

    logits = jnp.dot(normed, router, preferred_element_type=F32)
    logits = jnp.transpose(logits.reshape(SEQ, 64, NE), (1, 0, 2)).reshape(ROWS, NE)
    chosen = ids[:, :, None] == jnp.arange(NE, dtype=jnp.int32)
    gates = jax.nn.softmax(jnp.sum(jnp.where(chosen, logits[:, None, :], 0.0), axis=-1), axis=-1)

    back_a = exchange(run_experts(in_a, w_gate, w_up, w_down, False))
    back_b = exchange(run_experts(in_b, w_gate, w_up, w_down, True))
    out = combine(back_a, back_b, stream, *mixing(tgt, gates))
    return out.reshape(hidden_in.shape)


def solution(mesh):
    return jax.shard_map(
        on_device,
        mesh=mesh,
        in_specs=(
            P(("dp", "expert"), None, None, "tensor"),
            P(("dp", "expert"), None, None, "tensor"),
            P(("dp", "expert"), None, None, "tensor"),
            P(),
            P(),
            P("tensor", "expert"),
            P(("dp", "expert"), "tensor", None, None),
            P(),
            P(),
            P(("dp", "expert"), "tensor", None, None),
            P(("tensor", "expert"), None, None),
            P(("tensor", "expert"), None, None),
            P(("tensor", "expert"), None, None),
        ),
        out_specs=P(("dp", "expert"), "tensor", None, None),
        check_vma=False,
    )
```

```python
import functools

import jax
import jax.numpy as jnp
from jax import lax
from jax.experimental import pallas as pl
from jax.experimental.pallas import tpu as pltpu
from jax.sharding import PartitionSpec as P


theta_base = 1000000.0
eps_norm = 1e-06
neg_fill = -1e30
LOG2E = 1.4426950408889634

BF = jnp.bfloat16
F32 = jnp.float32
HD = 128
PB = 256
SEQ = 2
DM = 4096
FF = 768
NE = 64
TOP = 8
ROWS = 128
SLOT = 16
NMAIN = NE * SLOT
NALL = NMAIN + NE
HALF = 8
NHALF = NE * HALF
XA = HALF * 32
XB = XA + 32
VMEM_BIG = 60 * 1024 * 1024


def spot(z, y):
    return (z % 4) * 4 + (y % 4)


def y_move(k):
    return [(spot(z, y), spot(z, y + k)) for z in range(4) for y in range(4)]


def z_move(k):
    return [(spot(z, y), spot(z + k, y)) for z in range(4) for y in range(4)]


CORE_SWAP = [(i, i ^ 1) for i in range(4)]
X_SWAP = [(i, i ^ 2) for i in range(4)]


def ring_four(x, move):
    return [x] + [lax.ppermute(x, "expert", move(k)) for k in (1, 2, 3)]


def ring_parts(x, move, far):
    left = lax.ppermute(x, "expert", move(1))
    right = lax.ppermute(x, "expert", move(3))
    if far == "left":
        last = lax.ppermute(left, "expert", move(1))
    elif far == "right":
        last = lax.ppermute(right, "expert", move(3))
    else:
        last = lax.ppermute(x, "expert", move(2))
    return x, left, right, last


def rotate_tables(positions):
    freq = theta_base ** (-2.0 * jnp.arange(HD // 2, dtype=F32) / HD)
    ang = positions.astype(F32)[:, None] * freq[None, :]
    cs, sn = jnp.cos(ang), jnp.sin(ang)
    return jnp.concatenate([cs, cs], axis=1), jnp.concatenate([-sn, sn], axis=1)


def keys_kernel(k_ref, v_ref, cos_ref, sin_ref, gain_ref, o_ref):
    cs, sn, gain = cos_ref[...], sin_ref[...], gain_ref[...]
    for s in range(SEQ):
        k = k_ref[:, s * HD : (s + 1) * HD].astype(F32)
        k = k * lax.rsqrt(jnp.mean(k * k, axis=-1, keepdims=True) + eps_norm) * gain
        o_ref[s, 0:PB, :] = (k * cs + pltpu.roll(k, HD // 2, 1) * sn).astype(BF)
        v = jnp.transpose(v_ref[:, s * HD : (s + 1) * HD].astype(F32)).astype(BF)
        o_ref[s, PB : PB + HD, :] = v[:, :HD]
        o_ref[s, PB + HD :, :] = v[:, HD:]


def ready_keys(k2, v2, cs, sn, gain):
    return pl.pallas_call(
        keys_kernel, out_shape=jax.ShapeDtypeStruct((SEQ, 2 * PB, HD), BF), name="ready_keys"
    )(k2, v2, cs, sn, gain)


C2 = HD ** (-0.5) * LOG2E
VR = HD + 16
HEADS = 8


def attn_part(q_ref, key_of, val_of, load, save, s_buf, mask):
    ones = jnp.ones((16, PB), BF)

    def score(h, j):
        q = q_ref[:, pl.ds(pl.multiple_of(h * HD, HD), HD)]
        s = lax.dot_general(key_of(j), q, (((1,), (1,)), ((), ())), preferred_element_type=F32)
        return s if mask is None else mask(j, s)

    top = None
    for j in range(4):
        s = score(0, j)
        s_buf[0, j] = s
        part = jnp.max(s, axis=0, keepdims=True)
        top = part if j == 0 else jnp.maximum(top, part)

    def body(h, top):
        slot = h & 1
        m_old, acc = load(h)
        m_new = jnp.maximum(m_old, top)
        mc = m_new * C2
        acc = acc * jnp.exp2(m_old * C2 - mc)
        nxt = None
        for j in range(4):
            s = score((h + 1) & (HEADS - 1), j)
            p = jnp.exp2(s_buf[slot, j] * C2 - mc).astype(BF)
            s_buf[1 - slot, j] = s
            part = jnp.max(s, axis=0, keepdims=True)
            nxt = part if j == 0 else jnp.maximum(nxt, part)
            acc = acc + jnp.dot(
                jnp.concatenate([val_of(j), ones], axis=0), p, preferred_element_type=F32
            )
        save(h, m_new, acc)
        return nxt

    lax.fori_loop(0, HEADS, body, top)


def block_keys(kv_ref):
    return (
        lambda j: kv_ref[j, 0, 0:PB, :],
        lambda j: jnp.concatenate(
            [kv_ref[j, 0, PB : PB + HD, :], kv_ref[j, 0, PB + HD :, :]], axis=1
        ),
    )


def attn_first(sc, q_ref, cos_ref, sin_ref, gain_ref, kv_ref, qr_ref, m_ref, acc_ref, s_buf):
    y = sc[3]
    cs, sn, gain = cos_ref[...], sin_ref[...], gain_ref[...]

    def turn_head(h, _):
        lanes = pl.ds(pl.multiple_of(h * HD, HD), HD)
        q = q_ref[:, lanes].astype(F32)
        q = q * lax.rsqrt(jnp.mean(q * q, axis=-1, keepdims=True) + eps_norm) * gain
        qr_ref[:, lanes] = (q * cs + pltpu.roll(q, HD // 2, 1) * sn).astype(BF)
        return 0

    lax.fori_loop(0, HEADS, turn_head, 0)

    def mask(j, s):
        if j > 0:
            return s + jnp.where(j <= y, 0.0, neg_fill)
        key = lax.broadcasted_iota(jnp.int32, (PB, PB), 0)
        row = lax.broadcasted_iota(jnp.int32, (PB, PB), 1)
        return jnp.where(key <= row, s, neg_fill)

    def load(h):
        return jnp.full((1, PB), neg_fill, F32), jnp.zeros((VR, PB), F32)

    def save(h, m, acc):
        m_ref[h] = jnp.broadcast_to(m, (8, PB))
        acc_ref[h] = acc

    key_of, val_of = block_keys(kv_ref)
    attn_part(qr_ref, key_of, val_of, load, save, s_buf, mask)


def attn_next(sc, q_ref, m_in, acc_in, ka_ref, kb_ref, m_ref, acc_ref, s_buf):
    z = sc[2]

    @pl.when(z == 0)
    def _():
        m_ref[...] = m_in[...]
        acc_ref[...] = acc_in[...]

    for need, kv_ref, m_from, acc_from in ((1, ka_ref, m_in, acc_in), (3, kb_ref, m_ref, acc_ref)):

        @pl.when(z >= need)
        def _(kv_ref=kv_ref, m_from=m_from, acc_from=acc_from):
            def load(h):
                return m_from[h, 0:1, :], acc_from[h]

            def save(h, m, acc):
                m_ref[h] = jnp.broadcast_to(m, (8, PB))
                acc_ref[h] = acc

            key_of, val_of = block_keys(kv_ref)
            attn_part(q_ref, key_of, val_of, load, save, s_buf, None)


def attn_last(sc, q_ref, m_in, acc_in, kv_ref, o_ref, s_buf):
    z = sc[2]

    def finish(h, acc):
        out = jnp.transpose(acc[:HD] / acc[HD : HD + 1])
        o_ref[:, pl.ds(pl.multiple_of(h * HD, HD), HD)] = out.astype(BF)

    @pl.when(z >= 2)
    def _():
        key_of, val_of = block_keys(kv_ref)
        attn_part(
            q_ref,
            key_of,
            val_of,
            lambda h: (m_in[h, 0:1, :], acc_in[h]),
            lambda h, m, acc: finish(h, acc),
            s_buf,
            None,
        )

    @pl.when(z < 2)
    def _():
        def body(h, _):
            finish(h, acc_in[h])
            return 0

        lax.fori_loop(0, HEADS, body, 0)


Q_SPEC = pl.BlockSpec((PB, 1024), lambda i, sc: (0, i))
M_SPEC = pl.BlockSpec((HEADS, 8, PB), lambda i, sc: (i, 0, 0))
A_SPEC = pl.BlockSpec((HEADS, VR, PB), lambda i, sc: (i, 0, 0))


def kv_spec(n):
    return pl.BlockSpec((n, 1, 2 * PB, HD), lambda i, sc: (0, i, 0, 0))


def attn_call(kernel, in_specs, out_specs, out_shape, parts):
    return pl.pallas_call(
        kernel,
        out_shape=out_shape,
        grid_spec=pltpu.PrefetchScalarGridSpec(
            num_scalar_prefetch=1,
            grid=(SEQ,),
            in_specs=in_specs,
            out_specs=out_specs,
            scratch_shapes=[pltpu.VMEM((2, 4, PB, PB), F32)],
        ),
        compiler_params=pltpu.CompilerParams(vmem_limit_bytes=VMEM_BIG),
        cost_estimate=pl.CostEstimate(
            flops=parts * 4 * 2**30, bytes_accessed=8 * 2**20, transcendentals=parts * 4 * 2**20
        ),
    )


STATE = (
    jax.ShapeDtypeStruct((SEQ * HEADS, 8, PB), F32),
    jax.ShapeDtypeStruct((SEQ * HEADS, VR, PB), F32),
)


def attention(scal, q2, cs, sn, gain, pieces):
    own, left, right, far = pieces
    table = pl.BlockSpec((PB, HD), lambda i, sc: (0, 0))
    qr, m, acc = attn_call(
        attn_first,
        [Q_SPEC, table, table, pl.BlockSpec((1, HD), lambda i, sc: (0, 0)), kv_spec(4)],
        (Q_SPEC, M_SPEC, A_SPEC),
        (jax.ShapeDtypeStruct((PB, SEQ * 1024), BF),) + STATE,
        1,
    )(scal, q2, cs, sn, gain, own)
    m, acc = attn_call(
        attn_next, [Q_SPEC, M_SPEC, A_SPEC, kv_spec(4), kv_spec(4)], (M_SPEC, A_SPEC), STATE, 2
    )(scal, qr, m, acc, left, right)
    return attn_call(
        attn_last,
        [Q_SPEC, M_SPEC, A_SPEC, kv_spec(4)],
        Q_SPEC,
        jax.ShapeDtypeStruct((PB, SEQ * 1024), BF),
        1,
    )(scal, qr, m, acc, far)


WSPLIT = 576


def proj_kernel(part, sc, a_ref, *rest):
    w_in, (keep, send, lhs, w, sem) = rest[:8], rest[8:]
    c, xh = sc[0], sc[1]
    two = pl.ds(2 * part, 2)
    moves = []
    for half in range(2):
        rows = pl.ds(0, WSPLIT) if half == 0 else pl.ds(WSPLIT, 1024 - WSPLIT)
        for k, dy in enumerate((0, 1, 3, 2)):
            moves.append((dy, w_in[4 * half + k].at[two], w.at[:, dy, rows]))
    copies = [(d, pltpu.make_async_copy(a, b, sem.at[i])) for i, (d, a, b) in enumerate(moves)]
    for _, cp in copies:
        cp.start()
    for cc in (1, 0):
        for xx in range(2):
            base = pl.multiple_of(64 * (2 * (xh ^ xx) + (c ^ cc)), 64)
            for s in range(SEQ):
                at = cc * 256 + xx * 128 + s * 64
                lhs[at : at + 64, :] = a_ref[pl.ds(base, 64), s * 1024 : (s + 1) * 1024]
    for dy in (0, 1, 3, 2):
        for d, cp in copies:
            if d == dy:
                cp.wait()
        for i in range(2):
            res = jnp.dot(lhs[...], w[i, dy], preferred_element_type=F32).astype(BF)
            lane = (i * 4 + dy) * 256
            keep[:, lane : lane + 256] = res[:256]
            send[:, lane : lane + 256] = res[256:]


def project(part, scal, attn, halves):
    pieces = [x for h in halves for x in h]
    full = pl.BlockSpec(memory_space=pltpu.VMEM)
    return pl.pallas_call(
        functools.partial(proj_kernel, part),
        out_shape=(
            jax.ShapeDtypeStruct((256, DM // 2), BF),
            jax.ShapeDtypeStruct((256, DM // 2), BF),
        ),
        in_specs=[pl.BlockSpec(memory_space=pltpu.SMEM), full]
        + [pl.BlockSpec(memory_space=pl.ANY)] * len(pieces),
        out_specs=(full, full),
        scratch_shapes=[
            pltpu.VMEM((512, 1024), BF),
            pltpu.VMEM((2, 4, 1024, 256), BF),
            pltpu.SemaphoreType.DMA((8,)),
        ],
        compiler_params=pltpu.CompilerParams(vmem_limit_bytes=VMEM_BIG),
        cost_estimate=pl.CostEstimate(
            flops=2 * 2**30, bytes_accessed=7 * 2**20, transcendentals=0
        ),
    )(scal, attn, *pieces)


def pair_tile(x):
    both = [x[:, k * 128 : (k + 1) * 128].reshape(NE, HALF, 128) for k in range(2)]
    return jnp.concatenate(both, axis=1).astype(BF)


def open_tiles(ref, count):
    out = []
    for i in range(count):
        x = ref[:, i * 16 : (i + 1) * 16, :].astype(F32)
        out += [x[:, :HALF].reshape(NHALF, 128), x[:, HALF:].reshape(NHALF, 128)]
    return jnp.concatenate(out, axis=1).astype(BF)


def pick_kernel(tgt_ref, o_ref):
    def block(b, _):
        base = pl.multiple_of(b * 64, 64)
        line = lax.broadcasted_iota(jnp.int32, (64, ROWS), 0) + base
        hit = jnp.zeros((64, ROWS), F32)
        for k in range(TOP):
            hit = jnp.where(line == tgt_ref[k : k + 1, :], 1.0, hit)
        o_ref[pl.ds(base, 64), :] = hit.astype(BF)
        return 0

    lax.fori_loop(0, NALL // 64, block, 0)


def picking(tgt_t):
    return pl.pallas_call(
        pick_kernel,
        out_shape=jax.ShapeDtypeStruct((NALL, ROWS), BF),
        cost_estimate=pl.CostEstimate(flops=2**22, bytes_accessed=2**19, transcendentals=0),
        name="picking",
    )(tgt_t)


def dispatch_kernel(
    sc, k0, k1, g0, g1, r0, r1, h_ref, gain_ref, pick, st_ref, nm_ref, xa_hbm, xb_hbm, x_ref, sem
):
    z, y = sc[2], sc[3]
    square = jnp.zeros((ROWS, 1), F32)
    for dz in range(4):
        k_ref, g_ref, r_ref = (k0, g0, r0) if dz < 2 else (k1, g1, r1)
        for dy in range(4):
            here = (dz & 1) * 1024 + dy * 256
            there = pl.multiple_of((((z - dz) & 3) * 4 + ((y - dy) & 3)) * 256, 256)
            span = slice(here, here + 256)
            total = (
                h_ref[:, pl.ds(there, 256)].astype(F32)
                + (k_ref[:, span].astype(F32) + g_ref[:, span].astype(F32))
                + r_ref[:, span].astype(F32)
            )
            st = total.astype(BF)
            st_ref[:, pl.ds(there, 256)] = st
            sf = st.astype(F32)
            square = square + jnp.sum(sf * sf, axis=-1, keepdims=True)
    scale = lax.rsqrt(square / DM + eps_norm)
    nm_ref[...] = (st_ref[...].astype(F32) * scale * gain_ref[...]).astype(BF)

    def out_copy(chunk, j):
        rows = pl.ds(pl.multiple_of(j * 32, 32), 32)
        to = xa_hbm if chunk == 0 else xb_hbm
        return pltpu.make_async_copy(x_ref.at[chunk, :, rows], to.at[:, rows], sem.at[chunk, j])

    def send_part(it, _):
        for jj in range(2):
            j = 2 * it + jj
            n = nm_ref[:, pl.ds(pl.multiple_of(j * 512, 512), 512)]
            for chunk in range(2):
                main = jnp.dot(
                    pick[chunk * NHALF : (chunk + 1) * NHALF, :], n, preferred_element_type=F32
                )
                for i in range(2):
                    at = pl.multiple_of(j * 32 + i * 16, 16)
                    x_ref[chunk, :, pl.ds(at, 16), :] = pair_tile(
                        main[:, i * 256 : (i + 1) * 256]
                    )
                out_copy(chunk, j).start()
        return 0

    lax.fori_loop(0, 4, send_part, 0)
    ov = jnp.dot(pick[NMAIN:, :], nm_ref[...], preferred_element_type=F32).astype(BF)
    x_ref[1, :, XA:XB, :] = ov.reshape(NE, 32, 128)
    out_copy(1, 8).start()
    for chunk in range(2):
        for j in range(8 + chunk):
            out_copy(chunk, j).wait()


def dispatch(scal, keeps, gots, rests, hid, gain, pick):
    at = lambda i, sc: (0, 0)
    half = pl.BlockSpec((ROWS, DM // 2), at)
    line = pl.BlockSpec((ROWS, DM), at)
    return pl.pallas_call(
        dispatch_kernel,
        out_shape=(
            jax.ShapeDtypeStruct((ROWS, DM), BF),
            jax.ShapeDtypeStruct((ROWS, DM), BF),
            jax.ShapeDtypeStruct((NE, XA, 128), BF),
            jax.ShapeDtypeStruct((NE, XB, 128), BF),
        ),
        grid_spec=pltpu.PrefetchScalarGridSpec(
            num_scalar_prefetch=1,
            grid=(1,),
            in_specs=[half] * 6
            + [line, pl.BlockSpec((1, DM), at), pl.BlockSpec((NALL, ROWS), at)],
            out_specs=(line, line) + (pl.BlockSpec(memory_space=pl.ANY),) * 2,
            scratch_shapes=[pltpu.VMEM((2, NE, XB, 128), BF), pltpu.SemaphoreType.DMA((2, 9))],
        ),
        compiler_params=pltpu.CompilerParams(vmem_limit_bytes=VMEM_BIG),
        cost_estimate=pl.CostEstimate(
            flops=2**30, bytes_accessed=14 * 2**20, transcendentals=0
        ),
        name="dispatch",
    )(scal, *keeps, *gots, *rests, hid, gain, pick)


def expert_kernel(over, *refs):
    x_ref, refs = refs[0], refs[1:]
    if over:
        xo_ref, refs = refs[0], refs[1:]
    wg_ref, wu_ref, wd_ref, y_hbm, ga, ua, inner, yb, sem = refs[:9]
    if over:
        xov, yo = refs[9:]
    step = pl.program_id(0)

    if over:

        @pl.when(step == 0)
        def _():
            xov[...] = xo_ref[...].reshape(NE, DM)

    @pl.when(step < 4)
    def _():
        rows = open_tiles(x_ref, 4)
        if over:
            lane = pl.multiple_of(step * 1024, 1024)
            rows = jnp.concatenate([rows, xov[:, pl.ds(lane, 1024)]], axis=0)
        g = jnp.dot(rows, wg_ref[0], preferred_element_type=F32)
        u = jnp.dot(rows, wu_ref[0], preferred_element_type=F32)

        @pl.when(step == 0)
        def _():
            ga[...] = g
            ua[...] = u

        @pl.when(step > 0)
        def _():
            ga[...] += g
            ua[...] += u

    @pl.when(step == 4)
    def _():
        g = ga[...]
        inner[...] = (g / (1.0 + jnp.exp(-g)) * ua[...]).astype(BF)

    def out_copy(j):
        rows = pl.ds(pl.multiple_of(j * 64, 64), 64)
        return pltpu.make_async_copy(yb.at[j & 1], y_hbm.at[:, rows], sem.at[j & 1])

    @pl.when(step >= 4)
    def _():
        j = step - 4
        out = jnp.dot(inner[...], wd_ref[0], preferred_element_type=F32)

        @pl.when(j >= 2)
        def _():
            out_copy(j - 2).wait()

        for i in range(4):
            yb[j & 1, :, i * 16 : (i + 1) * 16, :] = pair_tile(
                out[:NHALF, i * 256 : (i + 1) * 256]
            )
        out_copy(j).start()
        if over:
            xov[:, pl.ds(pl.multiple_of(j * 1024, 1024), 1024)] = out[NHALF:].astype(BF)

        @pl.when(j == 3)
        def _():
            if over:
                yo[...] = xov[...].reshape(NE, 32, 128)
                last = pltpu.make_async_copy(yo, y_hbm.at[:, pl.ds(XA, 32)], sem.at[2])
                last.start()
                last.wait()
            out_copy(2).wait()
            out_copy(3).wait()


def run_experts(x, wg, wu, wd, over):
    lo = lambda i: jnp.minimum(i, 3)
    n = NHALF + (NE if over else 0)
    x_specs = [pl.BlockSpec((NE, 64, 128), lambda i: (0, lo(i), 0))]
    extra = []
    if over:
        x_specs.append(pl.BlockSpec((NE, 32, 128), lambda i: (0, 8, 0)))
        extra = [pltpu.VMEM((NE, DM), BF), pltpu.VMEM((NE, 32, 128), BF)]
    return pl.pallas_call(
        functools.partial(expert_kernel, over),
        grid=(8,),
        out_shape=jax.ShapeDtypeStruct(x.shape, BF),
        in_specs=x_specs
        + [
            pl.BlockSpec((1, 1024, FF), lambda i: (0, lo(i), 0)),
            pl.BlockSpec((1, 1024, FF), lambda i: (0, lo(i), 0)),
            pl.BlockSpec((1, FF, 1024), lambda i: (0, 0, jnp.maximum(i - 4, 0))),
        ],
        out_specs=pl.BlockSpec(memory_space=pl.ANY),
        scratch_shapes=[
            pltpu.VMEM((n, FF), F32),
            pltpu.VMEM((n, FF), F32),
            pltpu.VMEM((n, FF), BF),
            pltpu.VMEM((2, NE, 64, 128), BF),
            pltpu.SemaphoreType.DMA((3,)),
        ]
        + extra,
        compiler_params=pltpu.CompilerParams(vmem_limit_bytes=VMEM_BIG),
        cost_estimate=pl.CostEstimate(
            flops=10 * 2**30, bytes_accessed=27 * 2**20, transcendentals=2**19
        ),
        name="experts_b" if over else "experts_a",
    )(*([x] * len(x_specs)), wg, wu, wd)


def mix_kernel(tgt_ref, gate_ref, gm, go):
    def block(b, _):
        base = pl.multiple_of(b * 32, 32)
        own, other = pl.ds(base, 32), pl.ds(base + ROWS, 32)
        lane = lax.broadcasted_iota(jnp.int32, (32, NALL), 1)
        mix = jnp.zeros((32, NALL), F32)
        for k in range(TOP):
            mix = jnp.where(lane == tgt_ref[own, k : k + 1], gate_ref[own, k : k + 1], mix)
        hi = mix.astype(BF)
        lo = (mix - hi.astype(F32)).astype(BF)
        gm[own, :] = hi[:, :NMAIN]
        gm[other, :] = lo[:, :NMAIN]
        go[own, :] = hi[:, NMAIN:]
        go[other, :] = lo[:, NMAIN:]
        return 0

    lax.fori_loop(0, ROWS // 32, block, 0)


def mixing(tgt, gates):
    return pl.pallas_call(
        mix_kernel,
        out_shape=(
            jax.ShapeDtypeStruct((2 * ROWS, NMAIN), BF),
            jax.ShapeDtypeStruct((2 * ROWS, NE), BF),
        ),
        cost_estimate=pl.CostEstimate(flops=2**22, bytes_accessed=2**20, transcendentals=0),
        name="mixing",
    )(tgt, gates)


def combine_first(y_ref, st_ref, gm_ref, o_ref):
    both = jnp.dot(gm_ref[...], open_tiles(y_ref, 4), preferred_element_type=F32)
    r = lax.broadcasted_iota(jnp.int32, (ROWS, ROWS), 0)
    c = lax.broadcasted_iota(jnp.int32, (ROWS, ROWS), 1)
    turn = jnp.where(c == (r & 1) * 64 + (r >> 1), 1.0, 0.0).astype(BF)
    st = jnp.dot(turn, st_ref[...], preferred_element_type=F32)
    o_ref[...] = st + (both[:ROWS] + both[ROWS:])


def combine_last(y_ref, yo_ref, sum_ref, gm_ref, go_ref, o_ref, yov):
    step = pl.program_id(0)

    @pl.when(step == 0)
    def _():
        yov[...] = yo_ref[...].reshape(NE, DM)

    at = pl.multiple_of(step * 1024, 1024)
    both = jnp.dot(gm_ref[...], open_tiles(y_ref, 4), preferred_element_type=F32) + jnp.dot(
        go_ref[...], yov[:, pl.ds(at, 1024)], preferred_element_type=F32
    )
    o_ref[...] = (sum_ref[...] + (both[:ROWS] + both[ROWS:])).astype(BF)


def combine(ya, yb, stream, gm, go):
    tile = pl.BlockSpec((NE, 64, 128), lambda i: (0, i, 0))
    line = pl.BlockSpec((ROWS, 1024), lambda i: (0, i))
    params = pltpu.CompilerParams(vmem_limit_bytes=VMEM_BIG)
    cost = pl.CostEstimate(flops=2**30, bytes_accessed=6 * 2**20, transcendentals=0)
    total = pl.pallas_call(
        combine_first,
        grid=(4,),
        out_shape=jax.ShapeDtypeStruct((ROWS, DM), F32),
        in_specs=[tile, line, pl.BlockSpec((2 * ROWS, NHALF), lambda i: (0, 0))],
        out_specs=line,
        compiler_params=params,
        cost_estimate=cost,
        name="combine_first",
    )(ya, stream, gm)
    return pl.pallas_call(
        combine_last,
        grid=(4,),
        out_shape=jax.ShapeDtypeStruct((ROWS, DM), BF),
        in_specs=[
            tile,
            pl.BlockSpec((NE, 32, 128), lambda i: (0, 8, 0)),
            line,
            pl.BlockSpec((2 * ROWS, NHALF), lambda i: (0, 1)),
            pl.BlockSpec((2 * ROWS, NE), lambda i: (0, 0)),
        ],
        out_specs=line,
        scratch_shapes=[pltpu.VMEM((NE, DM), BF)],
        compiler_params=params,
        cost_estimate=cost,
        name="combine_last",
    )(yb, yb, total, gm, go)


def slots(ids):
    catalog = jnp.arange(NE, dtype=jnp.int32)
    hits = jnp.any(ids[:, :, None] == catalog, axis=1).astype(BF)
    below = (jnp.arange(ROWS)[:, None] > jnp.arange(ROWS)[None, :]).astype(BF)
    before = jnp.dot(below, hits, preferred_element_type=F32)
    slot = jnp.sum(
        jnp.where(ids[:, :, None] == catalog, before[:, None, :], 0.0), axis=-1
    ).astype(jnp.int32)
    main = ids * HALF + (slot & (HALF - 1)) + jnp.where(slot < HALF, 0, NHALF)
    return jnp.where(slot < SLOT, main, NMAIN + ids)


def on_device(
    queries,
    keys,
    values,
    q_gain,
    k_gain,
    out_weight,
    hidden_in,
    norm_gain,
    router,
    expert_ids,
    w_gate,
    w_up,
    w_down,
):
    t, e = lax.axis_index("tensor"), lax.axis_index("expert")
    scal = jnp.stack([t & 1, t >> 1, e >> 2, e & 3]).astype(jnp.int32)
    cs, sn = rotate_tables(e * PB + jnp.arange(PB, dtype=jnp.int32))

    kv = ready_keys(
        keys[0].reshape(PB, SEQ * HD), values[0].reshape(PB, SEQ * HD), cs, sn, k_gain.reshape(1, HD)
    )
    kv_all = ring_parts(jnp.stack(ring_four(kv, y_move)), z_move, "direct")
    w_all = [
        ring_parts(jnp.stack(ring_four(w, z_move)), y_move, far)
        for w, far in ((out_weight[:WSPLIT], "left"), (out_weight[WSPLIT:], "right"))
    ]

    q2 = queries[0].reshape(PB, SEQ * 1024)
    ids = expert_ids[0].reshape(ROWS, TOP)
    tgt = slots(ids)
    tgt_t = jnp.transpose(tgt.reshape(64, SEQ, TOP), (2, 1, 0)).reshape(TOP, ROWS)
    pick = picking(tgt_t)
    hid = jnp.transpose(hidden_in[0], (1, 0, 2)).reshape(ROWS, DM)

    attn = attention(scal, q2, cs, sn, q_gain.reshape(1, HD), kv_all)
    keeps, gots, rests = [], [], []
    for part in range(2):
        keep, send = project(part, scal, attn, w_all)
        got = lax.ppermute(send, "tensor", CORE_SWAP)
        other = (keep[128:].astype(F32) + got[128:].astype(F32)).astype(BF)
        keeps.append(keep)
        gots.append(got)
        rests.append(lax.ppermute(other, "tensor", X_SWAP))
    stream, normed, xa, xb = dispatch(scal, keeps, gots, rests, hid, norm_gain.reshape(1, DM), pick)

    def exchange(x):
        return lax.all_to_all(x, ("tensor", "expert"), split_axis=0, concat_axis=0, tiled=True)

    in_a, in_b = exchange(xa), exchange(xb)

    logits = jnp.dot(normed, router, preferred_element_type=F32)
    logits = jnp.transpose(logits.reshape(SEQ, 64, NE), (1, 0, 2)).reshape(ROWS, NE)
    chosen = ids[:, :, None] == jnp.arange(NE, dtype=jnp.int32)
    gates = jax.nn.softmax(jnp.sum(jnp.where(chosen, logits[:, None, :], 0.0), axis=-1), axis=-1)

    back_a = exchange(run_experts(in_a, w_gate, w_up, w_down, False))
    back_b = exchange(run_experts(in_b, w_gate, w_up, w_down, True))
    out = combine(back_a, back_b, stream, *mixing(tgt, gates))
    return out.reshape(hidden_in.shape)


def solution(mesh):
    return jax.shard_map(
        on_device,
        mesh=mesh,
        in_specs=(
            P(("dp", "expert"), None, None, "tensor"),
            P(("dp", "expert"), None, None, "tensor"),
            P(("dp", "expert"), None, None, "tensor"),
            P(),
            P(),
            P("tensor", "expert"),
            P(("dp", "expert"), "tensor", None, None),
            P(),
            P(),
            P(("dp", "expert"), "tensor", None, None),
            P(("tensor", "expert"), None, None),
            P(("tensor", "expert"), None, None),
            P(("tensor", "expert"), None, None),
        ),
        out_specs=P(("dp", "expert"), "tensor", None, None),
        check_vma=False,
    )
```
